256 devices in a mesh: blk: 64 (over z, y, core), rep: 4 (over x).
Axes of the slice: x: 4, y: 4, z: 8, core: 2. Of those that a mesh axis runs over, the one named last changes fastest.
Arguments:
- saved_inputs: bfloat16 [2, 65536, 256], P(None, ('rep', 'blk')), parts along dimension 1, may hold values from -6 to 6
- output_grads: bfloat16 [65536, 256], P(('rep', 'blk')), parts along dimension 0, may hold values from -6 to 6
- owner_ids: int32 [2, 65536, 1], P(None, 'rep'), parts along dimension 1, may hold values from 0 to 63; in each aligned block of 256 rows (0 to 255, 256 to 511, ..., all dimensions but the last counted through in order) at most 8 rows name the same one
- attend_weight: bfloat16 [2, 256, 768], replicated, may hold values from -8 to 8
- output_weight: bfloat16 [2, 256, 256], replicated, may hold values from -0.375 to 0.375
- up_weight: bfloat16 [2, 256, 1024], replicated, may hold values from -0.375 to 0.375
- down_weight: bfloat16 [2, 1024, 256], replicated, may hold values from -0.1875 to 0.1875
Outputs:
- input_grads: bfloat16 [65536, 256], P(('rep', 'blk')), parts along dimension 0
The draws below stay inside these ranges and needn't reach their ends.
There are 4 independent parts, one for each index of `rep`. The reference program is written for one: setup_inputs(seed, part) draws one part's arguments, and reference() takes and returns one part's arrays. A program takes and returns all parts, laid end to end along the dimension named above; an argument that names none is the same for every part. Nothing has to cross between parts.
Inputs may be any that keep to these rules, and one draw needn't show every extreme that they name: `owner_ids`: in each layer, at most 8 of the points of one device have the same owner, and in every draw some device's points name one owner exactly 8 times.
All inputs are finite; a program needn't handle non-finite values.
Results may differ from the reference program's by a relative error of at most 0.02.
The reference program's roundings to bfloat16 on the way count: a program that leaves them out, or rounds other values in their place, can miss the bound.
Values may be sent and summed in bfloat16 or wider, within the bound.
No kernel may reach another device: no remote copies, remote signals or barrier semaphores. Data moves between devices by JAX's collectives and lax.ppermute only.
A program may use at most 64 MiB of HBM per device.

```python
import math
import jax
import jax.numpy as jnp
import numpy as np
from jax import lax

D = 256
HEADS = 8
FF = 1024
WIN = 512
LAYERS = 2
P_DEV = 256
CAP = 8
TOTAL = 16384
N_BLK = 64


def draw_attend_weight(key, part):
    base_key = jax.random.fold_in(jax.random.fold_in(key, 17), 0)
    base_draw = jax.random.normal(base_key, (LAYERS, D, 3 * D), jnp.float32) * D ** (-0.5)
    return base_draw.astype(jnp.bfloat16)


def shard_levels(stream_key, dims, cuts, low, top_value):
    def one(dim, parts):
        steps = jax.random.uniform(jax.random.fold_in(jax.random.fold_in(stream_key, 6), dim), (parts,), jnp.float32, low / len(cuts), top_value / len(cuts))
        return jnp.repeat(jnp.exp(steps), dims[dim] // parts).reshape((-1,) + (1,) * (len(dims) - dim - 1))

    loudness = one(*cuts[0])
    for cut in cuts[1:]:
        loudness = loudness * one(*cut)
    return loudness


def deal_out(own_key, own, number, rows, number_of, top, reach, lean):
    ranking = jax.random.permutation(own_key, number_of)
    heavy_load, ordinary = shares(number_of, rows * top, reach, lean, True), shares(number_of, rows * top, reach, lean, False)
    places = jnp.arange(number_of)

    def named(lengths, rotation):
        used = int((lengths > 0).sum())
        fixed = max(1, used // 4)
        moved = fixed + (places - fixed + rotation * (used - fixed)) % max(1, number_of - fixed)
        return jnp.zeros((number_of,), jnp.int32).at[ranking[jnp.where(places < fixed, places, moved)]].set(jnp.asarray(lengths, jnp.int32))

    lengths = jnp.where(number % 4 == 0, named(heavy_load, number // 4), named(ordinary, number - number // 4 - 1))
    mixed = jax.random.permutation(jax.random.fold_in(own, 3), number_of)
    giver, receiver = mixed[0:number_of // 2 * 2:2], mixed[1:number_of // 2 * 2:2]
    margin = jnp.minimum(lengths[giver] - 1, reach - lengths[receiver]) // 2
    margin = jnp.where((giver == ranking[0]) | (receiver == ranking[0]) | (lengths[receiver] == 0), 0, jnp.maximum(margin, 0))
    moved = jax.random.randint(jax.random.fold_in(own, 4), (number_of // 2,), 0, 1 << 20) % (margin + 1)
    lengths = lengths.at[giver].add(-moved).at[receiver].add(moved)
    labels = jnp.searchsorted(jnp.cumsum(lengths), jnp.arange(rows * top), side="right").astype(jnp.int32)
    listing = labels.reshape(top, rows).T
    listing = listing[jax.random.permutation(jax.random.fold_in(own, 1), rows)]
    rotation = jax.random.randint(jax.random.fold_in(own, 2), (rows, 1), 0, top)
    return jnp.take_along_axis(listing, (jnp.arange(top)[None, :] + rotation) % top, axis=1)


def shares(number_of, total, limit, skew, full):
    loads = [(1 << 20) // math.isqrt(grade ** skew) + 1 for grade in range(1, number_of + 1)]
    largest = limit if full else min(limit, max(-(-total // number_of), total * loads[0] // sum(loads)))
    least = 1 if total - largest >= number_of - 1 else 0
    given, spare = [largest] + [least] * (number_of - 1), total - largest - least * (number_of - 1)
    while spare > 0:
        movable = [i for i in range(1, number_of) if given[i] < largest] or [i for i in range(1, number_of) if given[i] < limit]
        whole, budget = sum([loads[i] for i in movable]), spare
        for i in movable:
            extra = min(limit - given[i], max(1, budget * loads[i] // whole), spare)
            given[i] = given[i] + extra
            spare = spare - extra
    return np.array(given)


def normal_values(key, shape, scale, most, cuts=(), held_as=jnp.bfloat16):
    values = jax.random.normal(key, shape, jnp.float32) * scale
    if len(cuts) > 0:
        values = shard_levels(key, shape, cuts, -0.22, 0.18) * values
    return jnp.clip(values, min=-most, max=most).astype(held_as)


def setup_inputs(seed: int = 0, part: int = 0) -> dict:
    streams_of = jax.random.split(jax.random.key(seed), 8)
    part_splits = jax.random.split(jax.random.fold_in(streams_of[7], part), 8)
    saved_inputs = normal_values(part_splits[0], (LAYERS, TOTAL, D), 1.0, 6.0, ((1, 64),))
    output_grads = normal_values(part_splits[1], (TOTAL, D), 1.0, 6.0, ((0, 64),))
    owner_ids_keys = jax.random.split(jax.random.fold_in(part_splits[2], 1), LAYERS * TOTAL // P_DEV)
    owner_ids_turns = jax.random.permutation(jax.random.fold_in(part_splits[2], 3), LAYERS * TOTAL // P_DEV)
    owner_ids = jax.vmap(lambda own, number: deal_out(jax.random.fold_in(part_splits[2], 2), own, number, P_DEV, N_BLK, 1, CAP, 2))(owner_ids_keys, owner_ids_turns).reshape((LAYERS, TOTAL, 1))
    attend_weight = draw_attend_weight(jax.random.fold_in(streams_of[7], 71), part)
    output_weight = normal_values(streams_of[4], (LAYERS, D, D), D ** -0.5, 0.375)
    up_weight = normal_values(streams_of[5], (LAYERS, D, FF), D ** -0.5, 0.375)
    down_weight = normal_values(streams_of[6], (LAYERS, FF, D), FF ** -0.5, 0.1875)
    return dict(saved_inputs=saved_inputs, output_grads=output_grads, owner_ids=owner_ids, attend_weight=attend_weight, output_weight=output_weight, up_weight=up_weight, down_weight=down_weight)


EPSILON = 1e-05
MASKED = -1e+30

def layer_norm(values):
    centered = values - lax.optimization_barrier(jnp.mean(values, axis=-1, keepdims=True))
    return centered * lax.rsqrt(lax.optimization_barrier(jnp.mean(centered * centered, axis=-1, keepdims=True)) + EPSILON)

def times_t(left_side, right_side):
    return jnp.dot(left_side, right_side.T, preferred_element_type=jnp.float32)

def soft_window(queries, key_rows, alive_keys, scaling):
    scores = jnp.einsum('qhd,khd->hqk', queries.astype(jnp.float32), key_rows.astype(jnp.float32)) * scaling
    scores = jnp.where(alive_keys[None, None, :], scores, MASKED)
    largest = lax.optimization_barrier(jnp.max(scores, axis=-1, keepdims=True))
    exponent = jnp.exp(scores - largest)
    return exponent / lax.optimization_barrier(jnp.sum(exponent, axis=-1, keepdims=True))

def split_windows(projected, alive_mask):
    slot_count = projected.shape[0]
    stacked = projected.reshape(slot_count // WIN, WIN, 3, HEADS, D // HEADS)
    return (stacked, alive_mask.reshape(slot_count // WIN, WIN))

def attend_forward(inputs, alive_mask, attend_layer, output_layer):
    normed = layer_norm(inputs.astype(jnp.float32)).astype(jnp.bfloat16)
    projected = jnp.dot(normed, attend_layer, preferred_element_type=jnp.float32).astype(jnp.bfloat16)
    stacked, alive_win = split_windows(projected, alive_mask)
    scaling = (D // HEADS) ** (-0.5)

    def one_window(operand):
        window_block, alive_keys = operand
        attention = soft_window(window_block[:, 0], window_block[:, 1], alive_keys, scaling).astype(jnp.bfloat16)
        return jnp.einsum('hqk,khd->qhd', attention.astype(jnp.float32), window_block[:, 2].astype(jnp.float32)).astype(jnp.bfloat16)
    attended = lax.map(one_window, (stacked, alive_win)).reshape(inputs.shape[0], D)
    mixed_out = jnp.dot(attended, output_layer, preferred_element_type=jnp.float32).astype(jnp.bfloat16)
    return (projected, mixed_out)

def mlp_backward(inputs, mixed_out, gradients, up_layer, down_layer):
    middle = inputs.astype(jnp.float32) + mixed_out.astype(jnp.float32)
    normed, norm_pull = jax.vjp(layer_norm, middle)
    hidden_pre = jnp.dot(normed.astype(jnp.bfloat16), up_layer, preferred_element_type=jnp.float32)
    hidden_grad = times_t(gradients, down_layer)
    _, gelu_pull = jax.vjp(jax.nn.gelu, hidden_pre)
    pre_grad = gelu_pull(hidden_grad)[0].astype(jnp.bfloat16)
    normed_grad = times_t(pre_grad, up_layer)
    return (gradients.astype(jnp.float32) + norm_pull(normed_grad)[0]).astype(jnp.bfloat16)

def attend_backward(inputs, alive_mask, projected, grad_mid, attend_layer, output_layer):
    head_grads = times_t(grad_mid, output_layer).astype(jnp.bfloat16)
    stacked, alive_win = split_windows(projected, alive_mask)
    upstream_all = head_grads.reshape(stacked.shape[0], WIN, HEADS, D // HEADS)
    scaling = (D // HEADS) ** (-0.5)

    def one_window(operand):
        window_block, alive_keys, upstream = operand
        queries = window_block[:, 0].astype(jnp.float32)
        key_rows = window_block[:, 1].astype(jnp.float32)
        values = window_block[:, 2].astype(jnp.float32)
        upstream = upstream.astype(jnp.float32)
        attention = soft_window(window_block[:, 0], window_block[:, 1], alive_keys, scaling)
        rounded = attention.astype(jnp.bfloat16).astype(jnp.float32)
        value_grads = jnp.einsum('hqk,qhd->khd', rounded, upstream)
        prob_grads = jnp.einsum('qhd,khd->hqk', upstream, values)
        score_grads = (attention * (prob_grads - lax.optimization_barrier(jnp.sum(prob_grads * attention, axis=-1, keepdims=True)))).astype(jnp.bfloat16).astype(jnp.float32)
        query_grads = jnp.einsum('hqk,khd->qhd', score_grads, key_rows) * scaling
        key_grads = jnp.einsum('hqk,qhd->khd', score_grads, queries) * scaling
        return jnp.stack([query_grads, key_grads, value_grads], axis=1).astype(jnp.bfloat16)
    projected_grads = lax.map(one_window, (stacked, alive_win, upstream_all)).reshape(inputs.shape[0], 3 * D)
    normed_grads = times_t(projected_grads, attend_layer)
    _, norm_pull = jax.vjp(layer_norm, inputs.astype(jnp.float32))
    return norm_pull(normed_grads)[0].astype(jnp.bfloat16)

def slot_backward(inputs, gradients, alive_mask, weights):
    attend_layer, output_layer, up_layer, down_layer = weights
    projected, mixed_out = attend_forward(inputs, alive_mask, attend_layer, output_layer)
    grad_mid = mlp_backward(inputs, mixed_out, gradients, up_layer, down_layer)
    branch = attend_backward(inputs, alive_mask, projected, grad_mid, attend_layer, output_layer)
    return (grad_mid.astype(jnp.float32) + branch.astype(jnp.float32)).astype(jnp.bfloat16)

def reference(saved_inputs, output_grads, owner_ids, attend_weight, output_weight, up_weight, down_weight):
    slot_count = 2 * P_DEV
    total_rows = N_BLK * slot_count
    device_ids = jnp.arange(N_BLK, dtype=jnp.int32)
    source_dev = jnp.repeat(device_ids, P_DEV)
    gradient = output_grads
    for layer_at in range(LAYERS - 1, -1, -1):
        owner_all = owner_ids[layer_at, :, 0].astype(jnp.int32)
        one_hot = (owner_all.reshape(N_BLK, P_DEV)[:, :, None] == device_ids[None, None, :]).astype(jnp.int32)
        bucket_rank = lax.optimization_barrier(jnp.sum((jnp.cumsum(one_hot, axis=1) - one_hot) * one_hot, axis=2)).reshape(-1)
        slot_row = (owner_all * slot_count + bucket_rank * N_BLK + source_dev).astype(jnp.int32)
        input_slots = jnp.zeros((total_rows, D), jnp.bfloat16).at[slot_row].set(saved_inputs[layer_at])
        grad_slots = jnp.zeros((total_rows, D), jnp.bfloat16).at[slot_row].set(gradient)
        alive_mask = jnp.zeros((total_rows,), jnp.int32).at[slot_row].set(1) > 0
        weights = (attend_weight[layer_at], output_weight[layer_at], up_weight[layer_at], down_weight[layer_at])

        def per_device(operand):
            return slot_backward(operand[0], operand[1], operand[2], weights)
        result = lax.map(per_device, (input_slots.reshape(N_BLK, slot_count, D), grad_slots.reshape(N_BLK, slot_count, D), alive_mask.reshape(N_BLK, slot_count)))
        gradient = result.reshape(total_rows, D)[slot_row]
    return gradient
```

```python
import jax
import jax.numpy as jnp
from jax import lax
from jax.experimental import pallas as pl
from jax.experimental.pallas import tpu as pltpu
from jax.sharding import PartitionSpec as P

D = 256
HEADS = 8
HD = D // HEADS
EPSILON = 1e-05
MASKED = -1e30
SCALE = HD ** (-0.5)
LOG2E = 1.4426950408889634
BF = jnp.bfloat16
F32 = jnp.float32


def mm(left, right):
    return lax.dot_general(left, right, (((1,), (0,)), ((), ())), preferred_element_type=F32)


def mm_t(left, right):
    return lax.dot_general(left, right, (((1,), (1,)), ((), ())), preferred_element_type=F32)


def iota(shape, axis):
    return lax.broadcasted_iota(jnp.int32, shape, axis)


def vmem_call(kernel, outs, name, limit=40 << 20):
    return pl.pallas_call(
        kernel,
        out_shape=outs,
        name=name,
        compiler_params=pltpu.CompilerParams(vmem_limit_bytes=limit),
    )


def destination_row(own_row):
    points = own_row.shape[1]
    rows, cols = iota((points, points), 0), iota((points, points), 1)
    wide = jnp.broadcast_to(own_row, (points, points))
    own_col = jnp.sum(jnp.where(rows == cols, wide, 0.0), axis=1, keepdims=True)
    same = jnp.where((own_col == wide) & (rows < cols), 1.0, 0.0)
    rank = jnp.sum(same, axis=0, keepdims=True)
    return own_row * 8.0 + rank


def one_hot(dest_row, slots):
    shape = (slots, dest_row.shape[1])
    return jnp.where(iota(shape, 0).astype(F32) == dest_row, 1.0, 0.0).astype(BF)


def key_bias(owners, my_index):
    devices = owners.shape[0]
    count = jnp.sum(jnp.where(owners == my_index, 1.0, 0.0), axis=1, keepdims=True)
    shape = (devices * 8, devices)
    spread = jnp.where(iota(shape, 0) // 8 == iota(shape, 1), 1.0, 0.0).astype(BF)
    slot_count = mm(spread, jnp.broadcast_to(count, (devices, 128)).astype(BF))
    rank = (iota(slot_count.shape, 0) % 8).astype(F32)
    return jnp.where(rank < slot_count, 0.0, MASKED).astype(BF)


def route_first_kernel(index_ref, owners_ref, x_ref, dest_ref, out_ref):
    my = index_ref[0]
    dest = destination_row(owners_ref[pl.ds(my, 1), :].astype(F32))
    dest_ref[...] = jnp.broadcast_to(dest, dest_ref.shape)
    out_ref[...] = mm(one_hot(dest, out_ref.shape[0]), x_ref[...]).astype(BF)


def route_second_kernel(
    index_ref, owners_one_ref, owners_zero_ref, dest_one_ref, g_ref, x_ref, dest_ref, out_ref, bias_ref
):
    my = index_ref[0]
    slots = out_ref.shape[0]
    out_ref[:, :D] = mm(one_hot(dest_one_ref[0:1, :], slots), g_ref[...]).astype(BF)
    dest = destination_row(owners_zero_ref[pl.ds(my, 1), :].astype(F32))
    dest_ref[...] = jnp.broadcast_to(dest, dest_ref.shape)
    out_ref[:, D:] = mm(one_hot(dest, slots), x_ref[...]).astype(BF)
    bias_ref[1] = key_bias(owners_one_ref[...], my)
    bias_ref[0] = key_bias(owners_zero_ref[...], my)


def unpack(dest_row, rows):
    hot = one_hot(dest_row, rows.shape[0])
    return lax.dot_general(hot, rows, (((0,), (0,)), ((), ())), preferred_element_type=F32).astype(BF)


def repack_kernel(dest_one_ref, dest_zero_ref, rows_ref, out_ref):
    gradient = unpack(dest_one_ref[0:1, :], rows_ref[...])
    out_ref[...] = mm(one_hot(dest_zero_ref[0:1, :], out_ref.shape[0]), gradient).astype(BF)


def unpack_kernel(dest_ref, rows_ref, out_ref):
    out_ref[...] = unpack(dest_ref[0:1, :], rows_ref[...])


def normalized(values):
    centered = values - jnp.mean(values, axis=1, keepdims=True)
    inverse = lax.rsqrt(jnp.mean(centered * centered, axis=1, keepdims=True) + EPSILON)
    return centered * inverse, inverse


def norm_gradient(upstream, hat, inverse):
    mean_one = jnp.mean(upstream, axis=1, keepdims=True)
    mean_two = jnp.mean(upstream * hat, axis=1, keepdims=True)
    return inverse * (upstream - mean_one - hat * mean_two)


def head_lanes(shape, head):
    lane = iota(shape, 1)
    return (lane >= head * HD) & (lane < head * HD + HD)


def gelu_slope(pre):
    root, cubic = 0.7978845608028654, 0.044715
    square = pre * pre
    bend = jnp.tanh(root * (pre + cubic * (pre * square)))
    return 0.5 * (1.0 + bend) + 0.5 * pre * (1.0 - bend * bend) * (root * (1.0 + 3.0 * cubic * square))


def forward_kernel(
    x_ref, bias_ref, attend_ref, output_ref, up_ref,
    qkv_ref, probs_ref, hat_ref, inverse_ref, slope_ref,
    value_t_ref, mixed_t_ref,
):
    x = x_ref[...].astype(F32)
    normed, _ = normalized(x)
    qkv = mm(normed.astype(BF), attend_ref[...]).astype(BF)
    qkv_ref[...] = qkv
    value_t_ref[...] = qkv[:, 2 * D :].T
    slots = x.shape[0]

    def one_head(head, carry):
        spare = jnp.where(head == 0, D - 1, 0)
        lane = iota((slots, D), 1)
        bias = jnp.concatenate([bias_ref[...], bias_ref[...]], axis=1)
        keys = jnp.where(
            head_lanes((slots, D), head),
            qkv_ref[:, D : 2 * D],
            jnp.where(lane == spare, bias, jnp.zeros_like(bias)),
        )
        queries = jnp.where(lane == spare, jnp.ones((slots, D), BF), qkv_ref[:, :D])
        scores = mm_t(keys, queries)
        largest = jnp.max(scores, axis=0, keepdims=True)
        exponent = jnp.exp2((scores - largest) * (SCALE * LOG2E))
        total = jnp.sum(exponent, axis=0, keepdims=True)
        probs = (exponent * (1.0 / total)).astype(BF)
        probs_ref[head] = probs
        at = pl.multiple_of(head * HD, HD)
        mixed_t_ref[pl.ds(at, HD), :] = mm(value_t_ref[pl.ds(at, HD), :], probs)
        return carry

    lax.fori_loop(0, HEADS, one_head, 0)
    attended = mixed_t_ref[...].astype(BF).T
    mixed = mm(attended, output_ref[...]).astype(BF).astype(F32)
    hat, inverse = normalized(x + mixed)
    hat_ref[...] = hat
    inverse_ref[...] = inverse
    slope_ref[...] = gelu_slope(mm(hat.astype(BF), up_ref[...]))


def backward_kernel(
    x_ref, g_ref, qkv_ref, probs_ref, hat_ref, inverse_ref, slope_ref,
    attend_ref, output_ref, up_ref, down_ref,
    out_ref,
    key_t_ref, query_grad_ref, key_grad_ref, value_grad_ref, up_grad_ref,
):
    g = g_ref[...]
    slots = g.shape[0]
    pre_grad = (slope_ref[...] * mm_t(g, down_ref[...])).astype(BF)
    grad_mid = (
        g.astype(F32) + norm_gradient(mm_t(pre_grad, up_ref[...]), hat_ref[...], inverse_ref[...])
    ).astype(BF)
    up_grad_ref[...] = mm_t(grad_mid, output_ref[...]).astype(BF)
    key_t_ref[...] = qkv_ref[:, D : 2 * D].T
    key_grad_ref[...] = jnp.zeros_like(key_grad_ref)
    value_grad_ref[...] = jnp.zeros_like(value_grad_ref)

    def one_head(head, carry):
        inside = head_lanes((slots, D), head)
        zero = jnp.zeros((slots, D), BF)
        values = jnp.where(inside, qkv_ref[:, 2 * D :], zero)
        prob_grads = mm_t(values, up_grad_ref[...])
        rounded = probs_ref[head]
        probs = rounded.astype(F32)
        total = jnp.sum(prob_grads * probs, axis=0, keepdims=True)
        score_grads = (probs * (prob_grads - total)).astype(BF)
        value_grad_ref[...] += mm(rounded, jnp.where(inside, up_grad_ref[...], zero))
        key_grad_ref[...] += mm(score_grads, jnp.where(inside, qkv_ref[:, :D], zero))
        at = pl.multiple_of(head * HD, HD)
        query_grad_ref[pl.ds(at, HD), :] = mm(key_t_ref[pl.ds(at, HD), :], score_grads)
        return carry

    lax.fori_loop(0, HEADS, one_head, 0)
    query_grads = (query_grad_ref[...] * SCALE).astype(BF).T
    key_grads = (key_grad_ref[...] * SCALE).astype(BF)
    value_grads = value_grad_ref[...].astype(BF)
    normed_grads = (
        mm_t(query_grads, attend_ref[:, :D])
        + mm_t(key_grads, attend_ref[:, D : 2 * D])
        + mm_t(value_grads, attend_ref[:, 2 * D :])
    )
    hat, inverse = normalized(x_ref[...].astype(F32))
    branch = norm_gradient(normed_grads, hat, inverse).astype(BF)
    out_ref[...] = (grad_mid.astype(F32) + branch.astype(F32)).astype(BF)


def forward(x, bias, attend, output, up):
    slots = x.shape[0]
    hidden = up.shape[1]
    return pl.pallas_call(
        forward_kernel,
        out_shape=(
            jax.ShapeDtypeStruct((slots, 3 * D), BF),
            jax.ShapeDtypeStruct((HEADS, slots, slots), BF),
            jax.ShapeDtypeStruct((slots, D), F32),
            jax.ShapeDtypeStruct((slots, 1), F32),
            jax.ShapeDtypeStruct((slots, hidden), F32),
        ),
        scratch_shapes=[pltpu.VMEM((D, slots), BF), pltpu.VMEM((D, slots), F32)],
        name="layer_forward",
        compiler_params=pltpu.CompilerParams(vmem_limit_bytes=40 << 20),
    )(x, bias, attend, output, up)


def backward(x, g, saved, attend, output, up, down):
    slots = x.shape[0]
    return pl.pallas_call(
        backward_kernel,
        out_shape=jax.ShapeDtypeStruct((slots, D), BF),
        scratch_shapes=[
            pltpu.VMEM((D, slots), BF),
            pltpu.VMEM((D, slots), F32),
            pltpu.VMEM((slots, D), F32),
            pltpu.VMEM((slots, D), F32),
            pltpu.VMEM((slots, D), BF),
        ],
        name="layer_backward",
        compiler_params=pltpu.CompilerParams(vmem_limit_bytes=40 << 20),
    )(x, g, *saved, attend, output, up, down)


def per_device(saved_inputs, output_grads, owner_ids, attend, output, up, down):
    devices = lax.axis_size("blk")
    points = saved_inputs.shape[1]
    slots = devices * 8
    my_index = lax.axis_index("blk").astype(jnp.int32).reshape(1)
    owners = owner_ids.reshape(2, devices, points)

    def exchange(rows):
        width = rows.shape[1]
        moved = lax.all_to_all(
            rows.reshape(devices, 8, width), "blk", split_axis=0, concat_axis=0, tiled=True
        )
        return moved.reshape(slots, width)

    smem = pl.BlockSpec(memory_space=pltpu.SMEM)
    vmem = pl.BlockSpec(memory_space=pltpu.VMEM)
    dest_shape = jax.ShapeDtypeStruct((8, points), F32)
    dest_one, packed_x = pl.pallas_call(
        route_first_kernel,
        out_shape=(dest_shape, jax.ShapeDtypeStruct((slots, D), BF)),
        in_specs=[smem, vmem, vmem],
        name="route_first",
    )(my_index, owners[1], saved_inputs[1])
    x_one = exchange(packed_x)
    dest_zero, packed_gx, bias = pl.pallas_call(
        route_second_kernel,
        out_shape=(
            dest_shape,
            jax.ShapeDtypeStruct((slots, 2 * D), BF),
            jax.ShapeDtypeStruct((2, slots, 128), BF),
        ),
        in_specs=[smem] + [vmem] * 5,
        name="route_second",
    )(my_index, owners[1], owners[0], dest_one, output_grads, saved_inputs[0])
    gx = exchange(packed_gx)
    saved_one = forward(x_one, bias[1], attend[1], output[1], up[1])
    result = backward(x_one, gx[:, :D], saved_one, attend[1], output[1], up[1], down[1])
    returned = exchange(result)
    x_zero = gx[:, D:]
    saved_zero = forward(x_zero, bias[0], attend[0], output[0], up[0])
    packed_g = vmem_call(repack_kernel, jax.ShapeDtypeStruct((slots, D), BF), "repack")(
        dest_one, dest_zero, returned
    )
    g_zero = exchange(packed_g)
    result = backward(x_zero, g_zero, saved_zero, attend[0], output[0], up[0], down[0])
    returned = exchange(result)
    return vmem_call(unpack_kernel, jax.ShapeDtypeStruct((points, D), BF), "unpack")(
        dest_zero, returned
    )


def solution(mesh):
    placed = (
        P(None, ("rep", "blk"), None),
        P(("rep", "blk"), None),
        P(None, "rep", None),
        P(),
        P(),
        P(),
        P(),
    )
    return jax.shard_map(
        per_device, mesh=mesh, in_specs=placed, out_specs=P(("rep", "blk"), None), check_vma=False
    )
```

```python
import jax
import jax.numpy as jnp
from jax import lax
from jax.experimental import pallas as pl
from jax.experimental.pallas import tpu as pltpu
from jax.sharding import PartitionSpec as P

D = 256
HEADS = 8
HD = D // HEADS
EPSILON = 1e-05
MASKED = -1e30
SCALE = HD ** (-0.5)
LOG2E = 1.4426950408889634
BF = jnp.bfloat16
F32 = jnp.float32


def mm(left, right):
    return lax.dot_general(left, right, (((1,), (0,)), ((), ())), preferred_element_type=F32)


def mm_t(left, right):
    return lax.dot_general(left, right, (((1,), (1,)), ((), ())), preferred_element_type=F32)


def iota(shape, axis):
    return lax.broadcasted_iota(jnp.int32, shape, axis)


def vmem_call(kernel, outs, name, limit=40 << 20):
    return pl.pallas_call(
        kernel,
        out_shape=outs,
        name=name,
        compiler_params=pltpu.CompilerParams(vmem_limit_bytes=limit),
    )


def destination_row(own_row):
    points = own_row.shape[1]
    rows, cols = iota((points, points), 0), iota((points, points), 1)
    wide = jnp.broadcast_to(own_row, (points, points))
    own_col = jnp.sum(jnp.where(rows == cols, wide, 0.0), axis=1, keepdims=True)
    same = jnp.where((own_col == wide) & (rows < cols), 1.0, 0.0)
    rank = jnp.sum(same, axis=0, keepdims=True)
    return own_row * 8.0 + rank


def one_hot(dest_row, slots):
    shape = (slots, dest_row.shape[1])
    return jnp.where(iota(shape, 0).astype(F32) == dest_row, 1.0, 0.0).astype(BF)


def key_bias(owners, my_index):
    devices = owners.shape[0]
    count = jnp.sum(jnp.where(owners == my_index, 1.0, 0.0), axis=1, keepdims=True)
    shape = (devices * 8, devices)
    spread = jnp.where(iota(shape, 0) // 8 == iota(shape, 1), 1.0, 0.0).astype(BF)
    slot_count = mm(spread, jnp.broadcast_to(count, (devices, 128)).astype(BF))
    rank = (iota(slot_count.shape, 0) % 8).astype(F32)
    return jnp.where(rank < slot_count, 0.0, MASKED).astype(BF)


def route_kernel(index_ref, owners_ref, x_ref, g_ref, dest_ref, out_ref):
    dest = destination_row(owners_ref[pl.ds(index_ref[0], 1), :].astype(F32))
    dest_ref[...] = jnp.broadcast_to(dest, dest_ref.shape)
    hot = one_hot(dest, out_ref.shape[0])
    out_ref[:, :D] = mm(hot, x_ref[...]).astype(BF)
    out_ref[:, D:] = mm(hot, g_ref[...]).astype(BF)


def unpack(dest_row, rows):
    hot = one_hot(dest_row, rows.shape[0])
    return lax.dot_general(hot, rows, (((0,), (0,)), ((), ())), preferred_element_type=F32).astype(BF)


def repack_kernel(dest_one_ref, dest_zero_ref, rows_ref, out_ref):
    gradient = unpack(dest_one_ref[0:1, :], rows_ref[:, :D])
    out_ref[...] = mm(one_hot(dest_zero_ref[0:1, :], out_ref.shape[0]), gradient).astype(BF)


def unpack_kernel(dest_ref, rows_ref, out_ref):
    out_ref[...] = unpack(dest_ref[0:1, :], rows_ref[...])


def normalized(values):
    centered = values - jnp.mean(values, axis=1, keepdims=True)
    inverse = lax.rsqrt(jnp.mean(centered * centered, axis=1, keepdims=True) + EPSILON)
    return centered * inverse, inverse


def norm_gradient(upstream, hat, inverse):
    mean_one = jnp.mean(upstream, axis=1, keepdims=True)
    mean_two = jnp.mean(upstream * hat, axis=1, keepdims=True)
    return inverse * (upstream - mean_one - hat * mean_two)


def head_lanes(shape, head):
    lane = iota(shape, 1)
    return (lane >= head * HD) & (lane < head * HD + HD)


def gelu_slope(pre):
    root, cubic = 0.7978845608028654, 0.044715
    square = pre * pre
    bend = jnp.tanh(root * (pre + cubic * (pre * square)))
    return 0.5 * (1.0 + bend) + 0.5 * pre * (1.0 - bend * bend) * (root * (1.0 + 3.0 * cubic * square))


def forward_part(
    x, bias_ref, attend_ref, output_ref, up_ref,
    qkv_ref, probs_ref, rest_ref, value_t_ref, mixed_t_ref, after_head,
):
    normed, _ = normalized(x)
    qkv = mm(normed.astype(BF), attend_ref[...]).astype(BF)
    qkv_ref[...] = qkv
    value_t_ref[...] = qkv[:, 2 * D :].T
    slots = x.shape[0]

    def one_head(head, carry):
        spare = jnp.where(head == 0, D - 1, 0)
        lane = iota((slots, D), 1)
        bias = jnp.concatenate([bias_ref[...], bias_ref[...]], axis=1)
        keys = jnp.where(
            head_lanes((slots, D), head),
            qkv_ref[:, D : 2 * D],
            jnp.where(lane == spare, bias, jnp.zeros_like(bias)),
        )
        queries = jnp.where(lane == spare, jnp.ones((slots, D), BF), qkv_ref[:, :D])
        scores = mm_t(keys, queries)
        largest = jnp.max(scores, axis=0, keepdims=True)
        exponent = jnp.exp2((scores - largest) * (SCALE * LOG2E))
        total = jnp.sum(exponent, axis=0, keepdims=True)
        probs = (exponent * (1.0 / total)).astype(BF)
        probs_ref[head] = probs
        after_head(head)
        at = pl.multiple_of(head * HD, HD)
        mixed_t_ref[pl.ds(at, HD), :] = mm(value_t_ref[pl.ds(at, HD), :], probs)
        return carry

    lax.fori_loop(0, HEADS, one_head, 0)
    attended = mixed_t_ref[...].astype(BF).T
    mixed = mm(attended, output_ref[...]).astype(BF).astype(F32)
    hat, inverse = normalized(x + mixed)
    hidden = up_ref.shape[1]
    rest_ref[:, hidden : hidden + D] = hat
    rest_ref[:, hidden + D :] = jnp.broadcast_to(inverse, (slots, 128))
    rest_ref[:, :hidden] = gelu_slope(mm(hat.astype(BF), up_ref[...]))


def backward_part(
    x, g, qkv_ref, probs_ref, rest_ref,
    attend_ref, output_ref, up_ref, down_ref,
    key_t_ref, query_grad_ref, key_grad_ref, value_grad_ref, up_grad_ref, before_rest, before_head,
):
    slots = g.shape[0]
    hidden_grad = mm_t(g, down_ref[...])
    before_rest()
    hidden = up_ref.shape[1]
    pre_grad = (rest_ref[:, :hidden] * hidden_grad).astype(BF)
    hat, inverse = rest_ref[:, hidden : hidden + D], rest_ref[:, hidden + D : hidden + D + 1]
    grad_mid = (
        g.astype(F32) + norm_gradient(mm_t(pre_grad, up_ref[...]), hat, inverse)
    ).astype(BF)
    up_grad_ref[...] = mm_t(grad_mid, output_ref[...]).astype(BF)
    key_t_ref[...] = qkv_ref[:, D : 2 * D].T
    key_grad_ref[...] = jnp.zeros_like(key_grad_ref)
    value_grad_ref[...] = jnp.zeros_like(value_grad_ref)

    def one_head(head, carry):
        inside = head_lanes((slots, D), head)
        zero = jnp.zeros((slots, D), BF)
        values = jnp.where(inside, qkv_ref[:, 2 * D :], zero)
        prob_grads = mm_t(values, up_grad_ref[...])
        before_head(head)
        rounded = probs_ref[head]
        probs = rounded.astype(F32)
        total = jnp.sum(prob_grads * probs, axis=0, keepdims=True)
        score_grads = (probs * (prob_grads - total)).astype(BF)
        value_grad_ref[...] += mm(rounded, jnp.where(inside, up_grad_ref[...], zero))
        key_grad_ref[...] += mm(score_grads, jnp.where(inside, qkv_ref[:, :D], zero))
        at = pl.multiple_of(head * HD, HD)
        query_grad_ref[pl.ds(at, HD), :] = mm(key_t_ref[pl.ds(at, HD), :], score_grads)
        return carry

    lax.fori_loop(0, HEADS, one_head, 0)
    query_grads = (query_grad_ref[...] * SCALE).astype(BF).T
    key_grads = (key_grad_ref[...] * SCALE).astype(BF)
    value_grads = value_grad_ref[...].astype(BF)
    normed_grads = (
        mm_t(query_grads, attend_ref[:, :D])
        + mm_t(key_grads, attend_ref[:, D : 2 * D])
        + mm_t(value_grads, attend_ref[:, 2 * D :])
    )
    hat, inverse = normalized(x)
    branch = norm_gradient(normed_grads, hat, inverse).astype(BF)
    return (grad_mid.astype(F32) + branch.astype(F32)).astype(BF)


def nothing(*_):
    return None


def whole_layer_kernel(
    index_ref, owners_one_ref, owners_zero_ref, xg_ref, next_x_ref,
    attend_ref, output_ref, up_ref, down_ref,
    out_ref, dest_ref, next_bias_ref,
    bias_ref, qkv_ref, probs_ref, rest_ref,
    value_t_ref, mixed_t_ref, query_grad_ref, key_grad_ref, value_grad_ref, up_grad_ref,
):
    my = index_ref[0]
    bias_ref[...] = key_bias(owners_one_ref[...], my)
    next_bias_ref[...] = key_bias(owners_zero_ref[...], my)
    dest = destination_row(owners_zero_ref[pl.ds(my, 1), :].astype(F32))
    dest_ref[...] = jnp.broadcast_to(dest, dest_ref.shape)
    out_ref[:, D:] = mm(one_hot(dest, out_ref.shape[0]), next_x_ref[...]).astype(BF)
    saved = (qkv_ref, probs_ref, rest_ref)
    forward_part(
        xg_ref[:, :D].astype(F32), bias_ref, attend_ref, output_ref, up_ref,
        *saved, value_t_ref, mixed_t_ref, nothing,
    )
    out_ref[:, :D] = backward_part(
        xg_ref[:, :D].astype(F32), xg_ref[:, D:], *saved,
        attend_ref, output_ref, up_ref, down_ref,
        value_t_ref, query_grad_ref, key_grad_ref, value_grad_ref, up_grad_ref, nothing, nothing,
    )


def forward_kernel(
    rx_ref, bias_ref, attend_ref, output_ref, up_ref,
    qkv_ref, probs_out_ref, rest_out_ref,
    probs_ref, rest_ref, value_t_ref, mixed_t_ref, probs_sem, rest_sem,
):
    def probs_copy(head):
        return pltpu.make_async_copy(probs_ref.at[head], probs_out_ref.at[head], probs_sem.at[head])

    forward_part(
        rx_ref[:, D:].astype(F32), bias_ref, attend_ref, output_ref, up_ref,
        qkv_ref, probs_ref, rest_ref,
        value_t_ref, mixed_t_ref, lambda head: probs_copy(head).start(),
    )
    rest_copy = pltpu.make_async_copy(rest_ref, rest_out_ref, rest_sem)
    rest_copy.start()
    for head in range(HEADS):
        probs_copy(head).wait()
    rest_copy.wait()


def backward_kernel(
    rx_ref, g_ref, qkv_ref, probs_in_ref, rest_in_ref,
    attend_ref, output_ref, up_ref, down_ref,
    out_ref,
    probs_ref, rest_ref, key_t_ref, query_grad_ref, key_grad_ref, value_grad_ref, up_grad_ref,
    probs_sem, rest_sem,
):
    def probs_copy(head):
        return pltpu.make_async_copy(probs_in_ref.at[head], probs_ref.at[head], probs_sem.at[head])

    rest_copy = pltpu.make_async_copy(rest_in_ref, rest_ref, rest_sem)
    rest_copy.start()
    for head in range(HEADS):
        probs_copy(head).start()
    out_ref[...] = backward_part(
        rx_ref[:, D:].astype(F32), g_ref[...], qkv_ref, probs_ref, rest_ref,
        attend_ref, output_ref, up_ref, down_ref,
        key_t_ref, query_grad_ref, key_grad_ref, value_grad_ref, up_grad_ref,
        rest_copy.wait, lambda head: probs_copy(head).wait(),
    )


SMEM_SPEC = pl.BlockSpec(memory_space=pltpu.SMEM)
VMEM_SPEC = pl.BlockSpec(memory_space=pltpu.VMEM)
HBM_SPEC = pl.BlockSpec(memory_space=pltpu.HBM)


def saved_shapes(slots, hidden):
    return dict(
        qkv=((slots, 3 * D), BF),
        probs=((HEADS, slots, slots), BF),
        rest=((slots, hidden + D + 128), F32),
    )


def gradient_scratch(slots):
    return [
        pltpu.VMEM((D, slots), BF),
        pltpu.VMEM((D, slots), F32),
        pltpu.VMEM((slots, D), F32),
        pltpu.VMEM((slots, D), F32),
        pltpu.VMEM((slots, D), BF),
    ]


def params():
    return pltpu.CompilerParams(vmem_limit_bytes=40 << 20)


def whole_layer(my_index, owners_one, owners_zero, xg, next_x, attend, output, up, down):
    slots, hidden = xg.shape[0], up.shape[1]
    shape = saved_shapes(slots, hidden)
    gradients = gradient_scratch(slots)
    return pl.pallas_call(
        whole_layer_kernel,
        out_shape=(
            jax.ShapeDtypeStruct((slots, 2 * D), BF),
            jax.ShapeDtypeStruct((8, next_x.shape[0]), F32),
            jax.ShapeDtypeStruct((slots, 128), BF),
        ),
        in_specs=[SMEM_SPEC] + [VMEM_SPEC] * 8,
        scratch_shapes=[pltpu.VMEM((slots, 128), BF)]
        + [pltpu.VMEM(*shape[n]) for n in ("qkv", "probs", "rest")]
        + [gradients[0], pltpu.VMEM((D, slots), F32)]
        + gradients[1:],
        name="whole_layer",
        compiler_params=params(),
    )(my_index, owners_one, owners_zero, xg, next_x, attend, output, up, down)


def forward(rx, bias, attend, output, up):
    slots, hidden = rx.shape[0], up.shape[1]
    shape = saved_shapes(slots, hidden)
    return pl.pallas_call(
        forward_kernel,
        out_shape=(
            jax.ShapeDtypeStruct(*shape["qkv"]),
            pltpu.HBM(*shape["probs"]),
            pltpu.HBM(*shape["rest"]),
        ),
        out_specs=(VMEM_SPEC, HBM_SPEC, HBM_SPEC),
        scratch_shapes=[
            pltpu.VMEM(*shape["probs"]),
            pltpu.VMEM(*shape["rest"]),
            pltpu.VMEM((D, slots), BF),
            pltpu.VMEM((D, slots), F32),
            pltpu.SemaphoreType.DMA((HEADS,)),
            pltpu.SemaphoreType.DMA,
        ],
        name="layer_forward",
        compiler_params=params(),
    )(rx, bias, attend, output, up)


def backward(rx, g, saved, attend, output, up, down):
    slots, hidden = g.shape[0], up.shape[1]
    shape = saved_shapes(slots, hidden)
    return pl.pallas_call(
        backward_kernel,
        out_shape=jax.ShapeDtypeStruct((slots, D), BF),
        in_specs=[VMEM_SPEC] * 3 + [HBM_SPEC] * 2 + [VMEM_SPEC] * 4,
        scratch_shapes=[pltpu.VMEM(*shape["probs"]), pltpu.VMEM(*shape["rest"])]
        + gradient_scratch(slots)
        + [pltpu.SemaphoreType.DMA((HEADS,)), pltpu.SemaphoreType.DMA],
        name="layer_backward",
        compiler_params=params(),
    )(
        rx, g, saved[0],
        *(pltpu.with_memory_space_constraint(s, pltpu.HBM) for s in saved[1:]),
        attend, output, up, down,
    )


def per_device(saved_inputs, output_grads, owner_ids, attend, output, up, down):
    devices = lax.axis_size("blk")
    points = saved_inputs.shape[1]
    slots = devices * 8
    my_index = lax.axis_index("blk").astype(jnp.int32).reshape(1)
    owners = owner_ids.reshape(2, devices, points)

    def exchange(rows):
        width = rows.shape[1]
        moved = lax.all_to_all(
            rows.reshape(devices, 8, width), "blk", split_axis=0, concat_axis=0, tiled=True
        )
        return moved.reshape(slots, width)

    dest_one, packed = pl.pallas_call(
        route_kernel,
        out_shape=(
            jax.ShapeDtypeStruct((8, points), F32),
            jax.ShapeDtypeStruct((slots, 2 * D), BF),
        ),
        in_specs=[SMEM_SPEC] + [VMEM_SPEC] * 3,
        name="route",
    )(my_index, owners[1], saved_inputs[1], output_grads)
    xg = exchange(packed)
    result, dest_zero, bias = whole_layer(
        my_index, owners[1], owners[0], xg, saved_inputs[0], attend[1], output[1], up[1], down[1]
    )
    rx = exchange(result)
    packed = vmem_call(repack_kernel, jax.ShapeDtypeStruct((slots, D), BF), "repack")(
        dest_one, dest_zero, rx
    )
    g_zero = exchange(packed)
    saved = forward(rx, bias, attend[0], output[0], up[0])
    result = backward(rx, g_zero, saved, attend[0], output[0], up[0], down[0])
    return vmem_call(unpack_kernel, jax.ShapeDtypeStruct((points, D), BF), "unpack")(
        dest_zero, exchange(result)
    )


def solution(mesh):
    placed = (
        P(None, ("rep", "blk"), None),
        P(("rep", "blk"), None),
        P(None, "rep", None),
        P(),
        P(),
        P(),
        P(),
    )
    return jax.shard_map(
        per_device, mesh=mesh, in_specs=placed, out_specs=P(("rep", "blk"), None), check_vma=False
    )
```

```python
import jax
import jax.numpy as jnp
from jax import lax
from jax.experimental import pallas as pl
from jax.experimental.pallas import tpu as pltpu
from jax.sharding import PartitionSpec as P

D = 256
HEADS = 8
HD = D // HEADS
EPSILON = 1e-05
MASKED = -1e30
SCALE = HD ** (-0.5)
LOG2E = 1.4426950408889634
BF = jnp.bfloat16
F32 = jnp.float32


def mm(left, right):
    return lax.dot_general(left, right, (((1,), (0,)), ((), ())), preferred_element_type=F32)


def mm_t(left, right):
    return lax.dot_general(left, right, (((1,), (1,)), ((), ())), preferred_element_type=F32)


def iota(shape, axis):
    return lax.broadcasted_iota(jnp.int32, shape, axis)


def destination_row(owners, my_index, points):
    wide_rows = points // LANES
    own_row = jnp.concatenate(
        [owners[pl.ds(my_index * wide_rows + i, 1), :] for i in range(wide_rows)], axis=1
    ).astype(F32)
    rows, cols = iota((points, points), 0), iota((points, points), 1)
    wide = jnp.broadcast_to(own_row, (points, points))
    own_col = jnp.sum(jnp.where(rows == cols, wide, 0.0), axis=1, keepdims=True)
    same = jnp.where((own_col == wide) & (rows < cols), 1.0, 0.0)
    rank = jnp.sum(same, axis=0, keepdims=True)
    return own_row * 8.0 + rank


def one_hot(dest_row, slots):
    shape = (slots, dest_row.shape[1])
    return jnp.where(iota(shape, 0).astype(F32) == dest_row, 1.0, 0.0).astype(BF)


def key_bias(owners, my_index, slots):
    rows = owners.shape[0]
    per_source = rows * 8 // slots
    count = jnp.sum(jnp.where(owners == my_index, 1.0, 0.0), axis=1, keepdims=True)
    shape = (slots, rows)
    spread = jnp.where(iota(shape, 0) // 8 == iota(shape, 1) // per_source, 1.0, 0.0).astype(BF)
    slot_count = mm(spread, jnp.broadcast_to(count, (rows, D)).astype(BF))
    rank = (iota(slot_count.shape, 0) % 8).astype(F32)
    return jnp.where(rank < slot_count, 0.0, MASKED).astype(BF)


def unpack(dest_row, rows):
    hot = one_hot(dest_row, rows.shape[0])
    return lax.dot_general(hot, rows, (((0,), (0,)), ((), ())), preferred_element_type=F32).astype(BF)


def fetch(sem, pairs):
    copies = [pltpu.make_async_copy(a, b, sem.at[i]) for i, (a, b) in enumerate(pairs)]
    for copy in copies:
        copy.start()
    return copies


def route_kernel(
    index_ref, owners_hbm, saved_hbm, g_hbm, dest_ref, out_ref, owners_ref, x_ref, g_ref, sem
):
    slots, points = out_ref.shape[0], g_hbm.shape[0]
    owners_in, x_in, g_in = fetch(
        sem, [(owners_hbm.at[1], owners_ref), (saved_hbm.at[1], x_ref), (g_hbm, g_ref)]
    )
    owners_in.wait()
    dest = destination_row(owners_ref, index_ref[0], points)
    dest_ref[...] = jnp.broadcast_to(dest, dest_ref.shape)
    hot = one_hot(dest, slots)
    x_in.wait()
    out_ref[:, :D] = mm(hot, x_ref[...]).astype(BF)
    g_in.wait()
    out_ref[:, D:] = mm(hot, g_ref[...]).astype(BF)


def repack_kernel(dest_one_ref, dest_zero_ref, rows_ref, out_ref):
    gradient = unpack(dest_one_ref[0:1, :], rows_ref[:, :D])
    out_ref[...] = mm(one_hot(dest_zero_ref[0:1, :], out_ref.shape[0]), gradient).astype(BF)


def unpack_kernel(dest_ref, rows_ref, out_ref):
    out_ref[...] = unpack(dest_ref[0:1, :], rows_ref[...])


def normalized(values):
    centered = values - jnp.mean(values, axis=1, keepdims=True)
    inverse = lax.rsqrt(jnp.mean(centered * centered, axis=1, keepdims=True) + EPSILON)
    return centered * inverse, inverse


def norm_gradient(upstream, hat, inverse):
    mean_one = jnp.mean(upstream, axis=1, keepdims=True)
    mean_two = jnp.mean(upstream * hat, axis=1, keepdims=True)
    return inverse * (upstream - mean_one - hat * mean_two)


def head_lanes(shape, head):
    lane = iota(shape, 1)
    return (lane >= head * HD) & (lane < head * HD + HD)


def gelu_slope(pre):
    root, cubic = 0.7978845608028654, 0.044715
    square = pre * pre
    bend = jnp.tanh(pre * (root + (root * cubic) * square))
    rise = pre * (root + (3.0 * root * cubic) * square)
    return (0.5 + 0.5 * bend) * (1.0 + (1.0 - bend) * rise)


HALVES = 2
LANES = 128


def forward_part(x, weights, kept, work, wait, after_head):
    attend_ref, output_ref, up_ref, _ = weights
    qkv_ref, probs_ref, slope_ref, norm_ref, mixed_t_ref = kept
    bias_ref, query_ref, value_t_ref, even_ref, odd_ref, even_max_ref, odd_max_ref = work
    slots = x.shape[0]
    half = slots // HALVES
    normed, _ = normalized(x)
    wait("attend")
    qkv = mm(normed.astype(BF), attend_ref[...]).astype(BF)
    qkv_ref[...] = qkv
    value_t_ref[...] = qkv[:, 2 * D :].T
    lane = iota((slots, D), 1)
    query_ref[...] = jnp.where(lane == 0, jnp.ones((slots, D), BF), qkv[:, :D])
    wait("owners")

    def score_half(keys, queries, part, scores_ref, max_ref):
        cols = slice(part * half, (part + 1) * half)
        scores = mm_t(keys, queries)
        scores_ref[:, cols] = scores
        max_ref[:, cols] = jnp.broadcast_to(jnp.max(scores, axis=0, keepdims=True), (8, half))

    def soft_half(head, part, scores_ref, max_ref):
        cols = slice(part * half, (part + 1) * half)
        largest = max_ref[0:1, cols]
        exponent = jnp.exp2((scores_ref[:, cols] - largest) * (SCALE * LOG2E))
        total = jnp.sum(exponent, axis=0, keepdims=True)
        probs = (exponent * (1.0 / total)).astype(BF)
        probs_ref[head, :, cols] = probs
        at = pl.multiple_of(head * HD, HD)
        mixed_t_ref[pl.ds(at, HD), cols] = mm(value_t_ref[pl.ds(at, HD), :], probs)

    bias = bias_ref[...]
    first_keys = jnp.where(
        head_lanes((slots, D), 0),
        qkv[:, D : 2 * D],
        jnp.where(lane == D - 1, bias, jnp.zeros_like(bias)),
    )
    first_queries = jnp.where(lane == D - 1, jnp.ones((slots, D), BF), qkv[:, :D])
    bias_ref[...] = jnp.where(lane == 0, bias, jnp.zeros_like(bias))
    for part in range(HALVES):
        rows = slice(part * half, (part + 1) * half)
        score_half(first_keys, first_queries[rows], part, even_ref, even_max_ref)

    def step(head, following, here, here_max, there, there_max):
        keys = jnp.where(head_lanes((slots, D), following), qkv_ref[:, D : 2 * D], bias_ref[...])
        for part in range(HALVES):
            rows = slice(part * half, (part + 1) * half)
            score_half(keys, query_ref[rows, :], part, there, there_max)
            soft_half(head, part, here, here_max)
        after_head(head)

    def pair(index, carry):
        step(2 * index, 2 * index + 1, even_ref, even_max_ref, odd_ref, odd_max_ref)
        following = jnp.minimum(2 * index + 2, HEADS - 1)
        step(2 * index + 1, following, odd_ref, odd_max_ref, even_ref, even_max_ref)
        return carry

    lax.fori_loop(0, HEADS // 2, pair, 0)
    attended = mixed_t_ref[...].astype(BF).T
    wait("output")
    mixed = mm(attended, output_ref[...]).astype(BF).astype(F32)
    hat, inverse = normalized(x + mixed)
    norm_ref[:, :D] = hat
    norm_ref[:, D:] = jnp.broadcast_to(inverse, (slots, LANES))
    rounded = hat.astype(BF)
    wait("up")
    for part in range(slope_ref.shape[0]):
        slope_ref[part] = gelu_slope(mm(rounded, up_ref[:, part * D : (part + 1) * D]))


def backward_part(x, g, weights, kept, work, wait, before_head):
    attend_ref, output_ref, up_ref, down_ref = weights
    qkv_ref, probs_ref, slope_ref, norm_ref, mixed_t_ref = kept
    pre_grad_ref, up_grad_ref, up_grad_t_ref, query_t_ref, key_t_ref, delta_ref, grads_t_ref = work
    slots = g.shape[0]
    half = slots // HALVES
    query_t_ref[...] = qkv_ref[:, :D].T
    key_t_ref[...] = qkv_ref[:, D : 2 * D].T
    wait("down")
    for part in range(slope_ref.shape[0]):
        rows = slice(part * D, (part + 1) * D)
        hidden_grad = mm_t(g, down_ref[rows, :])
        wait("slope", part)
        pre_grad_ref[:, rows] = (slope_ref[part] * hidden_grad).astype(BF)
    wait("up")
    normed_grad = mm_t(pre_grad_ref[...], up_ref[...])
    wait("norm")
    grad_mid = (
        g.astype(F32) + norm_gradient(normed_grad, norm_ref[:, :D], norm_ref[:, D : D + 1])
    ).astype(BF)
    wait("output")
    up_grad_ref[...] = mm_t(grad_mid, output_ref[...]).astype(BF)
    up_grad_t = mm_t(output_ref[...], grad_mid).astype(BF)
    up_grad_t_ref[...] = up_grad_t
    wait("mixed")
    weighted = mixed_t_ref[...] * up_grad_t.astype(F32)
    for head in range(HEADS):
        delta_ref[head : head + 1, :] = jnp.sum(
            weighted[head * HD : (head + 1) * HD], axis=0, keepdims=True
        )

    def one_head(head, carry):
        values = jnp.where(
            head_lanes((slots, D), head), qkv_ref[:, 2 * D :], jnp.zeros((slots, D), BF)
        )
        at = pl.multiple_of(head * HD, HD)
        key_grad = value_grad = 0.0
        before_head(head)
        for part in range(HALVES):
            cols = slice(part * half, (part + 1) * half)
            prob_grads = mm_t(values, up_grad_ref[cols, :])
            probs = probs_ref[head, :, cols]
            delta = delta_ref[pl.ds(head, 1), cols]
            score_grads = (probs.astype(F32) * (prob_grads - delta)).astype(BF)
            value_grad += mm_t(up_grad_t_ref[pl.ds(at, HD), cols], probs)
            key_grad += mm_t(query_t_ref[pl.ds(at, HD), cols], score_grads)
            grads_t_ref[pl.ds(at, HD), cols] = (
                mm(key_t_ref[pl.ds(at, HD), :], score_grads) * SCALE
            ).astype(BF)
        grads_t_ref[pl.ds(pl.multiple_of(D + at, HD), HD), :] = (key_grad * SCALE).astype(BF)
        grads_t_ref[pl.ds(pl.multiple_of(2 * D + at, HD), HD), :] = value_grad.astype(BF)
        return carry

    lax.fori_loop(0, HEADS, one_head, 0, unroll=BACK_UNROLL)
    wait("attend")
    normed_grads = mm(attend_ref[...], grads_t_ref[...]).T
    hat, inverse = normalized(x)
    branch = norm_gradient(normed_grads, hat, inverse).astype(BF)
    return (grad_mid.astype(F32) + branch.astype(F32)).astype(BF)


BACK_UNROLL = 1


def whole_layer_kernel(
    index_ref, xg_ref, owners_hbm, saved_hbm, *rest
):
    weights_hbm, (out_ref, dest_ref), rest = rest[:4], rest[4:6], rest[6:]
    weights, kept, forward_work, backward_work = rest[:4], rest[4:9], rest[9:16], rest[16:23]
    owners_ref, next_x_ref, sem = rest[23:]
    my = index_ref[0]
    slots = out_ref.shape[0]
    copies = fetch(
        sem,
        [(weights_hbm[0].at[1], weights[0]), (owners_hbm, owners_ref)]
        + [(weights_hbm[i].at[1], weights[i]) for i in (1, 2, 3)]
        + [(saved_hbm.at[0], next_x_ref)],
    )
    order = dict(attend=0, owners=1, output=2, up=3, down=4)
    waited = set()

    def wait(name, part=0):
        if name in order and name not in waited:
            waited.add(name)
            copies[order[name]].wait()
            if name == "owners":
                forward_work[0][...] = key_bias(owners_ref[1], my, slots)

    forward_part(
        xg_ref[:, :D].astype(F32), weights, kept, forward_work, wait, lambda head: None
    )
    dest = destination_row(owners_ref.at[0], my, next_x_ref.shape[0])
    dest_ref[...] = jnp.broadcast_to(dest, dest_ref.shape)
    copies[5].wait()
    out_ref[:, D:] = mm(one_hot(dest, slots), next_x_ref[...]).astype(BF)
    out_ref[:, :D] = backward_part(
        xg_ref[:, :D].astype(F32), xg_ref[:, D:], weights, kept, backward_work, wait,
        lambda head: None,
    )


def forward_kernel(index_ref, rx_ref, owners_hbm, *rest):
    weights_hbm, rest = rest[:3], rest[3:]
    qkv_ref, probs_out, slope_out, norm_out, mixed_out = rest[:5]
    weights, kept, work = rest[5:8], (qkv_ref,) + rest[8:12], rest[12:19]
    owners_ref, in_sem, out_sem, probs_sem = rest[19:]
    my = index_ref[0]
    slots = rx_ref.shape[0]
    copies = fetch(
        in_sem,
        [(weights_hbm[0].at[0], weights[0]), (owners_hbm.at[0], owners_ref)]
        + [(weights_hbm[i].at[0], weights[i]) for i in (1, 2)],
    )
    order = dict(attend=0, owners=1, output=2, up=3)

    def wait(name, part=0):
        copies[order[name]].wait()
        if name == "owners":
            work[0][...] = key_bias(owners_ref[...], my, slots)

    def probs_copy(head):
        return pltpu.make_async_copy(kept[1].at[head], probs_out.at[head], probs_sem.at[head])

    forward_part(
        rx_ref[:, D:].astype(F32), tuple(weights) + (None,), kept, work, wait,
        lambda head: probs_copy(head).start(),
    )
    leaving = fetch(
        out_sem, [(kept[2], slope_out), (kept[3], norm_out), (kept[4], mixed_out)]
    )
    for head in range(HEADS):
        probs_copy(head).wait()
    for copy in leaving:
        copy.wait()


def backward_kernel(rx_ref, g_ref, qkv_ref, *rest):
    probs_hbm, slope_hbm, norm_hbm, mixed_hbm = rest[:4]
    weights_hbm, out_ref, rest = rest[4:8], rest[8], rest[9:]
    weights, kept, work = rest[:4], (qkv_ref,) + rest[4:8], rest[8:15]
    sem, probs_sem = rest[15:]
    parts = slope_hbm.shape[0]
    names = ["down"] + ["slope"] * parts + ["up", "norm", "output", "mixed", "attend"]

    def probs_copy(head):
        return pltpu.make_async_copy(probs_hbm.at[head], kept[1].at[head], probs_sem.at[head])

    copies = fetch(
        sem,
        [(weights_hbm[3].at[0], weights[3])]
        + [(slope_hbm.at[i], kept[2].at[i]) for i in range(parts)]
        + [
            (weights_hbm[2].at[0], weights[2]),
            (norm_hbm, kept[3]),
            (weights_hbm[1].at[0], weights[1]),
            (mixed_hbm, kept[4]),
            (weights_hbm[0].at[0], weights[0]),
        ],
    )
    for head in range(HEADS):
        probs_copy(head).start()

    def wait(name, part=0):
        copies[names.index(name) + part].wait()

    out_ref[...] = backward_part(
        rx_ref[:, D:].astype(F32), g_ref[...], weights, kept, work, wait,
        lambda head: probs_copy(head).wait(),
    )


SMEM_SPEC = pl.BlockSpec(memory_space=pltpu.SMEM)
VMEM_SPEC = pl.BlockSpec(memory_space=pltpu.VMEM)
HBM_SPEC = pl.BlockSpec(memory_space=pltpu.HBM)


def in_hbm(array):
    return pltpu.with_memory_space_constraint(array, pltpu.HBM)


def kept_shapes(slots, hidden):
    return [
        ((slots, 3 * D), BF),
        ((HEADS, slots, slots), BF),
        ((hidden // D, slots, D), F32),
        ((slots, D + LANES), F32),
        ((D, slots), F32),
    ]


def weight_scratch(weights):
    return [pltpu.VMEM(w.shape[1:], BF) for w in weights]


def forward_scratch(slots):
    return [
        pltpu.VMEM((slots, D), BF),
        pltpu.VMEM((slots, D), BF),
        pltpu.VMEM((D, slots), BF),
        pltpu.VMEM((slots, slots), F32),
        pltpu.VMEM((slots, slots), F32),
        pltpu.VMEM((8, slots), F32),
        pltpu.VMEM((8, slots), F32),
    ]


def backward_scratch(slots, hidden):
    return [
        pltpu.VMEM((slots, hidden), BF),
        pltpu.VMEM((slots, D), BF),
        pltpu.VMEM((D, slots), BF),
        pltpu.VMEM((D, slots), BF),
        pltpu.VMEM((D, slots), BF),
        pltpu.VMEM((HEADS, slots), F32),
        pltpu.VMEM((3 * D, slots), BF),
    ]


def call(kernel, outs, in_specs, out_specs, scratch, name):
    return pl.pallas_call(
        kernel,
        out_shape=outs,
        in_specs=in_specs,
        out_specs=out_specs,
        scratch_shapes=scratch,
        name=name,
        compiler_params=pltpu.CompilerParams(vmem_limit_bytes=40 << 20),
    )


def whole_layer(my_index, xg, owners, saved_inputs, weights):
    slots, hidden = xg.shape[0], weights[2].shape[2]
    points = saved_inputs.shape[1]
    return call(
        whole_layer_kernel,
        (jax.ShapeDtypeStruct((slots, 2 * D), BF), jax.ShapeDtypeStruct((8, points), F32)),
        [SMEM_SPEC, VMEM_SPEC] + [HBM_SPEC] * 6,
        (VMEM_SPEC, VMEM_SPEC),
        weight_scratch(weights)
        + [pltpu.VMEM(*k) for k in kept_shapes(slots, hidden)]
        + forward_scratch(slots)
        + backward_scratch(slots, hidden)
        + [
            pltpu.VMEM(owners.shape, jnp.int32),
            pltpu.VMEM((points, D), BF),
            pltpu.SemaphoreType.DMA((6,)),
        ],
        "whole_layer",
    )(my_index, xg, owners, saved_inputs, *weights)


def forward(my_index, rx, owners, weights):
    slots, hidden = rx.shape[0], weights[2].shape[2]
    shapes = kept_shapes(slots, hidden)
    return call(
        forward_kernel,
        (jax.ShapeDtypeStruct(*shapes[0]),) + tuple(pltpu.HBM(*k) for k in shapes[1:]),
        [SMEM_SPEC, VMEM_SPEC] + [HBM_SPEC] * 4,
        (VMEM_SPEC,) + (HBM_SPEC,) * 4,
        weight_scratch(weights[:3])
        + [pltpu.VMEM(*k) for k in shapes[1:]]
        + forward_scratch(slots)
        + [
            pltpu.VMEM(owners.shape[1:], jnp.int32),
            pltpu.SemaphoreType.DMA((4,)),
            pltpu.SemaphoreType.DMA((3,)),
            pltpu.SemaphoreType.DMA((HEADS,)),
        ],
        "layer_forward",
    )(my_index, rx, owners, *weights[:3])


def backward(rx, g, kept, weights):
    slots, hidden = g.shape[0], weights[2].shape[2]
    return call(
        backward_kernel,
        jax.ShapeDtypeStruct((slots, D), BF),
        [VMEM_SPEC] * 3 + [HBM_SPEC] * 8,
        VMEM_SPEC,
        weight_scratch(weights)
        + [pltpu.VMEM(*k) for k in kept_shapes(slots, hidden)[1:]]
        + backward_scratch(slots, hidden)
        + [
            pltpu.SemaphoreType.DMA((6 + hidden // D,)),
            pltpu.SemaphoreType.DMA((HEADS,)),
        ],
        "layer_backward",
    )(rx, g, kept[0], *(in_hbm(k) for k in kept[1:]), *weights)


def per_device(saved_inputs, output_grads, owner_ids, attend, output, up, down):
    devices = lax.axis_size("blk")
    points = saved_inputs.shape[1]
    slots = devices * 8
    my_index = lax.axis_index("blk").astype(jnp.int32).reshape(1)
    owners = in_hbm(owner_ids.reshape(2, devices * points // LANES, LANES))
    saved_inputs, output_grads = in_hbm(saved_inputs), in_hbm(output_grads)
    weights = tuple(in_hbm(w) for w in (attend, output, up, down))

    def exchange(rows):
        width = rows.shape[1]
        moved = lax.all_to_all(
            rows.reshape(devices, 8, width), "blk", split_axis=0, concat_axis=0, tiled=True
        )
        return moved.reshape(slots, width)

    dest_one, packed = call(
        route_kernel,
        (jax.ShapeDtypeStruct((8, points), F32), jax.ShapeDtypeStruct((slots, 2 * D), BF)),
        [SMEM_SPEC] + [HBM_SPEC] * 3,
        (VMEM_SPEC, VMEM_SPEC),
        [
            pltpu.VMEM(owners.shape[1:], jnp.int32),
            pltpu.VMEM((points, D), BF),
            pltpu.VMEM((points, D), BF),
            pltpu.SemaphoreType.DMA((3,)),
        ],
        "route",
    )(my_index, owners, saved_inputs, output_grads)
    xg = exchange(packed)
    result, dest_zero = whole_layer(my_index, xg, owners, saved_inputs, weights)
    rx = exchange(result)
    packed = call(
        repack_kernel, jax.ShapeDtypeStruct((slots, D), BF), [VMEM_SPEC] * 3, VMEM_SPEC, [], "repack"
    )(dest_one, dest_zero, rx)
    g_zero = exchange(packed)
    kept = forward(my_index, rx, owners, weights)
    result = backward(rx, g_zero, kept, weights)
    return call(
        unpack_kernel, jax.ShapeDtypeStruct((points, D), BF), [VMEM_SPEC] * 2, VMEM_SPEC, [], "unpack"
    )(dest_zero, exchange(result))


def solution(mesh):
    placed = (
        P(None, ("rep", "blk"), None),
        P(("rep", "blk"), None),
        P(None, "rep", None),
        P(),
        P(),
        P(),
        P(),
    )
    return jax.shard_map(
        per_device, mesh=mesh, in_specs=placed, out_specs=P(("rep", "blk"), None), check_vma=False
    )
```

```python
import jax
import jax.numpy as jnp
from jax import lax
from jax.experimental import pallas as pl
from jax.experimental.pallas import tpu as pltpu
from jax.sharding import PartitionSpec as P

D = 256
HEADS = 8
HD = D // HEADS
EPSILON = 1e-05
MASKED = -1e30
SCALE = HD ** (-0.5)
LOG2E = 1.4426950408889634
BF = jnp.bfloat16
F32 = jnp.float32


def mm(left, right):
    return lax.dot_general(left, right, (((1,), (0,)), ((), ())), preferred_element_type=F32)


def mm_t(left, right):
    return lax.dot_general(left, right, (((1,), (1,)), ((), ())), preferred_element_type=F32)


def iota(shape, axis):
    return lax.broadcasted_iota(jnp.int32, shape, axis)


def destination_row(owners, my_index, points):
    wide_rows = points // LANES
    own_row = jnp.concatenate(
        [owners[pl.ds(my_index * wide_rows + i, 1), :] for i in range(wide_rows)], axis=1
    ).astype(F32)
    rows, cols = iota((points, points), 0), iota((points, points), 1)
    wide = jnp.broadcast_to(own_row, (points, points))
    own_col = jnp.sum(jnp.where(rows == cols, wide, 0.0), axis=1, keepdims=True)
    same = jnp.where((own_col == wide) & (rows < cols), 1.0, 0.0)
    rank = jnp.sum(same, axis=0, keepdims=True)
    return own_row * 8.0 + rank


def one_hot(dest_row, slots):
    shape = (slots, dest_row.shape[1])
    return jnp.where(iota(shape, 0).astype(F32) == dest_row, 1.0, 0.0).astype(BF)


def key_bias(owners, my_index, slots):
    rows = owners.shape[0]
    per_source = rows * 8 // slots
    count = jnp.sum(jnp.where(owners == my_index, 1.0, 0.0), axis=1, keepdims=True)
    shape = (slots, rows)
    spread = jnp.where(iota(shape, 0) // 8 == iota(shape, 1) // per_source, 1.0, 0.0).astype(BF)
    slot_count = mm(spread, jnp.broadcast_to(count, (rows, D)).astype(BF))
    rank = (iota(slot_count.shape, 0) % 8).astype(F32)
    return jnp.where(rank < slot_count, 0.0, MASKED).astype(BF)


def unpack(dest_row, rows):
    hot = one_hot(dest_row, rows.shape[0])
    return lax.dot_general(hot, rows, (((0,), (0,)), ((), ())), preferred_element_type=F32).astype(BF)


def fetch(sem, pairs):
    copies = [pltpu.make_async_copy(a, b, sem.at[i]) for i, (a, b) in enumerate(pairs)]
    for copy in copies:
        copy.start()
    return copies


def route_kernel(
    index_ref, owners_hbm, saved_hbm, g_hbm, dest_ref, out_ref, owners_ref, x_ref, g_ref, sem
):
    slots, points = out_ref.shape[0], g_hbm.shape[0]
    owners_in, x_in, g_in = fetch(
        sem, [(owners_hbm.at[1], owners_ref), (saved_hbm.at[1], x_ref), (g_hbm, g_ref)]
    )
    owners_in.wait()
    dest = destination_row(owners_ref, index_ref[0], points)
    dest_ref[...] = jnp.broadcast_to(dest, dest_ref.shape)
    hot = one_hot(dest, slots)
    x_in.wait()
    out_ref[:, :D] = mm(hot, x_ref[...]).astype(BF)
    g_in.wait()
    out_ref[:, D:] = mm(hot, g_ref[...]).astype(BF)


def repack_kernel(dest_one_ref, dest_zero_ref, rows_ref, out_ref):
    gradient = unpack(dest_one_ref[0:1, :], rows_ref[:, :D])
    out_ref[...] = mm(one_hot(dest_zero_ref[0:1, :], out_ref.shape[0]), gradient).astype(BF)


def unpack_kernel(dest_ref, rows_ref, out_ref):
    out_ref[...] = unpack(dest_ref[0:1, :], rows_ref[...])


def normalized(values):
    centered = values - jnp.mean(values, axis=1, keepdims=True)
    inverse = lax.rsqrt(jnp.mean(centered * centered, axis=1, keepdims=True) + EPSILON)
    return centered * inverse, inverse


def norm_gradient(upstream, hat, inverse):
    mean_one = jnp.mean(upstream, axis=1, keepdims=True)
    mean_two = jnp.mean(upstream * hat, axis=1, keepdims=True)
    return inverse * (upstream - mean_one - hat * mean_two)


def head_lanes(shape, head):
    lane = iota(shape, 1)
    return (lane >= head * HD) & (lane < head * HD + HD)


def gelu_slope(pre):
    root, cubic = 0.7978845608028654, 0.044715
    square = pre * pre
    bend = jnp.tanh(pre * (root + (root * cubic) * square))
    rise = pre * (root + (3.0 * root * cubic) * square)
    return (0.5 + 0.5 * bend) * (1.0 + (1.0 - bend) * rise)


LANES = 128


def forward_part(x, weights, kept, work, wait, after_head, unroll):
    attend_ref, output_ref, up_ref, _ = weights
    qkv_ref, probs_ref, slope_ref, norm_ref, mixed_t_ref = kept
    bias_ref, query_ref, value_t_ref, even_ref, odd_ref, even_max_ref, odd_max_ref = work
    slots = x.shape[0]
    normed, _ = normalized(x)
    wait("attend")
    qkv = mm(normed.astype(BF), attend_ref[...]).astype(BF)
    qkv_ref[...] = qkv
    value_t_ref[...] = qkv[:, 2 * D :].T
    lane = iota((slots, D), 1)
    query_ref[...] = jnp.where(lane == 0, jnp.ones((slots, D), BF), qkv[:, :D])
    wait("owners")

    def score(keys, queries, scores_ref, max_ref):
        scores = mm_t(keys, queries)
        scores_ref[...] = scores
        max_ref[...] = jnp.broadcast_to(jnp.max(scores, axis=0, keepdims=True), (8, slots))

    def soften(head, scores_ref, max_ref):
        exponent = jnp.exp2((scores_ref[...] - max_ref[0:1, :]) * (SCALE * LOG2E))
        total = jnp.sum(exponent, axis=0, keepdims=True)
        probs = (exponent * (1.0 / total)).astype(BF)
        probs_ref[head] = probs
        at = pl.multiple_of(head * HD, HD)
        mixed_t_ref[pl.ds(at, HD), :] = mm(value_t_ref[pl.ds(at, HD), :], probs)

    bias = bias_ref[...]
    first_keys = jnp.where(
        head_lanes((slots, D), 0),
        qkv[:, D : 2 * D],
        jnp.where(lane == D - 1, bias, jnp.zeros_like(bias)),
    )
    first_queries = jnp.where(lane == D - 1, jnp.ones((slots, D), BF), qkv[:, :D])
    bias_ref[...] = jnp.where(lane == 0, bias, jnp.zeros_like(bias))
    score(first_keys, first_queries, even_ref, even_max_ref)

    def step(head, following, here, here_max, there, there_max):
        keys = jnp.where(head_lanes((slots, D), following), qkv_ref[:, D : 2 * D], bias_ref[...])
        score(keys, query_ref[...], there, there_max)
        soften(head, here, here_max)
        after_head(head)

    def pair(index, carry):
        step(2 * index, 2 * index + 1, even_ref, even_max_ref, odd_ref, odd_max_ref)
        following = jnp.minimum(2 * index + 2, HEADS - 1)
        step(2 * index + 1, following, odd_ref, odd_max_ref, even_ref, even_max_ref)
        return carry

    lax.fori_loop(0, HEADS // 2, pair, 0, unroll=unroll)
    attended = mixed_t_ref[...].astype(BF).T
    wait("output")
    mixed = mm(attended, output_ref[...]).astype(BF).astype(F32)
    hat, inverse = normalized(x + mixed)
    norm_ref[:, :D] = hat
    norm_ref[:, D:] = jnp.broadcast_to(inverse, (slots, LANES))
    rounded = hat.astype(BF)
    wait("up")
    for part in range(slope_ref.shape[0]):
        slope_ref[part] = gelu_slope(mm(rounded, up_ref[:, part * D : (part + 1) * D]))


def backward_part(x, g, weights, kept, work, wait, before_heads):
    attend_ref, output_ref, up_ref, down_ref = weights
    qkv_ref, probs_ref, slope_ref, norm_ref, mixed_t_ref = kept
    pre_grad_ref, up_grad_ref, up_grad_t_ref, query_t_ref, key_t_ref, delta_ref, grads_t_ref = work
    slots = g.shape[0]
    query_t_ref[...] = qkv_ref[:, :D].T
    key_t_ref[...] = qkv_ref[:, D : 2 * D].T
    wait("down")
    for part in range(slope_ref.shape[0]):
        rows = slice(part * D, (part + 1) * D)
        hidden_grad = mm_t(g, down_ref[rows, :])
        wait("slope", part)
        pre_grad_ref[:, rows] = (slope_ref[part] * hidden_grad).astype(BF)
    wait("up")
    normed_grad = mm_t(pre_grad_ref[...], up_ref[...])
    wait("norm")
    grad_mid = (
        g.astype(F32) + norm_gradient(normed_grad, norm_ref[:, :D], norm_ref[:, D : D + 1])
    ).astype(BF)
    wait("output")
    up_grad_ref[...] = mm_t(grad_mid, output_ref[...]).astype(BF)
    up_grad_t = mm_t(output_ref[...], grad_mid).astype(BF)
    up_grad_t_ref[...] = up_grad_t
    wait("mixed")
    weighted = mixed_t_ref[...] * up_grad_t.astype(F32)
    for head in range(HEADS):
        delta_ref[head : head + 1, :] = jnp.sum(
            weighted[head * HD : (head + 1) * HD], axis=0, keepdims=True
        )

    before_heads()

    def one_head(head, carry):
        values = jnp.where(
            head_lanes((slots, D), head), qkv_ref[:, 2 * D :], jnp.zeros((slots, D), BF)
        )
        at = pl.multiple_of(head * HD, HD)
        prob_grads = mm_t(values, up_grad_ref[...])
        probs = probs_ref[head]
        delta = delta_ref[pl.ds(head, 1), :]
        score_grads = (probs.astype(F32) * (prob_grads - delta)).astype(BF)
        value_grad = mm_t(up_grad_t_ref[pl.ds(at, HD), :], probs)
        key_grad = mm_t(query_t_ref[pl.ds(at, HD), :], score_grads)
        grads_t_ref[pl.ds(at, HD), :] = (mm(key_t_ref[pl.ds(at, HD), :], score_grads) * SCALE).astype(BF)
        grads_t_ref[pl.ds(pl.multiple_of(D + at, HD), HD), :] = (key_grad * SCALE).astype(BF)
        grads_t_ref[pl.ds(pl.multiple_of(2 * D + at, HD), HD), :] = value_grad.astype(BF)
        return carry

    lax.fori_loop(0, HEADS, one_head, 0, unroll=HEADS)
    wait("attend")
    normed_grads = mm(attend_ref[...], grads_t_ref[...]).T
    hat, inverse = normalized(x)
    branch = norm_gradient(normed_grads, hat, inverse).astype(BF)
    return (grad_mid.astype(F32) + branch.astype(F32)).astype(BF)


def whole_layer_kernel(
    index_ref, xg_ref, owners_hbm, saved_hbm, *rest
):
    weights_hbm, (out_ref, dest_ref), rest = rest[:4], rest[4:6], rest[6:]
    weights, kept, forward_work, backward_work = rest[:4], rest[4:9], rest[9:16], rest[16:23]
    owners_ref, next_x_ref, sem = rest[23:]
    my = index_ref[0]
    slots = out_ref.shape[0]
    copies = fetch(
        sem,
        [(weights_hbm[0].at[1], weights[0]), (owners_hbm, owners_ref)]
        + [(weights_hbm[i].at[1], weights[i]) for i in (1, 2, 3)]
        + [(saved_hbm.at[0], next_x_ref)],
    )
    order = dict(attend=0, owners=1, output=2, up=3, down=4)
    waited = set()

    def wait(name, part=0):
        if name in order and name not in waited:
            waited.add(name)
            copies[order[name]].wait()
            if name == "owners":
                forward_work[0][...] = key_bias(owners_ref[1], my, slots)

    forward_part(
        xg_ref[:, :D].astype(F32), weights, kept, forward_work, wait, lambda head: None, HEADS // 2
    )
    dest = destination_row(owners_ref.at[0], my, next_x_ref.shape[0])
    dest_ref[...] = jnp.broadcast_to(dest, dest_ref.shape)
    copies[5].wait()
    out_ref[:, D:] = mm(one_hot(dest, slots), next_x_ref[...]).astype(BF)
    out_ref[:, :D] = backward_part(
        xg_ref[:, :D].astype(F32), xg_ref[:, D:], weights, kept, backward_work, wait,
        lambda: None,
    )


def forward_kernel(index_ref, rx_ref, owners_hbm, *rest):
    weights_hbm, rest = rest[:3], rest[3:]
    qkv_ref, norm_ref, mixed_ref, probs_out, slope_out = rest[:5]
    weights, kept, work = rest[5:8], (qkv_ref,) + rest[8:10] + (norm_ref, mixed_ref), rest[10:17]
    owners_ref, in_sem, out_sem, probs_sem = rest[17:]
    my = index_ref[0]
    slots = rx_ref.shape[0]
    copies = fetch(
        in_sem,
        [(weights_hbm[0].at[0], weights[0]), (owners_hbm.at[0], owners_ref)]
        + [(weights_hbm[i].at[0], weights[i]) for i in (1, 2)],
    )
    order = dict(attend=0, owners=1, output=2, up=3)

    def wait(name, part=0):
        copies[order[name]].wait()
        if name == "owners":
            work[0][...] = key_bias(owners_ref[...], my, slots)

    def probs_copy(head):
        return pltpu.make_async_copy(kept[1].at[head], probs_out.at[head], probs_sem.at[head])

    forward_part(
        rx_ref[:, D:].astype(F32), tuple(weights) + (None,), kept, work, wait,
        lambda head: probs_copy(head).start(), 1,
    )
    leaving = fetch(
        out_sem, [(kept[2].at[i], slope_out.at[i]) for i in range(slope_out.shape[0])]
    )
    for head in range(HEADS):
        probs_copy(head).wait()
    for copy in leaving:
        copy.wait()


def backward_kernel(rx_ref, g_ref, qkv_ref, norm_ref, mixed_ref, probs_hbm, slope_hbm, *rest):
    weights_hbm, out_ref, rest = rest[:4], rest[4], rest[5:]
    weights, kept, work = rest[:4], (qkv_ref,) + rest[4:6] + (norm_ref, mixed_ref), rest[6:13]
    sem, probs_sem = rest[13:]
    parts = slope_hbm.shape[0]
    pairs = [(weights_hbm[3].at[0], weights[3])]
    pairs += [(slope_hbm.at[i], kept[2].at[i]) for i in range(parts)]
    pairs += [(weights_hbm[i].at[0], weights[i]) for i in (2, 1, 0)]
    copies = [pltpu.make_async_copy(x, y, sem.at[i]) for i, (x, y) in enumerate(pairs)]
    names = ["down"] + ["slope"] * parts + ["up", "output", "attend"]

    def probs_copy(head):
        return pltpu.make_async_copy(probs_hbm.at[head], kept[1].at[head], probs_sem.at[head])

    for copy in copies[: 1 + parts]:
        copy.start()

    def wait(name, part=0):
        if name in names:
            copies[names.index(name) + part].wait()
        if name == "down":
            for copy in copies[1 + parts :]:
                copy.start()
        if name == "slope":
            for head in (2 * part, 2 * part + 1):
                probs_copy(head).start()

    def before_heads():
        for head in range(HEADS):
            probs_copy(head).wait()

    out_ref[...] = backward_part(
        rx_ref[:, D:].astype(F32), g_ref[...], weights, kept, work, wait, before_heads
    )


SMEM_SPEC = pl.BlockSpec(memory_space=pltpu.SMEM)
VMEM_SPEC = pl.BlockSpec(memory_space=pltpu.VMEM)
HBM_SPEC = pl.BlockSpec(memory_space=pltpu.HBM)


def in_hbm(array):
    return pltpu.with_memory_space_constraint(array, pltpu.HBM)


def kept_shapes(slots, hidden):
    return [
        ((slots, 3 * D), BF),
        ((HEADS, slots, slots), BF),
        ((hidden // D, slots, D), F32),
        ((slots, D + LANES), F32),
        ((D, slots), F32),
    ]


def weight_scratch(weights):
    return [pltpu.VMEM(w.shape[1:], BF) for w in weights]


def forward_scratch(slots):
    return [
        pltpu.VMEM((slots, D), BF),
        pltpu.VMEM((slots, D), BF),
        pltpu.VMEM((D, slots), BF),
        pltpu.VMEM((slots, slots), F32),
        pltpu.VMEM((slots, slots), F32),
        pltpu.VMEM((8, slots), F32),
        pltpu.VMEM((8, slots), F32),
    ]


def backward_scratch(slots, hidden):
    return [
        pltpu.VMEM((slots, hidden), BF),
        pltpu.VMEM((slots, D), BF),
        pltpu.VMEM((D, slots), BF),
        pltpu.VMEM((D, slots), BF),
        pltpu.VMEM((D, slots), BF),
        pltpu.VMEM((HEADS, slots), F32),
        pltpu.VMEM((3 * D, slots), BF),
    ]


def call(kernel, outs, in_specs, out_specs, scratch, name):
    return pl.pallas_call(
        kernel,
        out_shape=outs,
        in_specs=in_specs,
        out_specs=out_specs,
        scratch_shapes=scratch,
        name=name,
        compiler_params=pltpu.CompilerParams(vmem_limit_bytes=40 << 20),
    )


def whole_layer(my_index, xg, owners, saved_inputs, weights):
    slots, hidden = xg.shape[0], weights[2].shape[2]
    points = saved_inputs.shape[1]
    return call(
        whole_layer_kernel,
        (jax.ShapeDtypeStruct((slots, 2 * D), BF), jax.ShapeDtypeStruct((8, points), F32)),
        [SMEM_SPEC, VMEM_SPEC] + [HBM_SPEC] * 6,
        (VMEM_SPEC, VMEM_SPEC),
        weight_scratch(weights)
        + [pltpu.VMEM(*k) for k in kept_shapes(slots, hidden)]
        + forward_scratch(slots)
        + backward_scratch(slots, hidden)
        + [
            pltpu.VMEM(owners.shape, jnp.int32),
            pltpu.VMEM((points, D), BF),
            pltpu.SemaphoreType.DMA((6,)),
        ],
        "whole_layer",
    )(my_index, xg, owners, saved_inputs, *weights)


def forward(my_index, rx, owners, weights):
    slots, hidden = rx.shape[0], weights[2].shape[2]
    shapes = kept_shapes(slots, hidden)
    return call(
        forward_kernel,
        tuple(jax.ShapeDtypeStruct(*shapes[i]) for i in (0, 3, 4))
        + tuple(pltpu.HBM(*k) for k in shapes[1:3]),
        [SMEM_SPEC, VMEM_SPEC] + [HBM_SPEC] * 4,
        (VMEM_SPEC,) * 3 + (HBM_SPEC,) * 2,
        weight_scratch(weights[:3])
        + [pltpu.VMEM(*k) for k in shapes[1:3]]
        + forward_scratch(slots)
        + [
            pltpu.VMEM(owners.shape[1:], jnp.int32),
            pltpu.SemaphoreType.DMA((4,)),
            pltpu.SemaphoreType.DMA((hidden // D,)),
            pltpu.SemaphoreType.DMA((HEADS,)),
        ],
        "layer_forward",
    )(my_index, rx, owners, *weights[:3])


def backward(rx, g, kept, weights):
    slots, hidden = g.shape[0], weights[2].shape[2]
    return call(
        backward_kernel,
        jax.ShapeDtypeStruct((slots, D), BF),
        [VMEM_SPEC] * 5 + [HBM_SPEC] * 6,
        VMEM_SPEC,
        weight_scratch(weights)
        + [pltpu.VMEM(*k) for k in kept_shapes(slots, hidden)[1:3]]
        + backward_scratch(slots, hidden)
        + [
            pltpu.SemaphoreType.DMA((4 + hidden // D,)),
            pltpu.SemaphoreType.DMA((HEADS,)),
        ],
        "layer_backward",
    )(rx, g, *kept[:3], *(in_hbm(k) for k in kept[3:]), *weights)


def per_device(saved_inputs, output_grads, owner_ids, attend, output, up, down):
    devices = lax.axis_size("blk")
    points = saved_inputs.shape[1]
    slots = devices * 8
    my_index = lax.axis_index("blk").astype(jnp.int32).reshape(1)
    owners = in_hbm(owner_ids.reshape(2, devices * points // LANES, LANES))
    saved_inputs, output_grads = in_hbm(saved_inputs), in_hbm(output_grads)
    weights = tuple(in_hbm(w) for w in (attend, output, up, down))

    def exchange(rows):
        width = rows.shape[1]
        moved = lax.all_to_all(
            rows.reshape(devices, 8, width), "blk", split_axis=0, concat_axis=0, tiled=True
        )
        return moved.reshape(slots, width)

    dest_one, packed = call(
        route_kernel,
        (jax.ShapeDtypeStruct((8, points), F32), jax.ShapeDtypeStruct((slots, 2 * D), BF)),
        [SMEM_SPEC] + [HBM_SPEC] * 3,
        (VMEM_SPEC, VMEM_SPEC),
        [
            pltpu.VMEM(owners.shape[1:], jnp.int32),
            pltpu.VMEM((points, D), BF),
            pltpu.VMEM((points, D), BF),
            pltpu.SemaphoreType.DMA((3,)),
        ],
        "route",
    )(my_index, owners, saved_inputs, output_grads)
    xg = exchange(packed)
    result, dest_zero = whole_layer(my_index, xg, owners, saved_inputs, weights)
    rx = exchange(result)
    packed = call(
        repack_kernel, jax.ShapeDtypeStruct((slots, D), BF), [VMEM_SPEC] * 3, VMEM_SPEC, [], "repack"
    )(dest_one, dest_zero, rx)
    g_zero = exchange(packed)
    kept = forward(my_index, rx, owners, weights)
    result = backward(rx, g_zero, kept, weights)
    return call(
        unpack_kernel, jax.ShapeDtypeStruct((points, D), BF), [VMEM_SPEC] * 2, VMEM_SPEC, [], "unpack"
    )(dest_zero, exchange(result))


def solution(mesh):
    placed = (
        P(None, ("rep", "blk"), None),
        P(("rep", "blk"), None),
        P(None, "rep", None),
        P(),
        P(),
        P(),
        P(),
    )
    return jax.shard_map(
        per_device, mesh=mesh, in_specs=placed, out_specs=P(("rep", "blk"), None), check_vma=False
    )
```

```python
import jax
import jax.numpy as jnp
from jax import lax
from jax.experimental import pallas as pl
from jax.experimental.pallas import tpu as pltpu
from jax.sharding import PartitionSpec as P

D = 256
HEADS = 8
HD = D // HEADS
EPSILON = 1e-05
MASKED = -1e30
SCALE = HD ** (-0.5)
LOG2E = 1.4426950408889634
BF = jnp.bfloat16
F32 = jnp.float32


def mm(left, right):
    return lax.dot_general(left, right, (((1,), (0,)), ((), ())), preferred_element_type=F32)


def mm_t(left, right):
    return lax.dot_general(left, right, (((1,), (1,)), ((), ())), preferred_element_type=F32)


def iota(shape, axis):
    return lax.broadcasted_iota(jnp.int32, shape, axis)


def destination_row(owners, my_index, points):
    wide_rows = points // LANES
    own_row = jnp.concatenate(
        [owners[pl.ds(my_index * wide_rows + i, 1), :] for i in range(wide_rows)], axis=1
    ).astype(F32)
    rows, cols = iota((points, points), 0), iota((points, points), 1)
    wide = jnp.broadcast_to(own_row, (points, points))
    own_col = jnp.sum(jnp.where(rows == cols, wide, 0.0), axis=1, keepdims=True)
    same = jnp.where((own_col == wide) & (rows < cols), 1.0, 0.0)
    rank = jnp.sum(same, axis=0, keepdims=True)
    return own_row * 8.0 + rank


def one_hot(dest_row, slots):
    shape = (slots, dest_row.shape[1])
    return jnp.where(iota(shape, 0).astype(F32) == dest_row, 1.0, 0.0).astype(BF)


def key_bias(owners, my_index, slots):
    rows = owners.shape[0]
    per_source = rows * 8 // slots
    count = jnp.sum(jnp.where(owners == my_index, 1.0, 0.0), axis=1, keepdims=True)
    shape = (slots, rows)
    spread = jnp.where(iota(shape, 0) // 8 == iota(shape, 1) // per_source, 1.0, 0.0).astype(BF)
    slot_count = mm(spread, jnp.broadcast_to(count, (rows, D)).astype(BF))
    rank = (iota(slot_count.shape, 0) % 8).astype(F32)
    return jnp.where(rank < slot_count, 0.0, MASKED).astype(BF)


def unpack(dest_row, rows):
    hot = one_hot(dest_row, rows.shape[0])
    return lax.dot_general(hot, rows, (((0,), (0,)), ((), ())), preferred_element_type=F32).astype(BF)


def fetch(sem, pairs):
    copies = [pltpu.make_async_copy(a, b, sem.at[i]) for i, (a, b) in enumerate(pairs)]
    for copy in copies:
        copy.start()
    return copies


def route_kernel(
    index_ref, owners_hbm, saved_hbm, g_hbm, dest_ref, out_ref, owners_ref, x_ref, g_ref, sem
):
    slots, points = out_ref.shape[0], g_hbm.shape[0]
    owners_in, x_in, g_in = fetch(
        sem, [(owners_hbm.at[1], owners_ref), (saved_hbm.at[1], x_ref), (g_hbm, g_ref)]
    )
    owners_in.wait()
    dest = destination_row(owners_ref, index_ref[0], points)
    dest_ref[...] = jnp.broadcast_to(dest, dest_ref.shape)
    hot = one_hot(dest, slots)
    x_in.wait()
    out_ref[:, :D] = mm(hot, x_ref[...]).astype(BF)
    g_in.wait()
    out_ref[:, D:] = mm(hot, g_ref[...]).astype(BF)


def repack_kernel(dest_one_ref, dest_zero_ref, rows_ref, out_ref):
    gradient = unpack(dest_one_ref[0:1, :], rows_ref[:, :D])
    out_ref[...] = mm(one_hot(dest_zero_ref[0:1, :], out_ref.shape[0]), gradient).astype(BF)


def unpack_kernel(dest_ref, rows_ref, out_ref):
    out_ref[...] = unpack(dest_ref[0:1, :], rows_ref[...])


def normalized(values):
    centered = values - jnp.mean(values, axis=1, keepdims=True)
    inverse = lax.rsqrt(jnp.mean(centered * centered, axis=1, keepdims=True) + EPSILON)
    return centered * inverse, inverse


def norm_gradient(upstream, hat, inverse):
    mean_one = jnp.mean(upstream, axis=1, keepdims=True)
    mean_two = jnp.mean(upstream * hat, axis=1, keepdims=True)
    return inverse * (upstream - mean_one - hat * mean_two)


def head_lanes(shape, head):
    lane = iota(shape, 1)
    return (lane >= head * HD) & (lane < head * HD + HD)


def gelu_slope(pre):
    root, cubic = 0.7978845608028654, 0.044715
    square = pre * pre
    bend = jnp.tanh(pre * (root + (root * cubic) * square))
    rise = pre * (root + (3.0 * root * cubic) * square)
    return (0.5 + 0.5 * bend) * (1.0 + (1.0 - bend) * rise)


LANES = 128


def forward_part(x, weights, kept, work, wait, after_head, unroll):
    attend_ref, output_ref = weights[:2]
    value_ref, query_t_ref, key_t_ref, probs_ref, norm_ref, mixed_t_ref = kept
    bias_ref, query_ref, key_ref, value_t_ref, even_ref, odd_ref, even_max_ref, odd_max_ref = work
    slots = x.shape[0]
    normed, _ = normalized(x)
    wait("attend")
    qkv = mm(normed.astype(BF), attend_ref[...]).astype(BF)
    key_ref[...] = qkv[:, D : 2 * D]
    value_ref[...] = qkv[:, 2 * D :]
    value_t_ref[...] = qkv[:, 2 * D :].T
    query_t_ref[...] = qkv[:, :D].T
    key_t_ref[...] = qkv[:, D : 2 * D].T
    lane = iota((slots, D), 1)
    query_ref[...] = jnp.where(lane == 0, jnp.ones((slots, D), BF), qkv[:, :D])
    wait("owners")

    def score(keys, queries, scores_ref, max_ref):
        scores = mm_t(keys, queries)
        scores_ref[...] = scores
        max_ref[...] = jnp.broadcast_to(jnp.max(scores, axis=0, keepdims=True), (8, slots))

    def soften(head, scores_ref, max_ref):
        exponent = jnp.exp2((scores_ref[...] - max_ref[0:1, :]) * (SCALE * LOG2E))
        total = jnp.sum(exponent, axis=0, keepdims=True)
        probs = (exponent * (1.0 / total)).astype(BF)
        probs_ref[head] = probs
        at = pl.multiple_of(head * HD, HD)
        mixed_t_ref[pl.ds(at, HD), :] = mm(value_t_ref[pl.ds(at, HD), :], probs)

    bias = bias_ref[...]
    first_keys = jnp.where(
        head_lanes((slots, D), 0),
        qkv[:, D : 2 * D],
        jnp.where(lane == D - 1, bias, jnp.zeros_like(bias)),
    )
    first_queries = jnp.where(lane == D - 1, jnp.ones((slots, D), BF), qkv[:, :D])
    bias_ref[...] = jnp.where(lane == 0, bias, jnp.zeros_like(bias))
    score(first_keys, first_queries, even_ref, even_max_ref)

    def step(head, following, here, here_max, there, there_max):
        keys = jnp.where(head_lanes((slots, D), following), key_ref[...], bias_ref[...])
        score(keys, query_ref[...], there, there_max)
        soften(head, here, here_max)
        after_head(head)

    def pair(index, carry):
        step(2 * index, 2 * index + 1, even_ref, even_max_ref, odd_ref, odd_max_ref)
        following = jnp.minimum(2 * index + 2, HEADS - 1)
        step(2 * index + 1, following, odd_ref, odd_max_ref, even_ref, even_max_ref)
        return carry

    lax.fori_loop(0, HEADS // 2, pair, 0, unroll=unroll)
    attended = mixed_t_ref[...].astype(BF).T
    wait("output")
    mixed = mm(attended, output_ref[...]).astype(BF).astype(F32)
    hat, inverse = normalized(x + mixed)
    norm_ref[:, :D] = hat
    norm_ref[:, D:] = jnp.broadcast_to(inverse, (slots, LANES))


def backward_part(x, g, weights, kept, work, wait, before_heads):
    attend_ref, output_ref, up_ref, down_ref = weights
    value_ref, query_t_ref, key_t_ref, probs_ref, norm_ref, mixed_t_ref = kept
    pre_grad_ref, up_grad_ref, up_grad_t_ref, delta_ref, grads_t_ref = work
    slots = g.shape[0]
    rounded = norm_ref[:, :D].astype(BF)
    wait("up")
    wait("down")
    for part in range(up_ref.shape[1] // D):
        cols = slice(part * D, (part + 1) * D)
        slope = gelu_slope(mm(rounded, up_ref[:, cols]))
        pre_grad_ref[:, cols] = (slope * mm_t(g, down_ref[cols, :])).astype(BF)
    normed_grad = mm_t(pre_grad_ref[...], up_ref[...])
    grad_mid = (
        g.astype(F32) + norm_gradient(normed_grad, norm_ref[:, :D], norm_ref[:, D : D + 1])
    ).astype(BF)
    wait("output")
    up_grad_ref[...] = mm_t(grad_mid, output_ref[...]).astype(BF)
    up_grad_t = mm_t(output_ref[...], grad_mid).astype(BF)
    up_grad_t_ref[...] = up_grad_t
    weighted = mixed_t_ref[...] * up_grad_t.astype(F32)
    for head in range(HEADS):
        delta_ref[head : head + 1, :] = jnp.sum(
            weighted[head * HD : (head + 1) * HD], axis=0, keepdims=True
        )

    def one_head(head, carry):
        values = jnp.where(
            head_lanes((slots, D), head), value_ref[...], jnp.zeros((slots, D), BF)
        )
        at = pl.multiple_of(head * HD, HD)
        prob_grads = mm_t(values, up_grad_ref[...])
        probs = probs_ref[head]
        delta = delta_ref[pl.ds(head, 1), :]
        score_grads = (probs.astype(F32) * (prob_grads - delta)).astype(BF)
        value_grad = mm_t(up_grad_t_ref[pl.ds(at, HD), :], probs)
        key_grad = mm_t(query_t_ref[pl.ds(at, HD), :], score_grads)
        grads_t_ref[pl.ds(at, HD), :] = (mm(key_t_ref[pl.ds(at, HD), :], score_grads) * SCALE).astype(BF)
        grads_t_ref[pl.ds(pl.multiple_of(D + at, HD), HD), :] = (key_grad * SCALE).astype(BF)
        grads_t_ref[pl.ds(pl.multiple_of(2 * D + at, HD), HD), :] = value_grad.astype(BF)
        return carry

    before_heads()
    lax.fori_loop(0, HEADS, one_head, 0, unroll=HEADS)
    wait("attend")
    normed_grads = mm(attend_ref[...], grads_t_ref[...]).T
    hat, inverse = normalized(x)
    branch = norm_gradient(normed_grads, hat, inverse).astype(BF)
    return (grad_mid.astype(F32) + branch.astype(F32)).astype(BF)


def whole_layer_kernel(
    index_ref, xg_ref, owners_hbm, saved_hbm, *rest
):
    weights_hbm, (out_ref, dest_ref), rest = rest[:4], rest[4:6], rest[6:]
    weights, kept, forward_work, backward_work = rest[:4], rest[4:10], rest[10:18], rest[18:23]
    owners_ref, next_x_ref, sem = rest[23:]
    my = index_ref[0]
    slots = out_ref.shape[0]
    copies = fetch(
        sem,
        [(weights_hbm[0].at[1], weights[0]), (owners_hbm, owners_ref)]
        + [(weights_hbm[i].at[1], weights[i]) for i in (1, 2, 3)]
        + [(saved_hbm.at[0], next_x_ref)],
    )
    order = dict(attend=0, owners=1, output=2, up=3, down=4)
    waited = set()

    def wait(name):
        if name in order and name not in waited:
            waited.add(name)
            copies[order[name]].wait()
            if name == "owners":
                forward_work[0][...] = key_bias(owners_ref[1], my, slots)

    forward_part(
        xg_ref[:, :D].astype(F32), weights, kept, forward_work, wait, lambda head: None,
        HEADS // 2,
    )
    dest = destination_row(owners_ref.at[0], my, next_x_ref.shape[0])
    dest_ref[...] = jnp.broadcast_to(dest, dest_ref.shape)
    copies[5].wait()
    out_ref[:, D:] = mm(one_hot(dest, slots), next_x_ref[...]).astype(BF)
    out_ref[:, :D] = backward_part(
        xg_ref[:, :D].astype(F32), xg_ref[:, D:], weights, kept, backward_work, wait,
        lambda: None,
    )


def forward_kernel(index_ref, rx_ref, owners_hbm, *rest):
    attend_hbm, output_hbm, up_hbm = rest[:3]
    value_ref, query_t_ref, key_t_ref, norm_ref, mixed_t_ref, up_ref, probs_out = rest[3:10]
    attend_ref, output_ref, probs_ref = rest[10:13]
    work = rest[13:21]
    owners_ref, in_sem, probs_sem = rest[21:]
    my = index_ref[0]
    slots = rx_ref.shape[0]
    copies = fetch(
        in_sem,
        [
            (attend_hbm.at[0], attend_ref),
            (owners_hbm.at[0], owners_ref),
            (output_hbm.at[0], output_ref),
            (up_hbm.at[0], up_ref),
        ],
    )
    order = dict(attend=0, owners=1, output=2)

    def wait(name):
        copies[order[name]].wait()
        if name == "owners":
            work[0][...] = key_bias(owners_ref[...], my, slots)

    def probs_copy(head):
        return pltpu.make_async_copy(probs_ref.at[head], probs_out.at[head], probs_sem.at[head])

    forward_part(
        rx_ref[:, D:].astype(F32),
        (attend_ref, output_ref),
        (value_ref, query_t_ref, key_t_ref, probs_ref, norm_ref, mixed_t_ref),
        work, wait, lambda head: probs_copy(head).start(), 1,
    )
    copies[3].wait()
    for head in range(HEADS):
        probs_copy(head).wait()


def backward_kernel(
    rx_ref, g_ref, value_ref, query_t_ref, key_t_ref, norm_ref, mixed_t_ref, up_ref, probs_hbm,
    attend_hbm, output_hbm, down_hbm,
    out_ref,
    attend_ref, output_ref, down_ref, probs_ref, *rest,
):
    work, (sem, probs_sem) = rest[:5], rest[5:]
    copies = fetch(
        sem,
        [
            (down_hbm.at[0], down_ref),
            (output_hbm.at[0], output_ref),
            (attend_hbm.at[0], attend_ref),
        ],
    )
    order = dict(down=0, output=1, attend=2)

    def probs_copy(head):
        return pltpu.make_async_copy(probs_hbm.at[head], probs_ref.at[head], probs_sem.at[head])

    def wait(name):
        if name in order:
            copies[order[name]].wait()
        if name == "down":
            for head in range(HEADS):
                probs_copy(head).start()

    def before_heads():
        for head in range(HEADS):
            probs_copy(head).wait()

    out_ref[...] = backward_part(
        rx_ref[:, D:].astype(F32), g_ref[...], (attend_ref, output_ref, up_ref, down_ref),
        (value_ref, query_t_ref, key_t_ref, probs_ref, norm_ref, mixed_t_ref),
        work, wait, before_heads,
    )


SMEM_SPEC = pl.BlockSpec(memory_space=pltpu.SMEM)
VMEM_SPEC = pl.BlockSpec(memory_space=pltpu.VMEM)
HBM_SPEC = pl.BlockSpec(memory_space=pltpu.HBM)


def in_hbm(array):
    return pltpu.with_memory_space_constraint(array, pltpu.HBM)


def kept_shapes(slots):
    return [
        ((slots, D), BF),
        ((D, slots), BF),
        ((D, slots), BF),
        ((HEADS, slots, slots), BF),
        ((slots, D + LANES), F32),
        ((D, slots), F32),
    ]


def weight_scratch(weights):
    return [pltpu.VMEM(w.shape[1:], BF) for w in weights]


def forward_scratch(slots):
    return [
        pltpu.VMEM((slots, D), BF),
        pltpu.VMEM((slots, D), BF),
        pltpu.VMEM((slots, D), BF),
        pltpu.VMEM((D, slots), BF),
        pltpu.VMEM((slots, slots), F32),
        pltpu.VMEM((slots, slots), F32),
        pltpu.VMEM((8, slots), F32),
        pltpu.VMEM((8, slots), F32),
    ]


def backward_scratch(slots, hidden):
    return [
        pltpu.VMEM((slots, hidden), BF),
        pltpu.VMEM((slots, D), BF),
        pltpu.VMEM((D, slots), BF),
        pltpu.VMEM((HEADS, slots), F32),
        pltpu.VMEM((3 * D, slots), BF),
    ]


def call(kernel, outs, in_specs, out_specs, scratch, name):
    return pl.pallas_call(
        kernel,
        out_shape=outs,
        in_specs=in_specs,
        out_specs=out_specs,
        scratch_shapes=scratch,
        name=name,
        compiler_params=pltpu.CompilerParams(vmem_limit_bytes=40 << 20),
    )


def whole_layer(my_index, xg, owners, saved_inputs, weights):
    slots, hidden = xg.shape[0], weights[2].shape[2]
    points = saved_inputs.shape[1]
    return call(
        whole_layer_kernel,
        (jax.ShapeDtypeStruct((slots, 2 * D), BF), jax.ShapeDtypeStruct((8, points), F32)),
        [SMEM_SPEC, VMEM_SPEC] + [HBM_SPEC] * 6,
        (VMEM_SPEC, VMEM_SPEC),
        weight_scratch(weights)
        + [pltpu.VMEM(*k) for k in kept_shapes(slots)]
        + forward_scratch(slots)
        + backward_scratch(slots, hidden)
        + [
            pltpu.VMEM(owners.shape, jnp.int32),
            pltpu.VMEM((points, D), BF),
            pltpu.SemaphoreType.DMA((6,)),
        ],
        "whole_layer",
    )(my_index, xg, owners, saved_inputs, *weights)


def forward(my_index, rx, owners, weights):
    slots = rx.shape[0]
    shapes = kept_shapes(slots)
    attend, output, up = weights[:3]
    return call(
        forward_kernel,
        tuple(jax.ShapeDtypeStruct(*shapes[i]) for i in (0, 1, 2, 4, 5))
        + (jax.ShapeDtypeStruct(up.shape[1:], BF), pltpu.HBM(*shapes[3])),
        [SMEM_SPEC, VMEM_SPEC] + [HBM_SPEC] * 4,
        (VMEM_SPEC,) * 6 + (HBM_SPEC,),
        weight_scratch((attend, output))
        + [pltpu.VMEM(*shapes[3])]
        + forward_scratch(slots)
        + [
            pltpu.VMEM(owners.shape[1:], jnp.int32),
            pltpu.SemaphoreType.DMA((4,)),
            pltpu.SemaphoreType.DMA((HEADS,)),
        ],
        "layer_forward",
    )(my_index, rx, owners, attend, output, up)


def backward(rx, g, kept, weights):
    slots = g.shape[0]
    attend, output, up, down = weights
    return call(
        backward_kernel,
        jax.ShapeDtypeStruct((slots, D), BF),
        [VMEM_SPEC] * 8 + [HBM_SPEC] * 4,
        VMEM_SPEC,
        weight_scratch((attend, output, down))
        + [pltpu.VMEM(*kept_shapes(slots)[3])]
        + backward_scratch(slots, up.shape[2])
        + [pltpu.SemaphoreType.DMA((3,)), pltpu.SemaphoreType.DMA((HEADS,))],
        "layer_backward",
    )(rx, g, *kept[:6], in_hbm(kept[6]), attend, output, down)


def per_device(saved_inputs, output_grads, owner_ids, attend, output, up, down):
    devices = lax.axis_size("blk")
    points = saved_inputs.shape[1]
    slots = devices * 8
    my_index = lax.axis_index("blk").astype(jnp.int32).reshape(1)
    owners = in_hbm(owner_ids.reshape(2, devices * points // LANES, LANES))
    saved_inputs, output_grads = in_hbm(saved_inputs), in_hbm(output_grads)
    weights = tuple(in_hbm(w) for w in (attend, output, up, down))

    def exchange(rows):
        width = rows.shape[1]
        moved = lax.all_to_all(
            rows.reshape(devices, 8, width), "blk", split_axis=0, concat_axis=0, tiled=True
        )
        return moved.reshape(slots, width)

    dest_one, packed = call(
        route_kernel,
        (jax.ShapeDtypeStruct((8, points), F32), jax.ShapeDtypeStruct((slots, 2 * D), BF)),
        [SMEM_SPEC] + [HBM_SPEC] * 3,
        (VMEM_SPEC, VMEM_SPEC),
        [
            pltpu.VMEM(owners.shape[1:], jnp.int32),
            pltpu.VMEM((points, D), BF),
            pltpu.VMEM((points, D), BF),
            pltpu.SemaphoreType.DMA((3,)),
        ],
        "route",
    )(my_index, owners, saved_inputs, output_grads)
    xg = exchange(packed)
    result, dest_zero = whole_layer(my_index, xg, owners, saved_inputs, weights)
    rx = exchange(result)
    packed = call(
        repack_kernel, jax.ShapeDtypeStruct((slots, D), BF), [VMEM_SPEC] * 3, VMEM_SPEC, [], "repack"
    )(dest_one, dest_zero, rx)
    g_zero = exchange(packed)
    kept = forward(my_index, rx, owners, weights)
    result = backward(rx, g_zero, kept, weights)
    return call(
        unpack_kernel, jax.ShapeDtypeStruct((points, D), BF), [VMEM_SPEC] * 2, VMEM_SPEC, [], "unpack"
    )(dest_zero, exchange(result))


def solution(mesh):
    placed = (
        P(None, ("rep", "blk"), None),
        P(("rep", "blk"), None),
        P(None, "rep", None),
        P(),
        P(),
        P(),
        P(),
    )
    return jax.shard_map(
        per_device, mesh=mesh, in_specs=placed, out_specs=P(("rep", "blk"), None), check_vma=False
    )
```

```python
import jax
import jax.numpy as jnp
from jax import lax
from jax.experimental import pallas as pl
from jax.experimental.pallas import tpu as pltpu
from jax.sharding import PartitionSpec as P

D = 256
HEADS = 8
HD = D // HEADS
EPSILON = 1e-05
MASKED = -1e30
SCALE = HD ** (-0.5)
LOG2E = 1.4426950408889634
BF = jnp.bfloat16
F32 = jnp.float32


def mm(left, right):
    return lax.dot_general(left, right, (((1,), (0,)), ((), ())), preferred_element_type=F32)


def mm_t(left, right):
    return lax.dot_general(left, right, (((1,), (1,)), ((), ())), preferred_element_type=F32)


def iota(shape, axis):
    return lax.broadcasted_iota(jnp.int32, shape, axis)


def destination_row(owners, my_index, points):
    wide_rows = points // LANES
    own_row = jnp.concatenate(
        [owners[pl.ds(my_index * wide_rows + i, 1), :] for i in range(wide_rows)], axis=1
    ).astype(F32)
    rows, cols = iota((points, points), 0), iota((points, points), 1)
    wide = jnp.broadcast_to(own_row, (points, points))
    own_col = jnp.sum(jnp.where(rows == cols, wide, 0.0), axis=1, keepdims=True)
    same = jnp.where((own_col == wide) & (rows < cols), 1.0, 0.0)
    rank = jnp.sum(same, axis=0, keepdims=True)
    return own_row * 8.0 + rank


def one_hot(dest_row, slots):
    shape = (slots, dest_row.shape[1])
    return jnp.where(iota(shape, 0).astype(F32) == dest_row, 1.0, 0.0).astype(BF)


def key_bias(owners, my_index, slots):
    rows = owners.shape[0]
    per_source = rows * 8 // slots
    count = jnp.sum(jnp.where(owners == my_index, 1.0, 0.0), axis=1, keepdims=True)
    shape = (slots, rows)
    spread = jnp.where(iota(shape, 0) // 8 == iota(shape, 1) // per_source, 1.0, 0.0).astype(BF)
    slot_count = mm(spread, jnp.broadcast_to(count, (rows, D)).astype(BF))
    rank = (iota(slot_count.shape, 0) % 8).astype(F32)
    return jnp.where(rank < slot_count, 0.0, MASKED).astype(BF)


def unpack(dest_row, rows):
    hot = one_hot(dest_row, rows.shape[0])
    return lax.dot_general(hot, rows, (((0,), (0,)), ((), ())), preferred_element_type=F32).astype(BF)


def fetch(sem, pairs):
    copies = [pltpu.make_async_copy(a, b, sem.at[i]) for i, (a, b) in enumerate(pairs)]
    for copy in copies:
        copy.start()
    return copies


def route_kernel(
    index_ref, owners_hbm, saved_hbm, g_hbm, dest_ref, out_ref, owners_ref, x_ref, g_ref, sem
):
    slots, points = out_ref.shape[0], g_hbm.shape[0]
    owners_in, x_in, g_in = fetch(
        sem, [(owners_hbm.at[1], owners_ref), (saved_hbm.at[1], x_ref), (g_hbm, g_ref)]
    )
    owners_in.wait()
    dest = destination_row(owners_ref, index_ref[0], points)
    dest_ref[...] = jnp.broadcast_to(dest, dest_ref.shape)
    hot = one_hot(dest, slots)
    x_in.wait()
    out_ref[:, :D] = mm(hot, x_ref[...]).astype(BF)
    g_in.wait()
    out_ref[:, D:] = mm(hot, g_ref[...]).astype(BF)


def repack_kernel(dest_one_ref, dest_zero_ref, rows_ref, out_ref):
    gradient = unpack(dest_one_ref[0:1, :], rows_ref[:, :D])
    out_ref[...] = mm(one_hot(dest_zero_ref[0:1, :], out_ref.shape[0]), gradient).astype(BF)


def unpack_kernel(dest_ref, rows_ref, out_ref):
    out_ref[...] = unpack(dest_ref[0:1, :], rows_ref[...])


def normalized(values):
    centered = values - jnp.mean(values, axis=1, keepdims=True)
    inverse = lax.rsqrt(jnp.mean(centered * centered, axis=1, keepdims=True) + EPSILON)
    return centered * inverse, inverse


def norm_gradient(upstream, hat, inverse):
    mean_one = jnp.mean(upstream, axis=1, keepdims=True)
    mean_two = jnp.mean(upstream * hat, axis=1, keepdims=True)
    return inverse * (upstream - mean_one - hat * mean_two)


def head_lanes(shape, head):
    lane = iota(shape, 1)
    return (lane >= head * HD) & (lane < head * HD + HD)


def gelu_slope(pre):
    root, cubic = 0.7978845608028654, 0.044715
    square = pre * pre
    bend = jnp.tanh(pre * (root + (root * cubic) * square))
    rise = pre * (root + (3.0 * root * cubic) * square)
    return (0.5 + 0.5 * bend) * (1.0 + (1.0 - bend) * rise)


LANES = 128


def forward_part(x, weights, kept, work, wait, after_head, unroll):
    attend_ref, output_ref = weights[:2]
    value_ref, query_t_ref, key_t_ref, probs_ref, norm_ref, mixed_t_ref = kept
    bias_ref, query_ref, key_ref, value_t_ref, even_ref, odd_ref, even_max_ref, odd_max_ref = work
    slots = x.shape[0]
    normed, _ = normalized(x)
    wait("attend")
    qkv = mm(normed.astype(BF), attend_ref[...]).astype(BF)
    key_ref[...] = qkv[:, D : 2 * D]
    value_ref[...] = qkv[:, 2 * D :]
    value_t_ref[...] = qkv[:, 2 * D :].T
    query_t_ref[...] = qkv[:, :D].T
    key_t_ref[...] = qkv[:, D : 2 * D].T
    lane = iota((slots, D), 1)
    query_ref[...] = jnp.where(lane == 0, jnp.ones((slots, D), BF), qkv[:, :D])
    wait("owners")

    def score(keys, queries, scores_ref, max_ref):
        scores = mm_t(keys, queries)
        scores_ref[...] = scores
        max_ref[...] = jnp.broadcast_to(jnp.max(scores, axis=0, keepdims=True), (8, slots))

    def soften(head, scores_ref, max_ref):
        exponent = jnp.exp2((scores_ref[...] - max_ref[0:1, :]) * (SCALE * LOG2E))
        total = jnp.sum(exponent, axis=0, keepdims=True)
        probs = (exponent * (1.0 / total)).astype(BF)
        probs_ref[head] = probs
        at = pl.multiple_of(head * HD, HD)
        mixed_t_ref[pl.ds(at, HD), :] = mm(value_t_ref[pl.ds(at, HD), :], probs)

    bias = bias_ref[...]
    first_keys = jnp.where(
        head_lanes((slots, D), 0),
        qkv[:, D : 2 * D],
        jnp.where(lane == D - 1, bias, jnp.zeros_like(bias)),
    )
    first_queries = jnp.where(lane == D - 1, jnp.ones((slots, D), BF), qkv[:, :D])
    bias_ref[...] = jnp.where(lane == 0, bias, jnp.zeros_like(bias))
    score(first_keys, first_queries, even_ref, even_max_ref)

    def step(head, following, here, here_max, there, there_max):
        keys = jnp.where(head_lanes((slots, D), following), key_ref[...], bias_ref[...])
        score(keys, query_ref[...], there, there_max)
        soften(head, here, here_max)
        after_head(head)

    def pair(index, carry):
        step(2 * index, 2 * index + 1, even_ref, even_max_ref, odd_ref, odd_max_ref)
        following = jnp.minimum(2 * index + 2, HEADS - 1)
        step(2 * index + 1, following, odd_ref, odd_max_ref, even_ref, even_max_ref)
        return carry

    lax.fori_loop(0, HEADS // 2, pair, 0, unroll=unroll)
    attended = mixed_t_ref[...].astype(BF).T
    wait("output")
    mixed = mm(attended, output_ref[...]).astype(BF).astype(F32)
    hat, inverse = normalized(x + mixed)
    norm_ref[:, :D] = hat
    norm_ref[:, D:] = jnp.broadcast_to(inverse, (slots, LANES))


def backward_part(x_ref, g, weights, kept, work, wait, before_heads):
    attend_ref, output_ref, up_ref, down_ref = weights
    value_ref, query_t_ref, key_t_ref, probs_ref, norm_ref, mixed_t_ref = kept
    pre_grad_ref, up_grad_ref, up_grad_t_ref, delta_ref, grads_t_ref = work
    slots = g.shape[0]
    rounded = norm_ref[:, :D].astype(BF)
    wait("up")
    blocks = [slice(at, at + D) for at in range(0, up_ref.shape[1], D)]
    slopes = [gelu_slope(mm(rounded, up_ref[:, block])) for block in blocks]
    wait("down")
    for block, slope in zip(blocks, slopes):
        pre_grad_ref[:, block] = (slope * mm_t(g, down_ref[block, :])).astype(BF)
    normed_grad = mm_t(pre_grad_ref[...], up_ref[...])
    grad_mid = (
        g.astype(F32) + norm_gradient(normed_grad, norm_ref[:, :D], norm_ref[:, D : D + 1])
    ).astype(BF)
    wait("output")
    up_grad_ref[...] = mm_t(grad_mid, output_ref[...]).astype(BF)
    up_grad_t = mm_t(output_ref[...], grad_mid).astype(BF)
    up_grad_t_ref[...] = up_grad_t
    weighted = mixed_t_ref[...] * up_grad_t.astype(F32)
    for head in range(HEADS):
        delta_ref[head : head + 1, :] = jnp.sum(
            weighted[head * HD : (head + 1) * HD], axis=0, keepdims=True
        )

    def one_head(head, carry):
        values = jnp.where(
            head_lanes((slots, D), head), value_ref[...], jnp.zeros((slots, D), BF)
        )
        at = pl.multiple_of(head * HD, HD)
        prob_grads = mm_t(values, up_grad_ref[...])
        probs = probs_ref[head]
        delta = delta_ref[pl.ds(head, 1), :]
        score_grads = (probs.astype(F32) * (prob_grads - delta)).astype(BF)
        value_grad = mm_t(up_grad_t_ref[pl.ds(at, HD), :], probs)
        key_grad = mm_t(query_t_ref[pl.ds(at, HD), :], score_grads)
        grads_t_ref[pl.ds(at, HD), :] = (mm(key_t_ref[pl.ds(at, HD), :], score_grads) * SCALE).astype(BF)
        grads_t_ref[pl.ds(pl.multiple_of(D + at, HD), HD), :] = (key_grad * SCALE).astype(BF)
        grads_t_ref[pl.ds(pl.multiple_of(2 * D + at, HD), HD), :] = value_grad.astype(BF)
        return carry

    before_heads()
    lax.fori_loop(0, HEADS, one_head, 0, unroll=HEADS)
    wait("attend")
    normed_grads = mm(attend_ref[...], grads_t_ref[...]).T
    wait("x")
    hat, inverse = normalized(x_ref[...].astype(F32))
    branch = norm_gradient(normed_grads, hat, inverse).astype(BF)
    return (grad_mid.astype(F32) + branch.astype(F32)).astype(BF)


def prefetch_kernel(owners_hbm, saved_hbm, *rest):
    weights_hbm, (owners_ref, next_x_ref), weights = rest[1:5], rest[5:7], rest[7:11]
    copies = fetch(
        rest[11],
        [(owners_hbm, owners_ref), (saved_hbm.at[0], next_x_ref)]
        + [(hbm.at[1], ref) for hbm, ref in zip(weights_hbm, weights)],
    )
    for copy in copies:
        copy.wait()


def whole_layer_kernel(index_ref, xg_ref, owners_ref, next_x_ref, *rest):
    weights, (out_ref, dest_ref), rest = rest[:4], rest[4:6], rest[6:]
    kept, forward_work, backward_work = rest[:6], rest[6:14], rest[14:19]
    my = index_ref[0]
    slots = out_ref.shape[0]
    forward_work[0][...] = key_bias(owners_ref[1], my, slots)

    def wait(name):
        return None

    forward_part(
        xg_ref[:, :D].astype(F32), weights, kept, forward_work, wait, lambda head: None,
        HEADS // 2,
    )
    dest = destination_row(owners_ref.at[0], my, next_x_ref.shape[0])
    dest_ref[...] = jnp.broadcast_to(dest, dest_ref.shape)
    out_ref[:, D:] = mm(one_hot(dest, slots), next_x_ref[...]).astype(BF)
    out_ref[:, :D] = backward_part(
        xg_ref.at[:, pl.ds(0, D)], xg_ref[:, D:], weights, kept, backward_work, wait,
        lambda: None,
    )


def forward_kernel(index_ref, rx_ref, owners_hbm, *rest):
    attend_hbm, output_hbm, up_hbm, down_hbm = rest[:4]
    value_ref, norm_ref, mixed_t_ref, up_ref, down_ref = rest[4:9]
    probs_out, x_out, query_out, key_out = rest[9:13]
    attend_ref, output_ref, probs_ref, query_t_ref, key_t_ref = rest[13:18]
    work = rest[18:26]
    owners_ref, in_sem, probs_sem, out_sem = rest[26:]
    my = index_ref[0]
    slots = rx_ref.shape[0]
    copies = fetch(
        in_sem,
        [
            (attend_hbm.at[0], attend_ref),
            (owners_hbm.at[0], owners_ref),
            (output_hbm.at[0], output_ref),
            (up_hbm.at[0], up_ref),
            (down_hbm.at[0], down_ref),
            (rx_ref.at[:, pl.ds(D, D)], x_out),
        ],
    )
    order = dict(attend=0, owners=1, output=2)

    def wait(name):
        copies[order[name]].wait()
        if name == "owners":
            work[0][...] = key_bias(owners_ref[...], my, slots)

    def probs_copy(head):
        return pltpu.make_async_copy(probs_ref.at[head], probs_out.at[head], probs_sem.at[head])

    forward_part(
        rx_ref[:, D:].astype(F32),
        (attend_ref, output_ref),
        (value_ref, query_t_ref, key_t_ref, probs_ref, norm_ref, mixed_t_ref),
        work, wait, lambda head: probs_copy(head).start(), 1,
    )
    for copy in copies[3:] + fetch(out_sem, [(query_t_ref, query_out), (key_t_ref, key_out)]):
        copy.wait()
    for head in range(HEADS):
        probs_copy(head).wait()


def backward_kernel(
    g_ref, value_ref, norm_ref, mixed_t_ref, up_ref, down_ref, probs_hbm,
    x_hbm, query_hbm, key_hbm, attend_hbm, output_hbm,
    out_ref,
    attend_ref, output_ref, x_ref, probs_ref, query_t_ref, key_t_ref, *rest,
):
    work, (sem, probs_sem) = rest[:5], rest[5:]
    pairs = [(output_hbm.at[0], output_ref), (query_hbm, query_t_ref), (key_hbm, key_t_ref)]
    pairs += [(attend_hbm.at[0], attend_ref), (x_hbm, x_ref)]
    copies = [pltpu.make_async_copy(a, b, sem.at[i]) for i, (a, b) in enumerate(pairs)]
    for copy in copies[:3]:
        copy.start()
    order = dict(output=0, attend=3, x=4)

    def probs_copy(head):
        return pltpu.make_async_copy(probs_hbm.at[head], probs_ref.at[head], probs_sem.at[head])

    for head in range(HEADS):
        probs_copy(head).start()
    for copy in copies[3:]:
        copy.start()

    def wait(name):
        if name in order:
            copies[order[name]].wait()

    def before_heads():
        copies[1].wait()
        copies[2].wait()
        for head in range(HEADS):
            probs_copy(head).wait()

    out_ref[...] = backward_part(
        x_ref, g_ref[...], (attend_ref, output_ref, up_ref, down_ref),
        (value_ref, query_t_ref, key_t_ref, probs_ref, norm_ref, mixed_t_ref),
        work, wait, before_heads,
    )


SMEM_SPEC = pl.BlockSpec(memory_space=pltpu.SMEM)
VMEM_SPEC = pl.BlockSpec(memory_space=pltpu.VMEM)
HBM_SPEC = pl.BlockSpec(memory_space=pltpu.HBM)


def in_hbm(array):
    return pltpu.with_memory_space_constraint(array, pltpu.HBM)


def kept_shapes(slots):
    return [
        ((slots, D), BF),
        ((D, slots), BF),
        ((D, slots), BF),
        ((HEADS, slots, slots), BF),
        ((slots, D + LANES), F32),
        ((D, slots), F32),
    ]


def weight_scratch(weights):
    return [pltpu.VMEM(w.shape[1:], BF) for w in weights]


def forward_scratch(slots):
    return [
        pltpu.VMEM((slots, D), BF),
        pltpu.VMEM((slots, D), BF),
        pltpu.VMEM((slots, D), BF),
        pltpu.VMEM((D, slots), BF),
        pltpu.VMEM((slots, slots), F32),
        pltpu.VMEM((slots, slots), F32),
        pltpu.VMEM((8, slots), F32),
        pltpu.VMEM((8, slots), F32),
    ]


def backward_scratch(slots, hidden):
    return [
        pltpu.VMEM((slots, hidden), BF),
        pltpu.VMEM((slots, D), BF),
        pltpu.VMEM((D, slots), BF),
        pltpu.VMEM((HEADS, slots), F32),
        pltpu.VMEM((3 * D, slots), BF),
    ]


def call(kernel, outs, in_specs, out_specs, scratch, name):
    return pl.pallas_call(
        kernel,
        out_shape=outs,
        in_specs=in_specs,
        out_specs=out_specs,
        scratch_shapes=scratch,
        name=name,
        compiler_params=pltpu.CompilerParams(vmem_limit_bytes=40 << 20),
    )


def prefetch(after, owners, saved_inputs, weights):
    shapes = [(owners.shape, jnp.int32), (saved_inputs.shape[1:], BF)]
    shapes += [(w.shape[1:], BF) for w in weights]
    return call(
        prefetch_kernel,
        tuple(jax.ShapeDtypeStruct(*k) for k in shapes),
        [HBM_SPEC] * 2 + [VMEM_SPEC] + [HBM_SPEC] * 4,
        (VMEM_SPEC,) * 6,
        [pltpu.SemaphoreType.DMA((6,))],
        "prefetch",
    )(owners, saved_inputs, after, *weights)


def whole_layer(my_index, xg, owners, next_x, weights):
    slots, hidden, points = xg.shape[0], weights[2].shape[1], next_x.shape[0]
    return call(
        whole_layer_kernel,
        (jax.ShapeDtypeStruct((slots, 2 * D), BF), jax.ShapeDtypeStruct((8, points), F32)),
        [SMEM_SPEC] + [VMEM_SPEC] * 7,
        (VMEM_SPEC, VMEM_SPEC),
        [pltpu.VMEM(*k) for k in kept_shapes(slots)]
        + forward_scratch(slots)
        + backward_scratch(slots, hidden),
        "whole_layer",
    )(my_index, xg, owners, next_x, *weights)


def forward(my_index, rx, owners, weights):
    slots = rx.shape[0]
    shapes = kept_shapes(slots)
    attend, output, up, down = weights
    return call(
        forward_kernel,
        tuple(jax.ShapeDtypeStruct(*shapes[i]) for i in (0, 4, 5))
        + tuple(jax.ShapeDtypeStruct(w.shape[1:], BF) for w in (up, down))
        + tuple(pltpu.HBM(*k) for k in (shapes[3], shapes[0], shapes[1], shapes[2])),
        [SMEM_SPEC, VMEM_SPEC] + [HBM_SPEC] * 5,
        (VMEM_SPEC,) * 5 + (HBM_SPEC,) * 4,
        weight_scratch((attend, output))
        + [pltpu.VMEM(*shapes[i]) for i in (3, 1, 2)]
        + forward_scratch(slots)
        + [
            pltpu.VMEM(owners.shape[1:], jnp.int32),
            pltpu.SemaphoreType.DMA((6,)),
            pltpu.SemaphoreType.DMA((HEADS,)),
            pltpu.SemaphoreType.DMA((2,)),
        ],
        "layer_forward",
    )(my_index, rx, owners, *weights)


def backward(g, kept, weights):
    slots = g.shape[0]
    attend, output, up, _ = weights
    return call(
        backward_kernel,
        jax.ShapeDtypeStruct((slots, D), BF),
        [VMEM_SPEC] * 6 + [HBM_SPEC] * 6,
        VMEM_SPEC,
        weight_scratch((attend, output))
        + [pltpu.VMEM(*kept_shapes(slots)[i]) for i in (0, 3, 1, 2)]
        + backward_scratch(slots, up.shape[2])
        + [pltpu.SemaphoreType.DMA((5,)), pltpu.SemaphoreType.DMA((HEADS,))],
        "layer_backward",
    )(g, *kept[:5], *(in_hbm(k) for k in kept[5:]), attend, output)


def per_device(saved_inputs, output_grads, owner_ids, attend, output, up, down):
    devices = lax.axis_size("blk")
    points = saved_inputs.shape[1]
    slots = devices * 8
    my_index = lax.axis_index("blk").astype(jnp.int32).reshape(1)
    owners = in_hbm(owner_ids.reshape(2, devices * points // LANES, LANES))
    saved_inputs, output_grads = in_hbm(saved_inputs), in_hbm(output_grads)
    weights = tuple(in_hbm(w) for w in (attend, output, up, down))

    def exchange(rows):
        width = rows.shape[1]
        moved = lax.all_to_all(
            rows.reshape(devices, 8, width), "blk", split_axis=0, concat_axis=0, tiled=True
        )
        return moved.reshape(slots, width)

    dest_one, packed = call(
        route_kernel,
        (jax.ShapeDtypeStruct((8, points), F32), jax.ShapeDtypeStruct((slots, 2 * D), BF)),
        [SMEM_SPEC] + [HBM_SPEC] * 3,
        (VMEM_SPEC, VMEM_SPEC),
        [
            pltpu.VMEM(owners.shape[1:], jnp.int32),
            pltpu.VMEM((points, D), BF),
            pltpu.VMEM((points, D), BF),
            pltpu.SemaphoreType.DMA((3,)),
        ],
        "route",
    )(my_index, owners, saved_inputs, output_grads)
    xg = exchange(packed)
    fetched = prefetch(dest_one, owners, saved_inputs, weights)
    result, dest_zero = whole_layer(my_index, xg, *fetched[:2], fetched[2:])
    rx = exchange(result)
    packed = call(
        repack_kernel, jax.ShapeDtypeStruct((slots, D), BF), [VMEM_SPEC] * 3, VMEM_SPEC, [], "repack"
    )(dest_one, dest_zero, rx)
    g_zero = exchange(packed)
    kept = forward(my_index, rx, owners, weights)
    result = backward(g_zero, kept, weights)
    return call(
        unpack_kernel, jax.ShapeDtypeStruct((points, D), BF), [VMEM_SPEC] * 2, VMEM_SPEC, [], "unpack"
    )(dest_zero, exchange(result))


def solution(mesh):
    placed = (
        P(None, ("rep", "blk"), None),
        P(("rep", "blk"), None),
        P(None, "rep", None),
        P(),
        P(),
        P(),
        P(),
    )
    return jax.shard_map(
        per_device, mesh=mesh, in_specs=placed, out_specs=P(("rep", "blk"), None), check_vma=False
    )
```

```python
import jax
import jax.numpy as jnp
from jax import lax
from jax.experimental import pallas as pl
from jax.experimental.pallas import tpu as pltpu
from jax.sharding import PartitionSpec as P

D = 256
HEADS = 8
HD = D // HEADS
EPSILON = 1e-05
MASKED = -1e30
SCALE = HD ** (-0.5)
LOG2E = 1.4426950408889634
BF = jnp.bfloat16
F32 = jnp.float32


def mm(left, right):
    return lax.dot_general(left, right, (((1,), (0,)), ((), ())), preferred_element_type=F32)


def mm_t(left, right):
    return lax.dot_general(left, right, (((1,), (1,)), ((), ())), preferred_element_type=F32)


def iota(shape, axis):
    return lax.broadcasted_iota(jnp.int32, shape, axis)


def destination_row(owners, my_index, points):
    wide_rows = points // LANES
    own_row = jnp.concatenate(
        [owners[pl.ds(my_index * wide_rows + i, 1), :] for i in range(wide_rows)], axis=1
    ).astype(F32)
    rows, cols = iota((points, points), 0), iota((points, points), 1)
    wide = jnp.broadcast_to(own_row, (points, points))
    own_col = jnp.sum(jnp.where(rows == cols, wide, 0.0), axis=1, keepdims=True)
    same = jnp.where((own_col == wide) & (rows < cols), 1.0, 0.0)
    rank = jnp.sum(same, axis=0, keepdims=True)
    return own_row * 8.0 + rank


def one_hot(dest_row, slots):
    shape = (slots, dest_row.shape[1])
    return jnp.where(iota(shape, 0).astype(F32) == dest_row, 1.0, 0.0).astype(BF)


def key_bias(owners, my_index, slots):
    rows = owners.shape[0]
    per_source = rows * 8 // slots
    count = jnp.sum(jnp.where(owners == my_index, 1.0, 0.0), axis=1, keepdims=True)
    shape = (slots, rows)
    spread = jnp.where(iota(shape, 0) // 8 == iota(shape, 1) // per_source, 1.0, 0.0).astype(BF)
    slot_count = mm(spread, jnp.broadcast_to(count, (rows, D)).astype(BF))
    rank = (iota(slot_count.shape, 0) % 8).astype(F32)
    return jnp.where(rank < slot_count, 0.0, MASKED).astype(BF)


def unpack(dest_row, rows):
    hot = one_hot(dest_row, rows.shape[0])
    return lax.dot_general(hot, rows, (((0,), (0,)), ((), ())), preferred_element_type=F32).astype(BF)


def fetch(sem, pairs):
    copies = [pltpu.make_async_copy(a, b, sem.at[i]) for i, (a, b) in enumerate(pairs)]
    for copy in copies:
        copy.start()
    return copies


def route_kernel(
    index_ref, owners_hbm, saved_hbm, g_hbm, dest_ref, out_hbm,
    owners_ref, x_ref, g_ref, packed_x_ref, packed_g_ref, sem, out_sem,
):
    slots, points = out_hbm.shape[0], g_hbm.shape[0]
    owners_in, x_in, g_in = fetch(
        sem, [(owners_hbm.at[1], owners_ref), (saved_hbm.at[1], x_ref), (g_hbm, g_ref)]
    )
    owners_in.wait()
    dest = destination_row(owners_ref, index_ref[0], points)
    dest_ref[...] = jnp.broadcast_to(dest, dest_ref.shape)
    hot = one_hot(dest, slots)
    x_in.wait()
    packed_x_ref[...] = mm(hot, x_ref[...]).astype(BF)
    x_out = pltpu.make_async_copy(packed_x_ref, out_hbm.at[:, pl.ds(0, D)], out_sem.at[0])
    x_out.start()
    g_in.wait()
    packed_g_ref[...] = mm(hot, g_ref[...]).astype(BF)
    g_out = pltpu.make_async_copy(packed_g_ref, out_hbm.at[:, pl.ds(D, D)], out_sem.at[1])
    g_out.start()
    x_out.wait()
    g_out.wait()


def repack_kernel(dest_one_ref, dest_zero_ref, rows_ref, out_hbm, packed_ref, sem):
    gradient = unpack(dest_one_ref[0:1, :], rows_ref[:, :D])
    slots = packed_ref.shape[0]
    hot = one_hot(dest_zero_ref[0:1, :], slots)
    copies = []
    for part in range(2):
        rows = pl.ds(part * (slots // 2), slots // 2)
        at = slice(part * (slots // 2), (part + 1) * (slots // 2))
        packed_ref[at, :] = mm(hot[at], gradient).astype(BF)
        copies.append(pltpu.make_async_copy(packed_ref.at[rows], out_hbm.at[rows], sem.at[part]))
        copies[part].start()
    for copy in copies:
        copy.wait()


def unpack_kernel(dest_ref, rows_ref, out_ref):
    out_ref[...] = unpack(dest_ref[0:1, :], rows_ref[...])


def normalized(values):
    centered = values - jnp.mean(values, axis=1, keepdims=True)
    inverse = lax.rsqrt(jnp.mean(centered * centered, axis=1, keepdims=True) + EPSILON)
    return centered * inverse, inverse


def norm_gradient(upstream, hat, inverse):
    mean_one = jnp.mean(upstream, axis=1, keepdims=True)
    mean_two = jnp.mean(upstream * hat, axis=1, keepdims=True)
    return inverse * (upstream - mean_one - hat * mean_two)


def head_lanes(shape, head):
    lane = iota(shape, 1)
    return (lane >= head * HD) & (lane < head * HD + HD)


def gelu_slope(pre):
    root, cubic = 0.7978845608028654, 0.044715
    square = pre * pre
    bend = jnp.tanh(pre * (root + (root * cubic) * square))
    rise = pre * (root + (3.0 * root * cubic) * square)
    return (0.5 + 0.5 * bend) * (1.0 + (1.0 - bend) * rise)


LANES = 128


def forward_part(x, weights, kept, work, wait, after_head, unroll):
    attend_ref, output_ref = weights[:2]
    value_ref, query_t_ref, key_t_ref, probs_ref, norm_ref, mixed_t_ref = kept
    bias_ref, query_ref, key_ref, value_t_ref, even_ref, odd_ref, even_max_ref, odd_max_ref = work
    slots = x.shape[0]
    normed, _ = normalized(x)
    wait("attend")
    qkv = mm(normed.astype(BF), attend_ref[...]).astype(BF)
    key_ref[...] = qkv[:, D : 2 * D]
    value_ref[...] = qkv[:, 2 * D :]
    value_t_ref[...] = qkv[:, 2 * D :].T
    query_t_ref[...] = qkv[:, :D].T
    key_t_ref[...] = qkv[:, D : 2 * D].T
    lane = iota((slots, D), 1)
    query_ref[...] = jnp.where(lane == 0, jnp.ones((slots, D), BF), qkv[:, :D])
    wait("owners")

    def score(keys, queries, scores_ref, max_ref):
        scores = mm_t(keys, queries)
        scores_ref[...] = scores
        max_ref[...] = jnp.broadcast_to(jnp.max(scores, axis=0, keepdims=True), (8, slots))

    def soften(head, scores_ref, max_ref):
        exponent = jnp.exp2((scores_ref[...] - max_ref[0:1, :]) * (SCALE * LOG2E))
        total = jnp.sum(exponent, axis=0, keepdims=True)
        probs = (exponent * (1.0 / total)).astype(BF)
        probs_ref[head] = probs
        at = pl.multiple_of(head * HD, HD)
        mixed_t_ref[pl.ds(at, HD), :] = mm(value_t_ref[pl.ds(at, HD), :], probs)

    bias = bias_ref[...]
    first_keys = jnp.where(
        head_lanes((slots, D), 0),
        qkv[:, D : 2 * D],
        jnp.where(lane == D - 1, bias, jnp.zeros_like(bias)),
    )
    first_queries = jnp.where(lane == D - 1, jnp.ones((slots, D), BF), qkv[:, :D])
    bias_ref[...] = jnp.where(lane == 0, bias, jnp.zeros_like(bias))
    score(first_keys, first_queries, even_ref, even_max_ref)

    def step(head, following, here, here_max, there, there_max):
        keys = jnp.where(head_lanes((slots, D), following), key_ref[...], bias_ref[...])
        score(keys, query_ref[...], there, there_max)
        soften(head, here, here_max)
        after_head(head)

    def pair(index, carry):
        step(2 * index, 2 * index + 1, even_ref, even_max_ref, odd_ref, odd_max_ref)
        following = jnp.minimum(2 * index + 2, HEADS - 1)
        step(2 * index + 1, following, odd_ref, odd_max_ref, even_ref, even_max_ref)
        return carry

    lax.fori_loop(0, HEADS // 2, pair, 0, unroll=unroll)
    attended = mixed_t_ref[...].astype(BF).T
    wait("output")
    mixed = mm(attended, output_ref[...]).astype(BF).astype(F32)
    hat, inverse = normalized(x + mixed)
    norm_ref[:, :D] = hat
    norm_ref[:, D:] = jnp.broadcast_to(inverse, (slots, LANES))


def backward_part(x_ref, g, weights, kept, work, wait, before_heads):
    attend_ref, output_ref, up_ref, down_ref = weights
    value_ref, query_t_ref, key_t_ref, probs_ref, norm_ref, mixed_t_ref = kept
    pre_grad_ref, up_grad_ref, up_grad_t_ref, delta_ref, grads_t_ref = work
    slots = g.shape[0]
    rounded = norm_ref[:, :D].astype(BF)
    wait("up")
    blocks = [slice(at, at + D) for at in range(0, up_ref.shape[1], D)]
    slopes = [gelu_slope(mm(rounded, up_ref[:, block])) for block in blocks]
    wait("down")
    for block, slope in zip(blocks, slopes):
        pre_grad_ref[:, block] = (slope * mm_t(g, down_ref[block, :])).astype(BF)
    normed_grad = mm_t(pre_grad_ref[...], up_ref[...])
    grad_mid = (
        g.astype(F32) + norm_gradient(normed_grad, norm_ref[:, :D], norm_ref[:, D : D + 1])
    ).astype(BF)
    wait("output")
    up_grad_ref[...] = mm_t(grad_mid, output_ref[...]).astype(BF)
    up_grad_t = mm_t(output_ref[...], grad_mid).astype(BF)
    up_grad_t_ref[...] = up_grad_t
    weighted = mixed_t_ref[...] * up_grad_t.astype(F32)
    for head in range(HEADS):
        delta_ref[head : head + 1, :] = jnp.sum(
            weighted[head * HD : (head + 1) * HD], axis=0, keepdims=True
        )

    def one_head(head, carry):
        values = jnp.where(
            head_lanes((slots, D), head), value_ref[...], jnp.zeros((slots, D), BF)
        )
        at = pl.multiple_of(head * HD, HD)
        prob_grads = mm_t(values, up_grad_ref[...])
        probs = probs_ref[head]
        delta = delta_ref[pl.ds(head, 1), :]
        score_grads = (probs.astype(F32) * (prob_grads - delta)).astype(BF)
        value_grad = mm_t(up_grad_t_ref[pl.ds(at, HD), :], probs)
        key_grad = mm_t(query_t_ref[pl.ds(at, HD), :], score_grads)
        grads_t_ref[pl.ds(at, HD), :] = (mm(key_t_ref[pl.ds(at, HD), :], score_grads) * SCALE).astype(BF)
        grads_t_ref[pl.ds(pl.multiple_of(D + at, HD), HD), :] = (key_grad * SCALE).astype(BF)
        grads_t_ref[pl.ds(pl.multiple_of(2 * D + at, HD), HD), :] = value_grad.astype(BF)
        return carry

    before_heads()
    lax.fori_loop(0, HEADS, one_head, 0, unroll=HEADS)
    wait("attend")
    normed_grads = mm(attend_ref[...], grads_t_ref[...]).T
    wait("x")
    hat, inverse = normalized(x_ref[...].astype(F32))
    branch = norm_gradient(normed_grads, hat, inverse).astype(BF)
    return (grad_mid.astype(F32) + branch.astype(F32)).astype(BF)


def prefetch_kernel(owners_hbm, saved_hbm, *rest):
    weights_hbm, (owners_ref, next_x_ref), weights = rest[1:5], rest[5:7], rest[7:11]
    copies = fetch(
        rest[11],
        [(owners_hbm, owners_ref), (saved_hbm.at[0], next_x_ref)]
        + [(hbm.at[1], ref) for hbm, ref in zip(weights_hbm, weights)],
    )
    for copy in copies:
        copy.wait()


def whole_layer_kernel(index_ref, xg_ref, owners_ref, next_x_ref, *rest):
    weights, (out_ref, dest_ref), rest = rest[:4], rest[4:6], rest[6:]
    kept, forward_work, backward_work = rest[:6], rest[6:14], rest[14:19]
    my = index_ref[0]
    slots = out_ref.shape[0]
    forward_work[0][...] = key_bias(owners_ref[1], my, slots)

    def wait(name):
        return None

    forward_part(
        xg_ref[:, :D].astype(F32), weights, kept, forward_work, wait, lambda head: None,
        HEADS // 2,
    )
    dest = destination_row(owners_ref.at[0], my, next_x_ref.shape[0])
    dest_ref[...] = jnp.broadcast_to(dest, dest_ref.shape)
    out_ref[:, D:] = mm(one_hot(dest, slots), next_x_ref[...]).astype(BF)
    out_ref[:, :D] = backward_part(
        xg_ref.at[:, pl.ds(0, D)], xg_ref[:, D:], weights, kept, backward_work, wait,
        lambda: None,
    )


def forward_kernel(index_ref, rx_ref, owners_hbm, *rest):
    attend_hbm, output_hbm, up_hbm, down_hbm = rest[:4]
    norm_ref, mixed_t_ref, attend_ref, output_ref, up_ref, down_ref = rest[4:10]
    probs_out, x_out, value_out, query_out, key_out = rest[10:15]
    probs_ref, value_ref, query_t_ref, key_t_ref = rest[15:19]
    work = rest[19:27]
    owners_ref, in_sem, probs_sem, out_sem = rest[27:]
    my = index_ref[0]
    slots = rx_ref.shape[0]
    copies = fetch(
        in_sem,
        [
            (attend_hbm.at[0], attend_ref),
            (owners_hbm.at[0], owners_ref),
            (output_hbm.at[0], output_ref),
            (up_hbm.at[0], up_ref),
            (down_hbm.at[0], down_ref),
            (rx_ref.at[:, pl.ds(D, D)], x_out),
        ],
    )
    order = dict(attend=0, owners=1, output=2)

    def wait(name):
        copies[order[name]].wait()
        if name == "owners":
            work[0][...] = key_bias(owners_ref[...], my, slots)

    def probs_copy(head):
        return pltpu.make_async_copy(probs_ref.at[head], probs_out.at[head], probs_sem.at[head])

    forward_part(
        rx_ref[:, D:].astype(F32),
        (attend_ref, output_ref),
        (value_ref, query_t_ref, key_t_ref, probs_ref, norm_ref, mixed_t_ref),
        work, wait, lambda head: probs_copy(head).start(), 1,
    )
    for copy in copies[3:] + fetch(
        out_sem, [(value_ref, value_out), (query_t_ref, query_out), (key_t_ref, key_out)]
    ):
        copy.wait()
    for head in range(HEADS):
        probs_copy(head).wait()


def backward_kernel(
    g_ref, norm_ref, mixed_t_ref, attend_ref, output_ref, up_ref, down_ref,
    probs_hbm, x_hbm, value_hbm, query_hbm, key_hbm,
    out_ref,
    x_ref, probs_ref, value_ref, query_t_ref, key_t_ref, *rest,
):
    work, sem = rest[:5], rest[5]
    pairs = [(value_hbm, value_ref), (query_hbm, query_t_ref), (key_hbm, key_t_ref)]
    pairs += [(x_hbm, x_ref)]
    pairs += [(probs_hbm.at[head], probs_ref.at[head]) for head in range(HEADS)]
    copies = fetch(sem, pairs)

    def before_heads():
        for copy in copies:
            copy.wait()

    out_ref[...] = backward_part(
        x_ref, g_ref[...], (attend_ref, output_ref, up_ref, down_ref),
        (value_ref, query_t_ref, key_t_ref, probs_ref, norm_ref, mixed_t_ref),
        work, lambda name: None, before_heads,
    )


SMEM_SPEC = pl.BlockSpec(memory_space=pltpu.SMEM)
VMEM_SPEC = pl.BlockSpec(memory_space=pltpu.VMEM)
HBM_SPEC = pl.BlockSpec(memory_space=pltpu.HBM)


def in_hbm(array):
    return pltpu.with_memory_space_constraint(array, pltpu.HBM)


def kept_shapes(slots):
    return [
        ((slots, D), BF),
        ((D, slots), BF),
        ((D, slots), BF),
        ((HEADS, slots, slots), BF),
        ((slots, D + LANES), F32),
        ((D, slots), F32),
    ]


def forward_scratch(slots):
    return [
        pltpu.VMEM((slots, D), BF),
        pltpu.VMEM((slots, D), BF),
        pltpu.VMEM((slots, D), BF),
        pltpu.VMEM((D, slots), BF),
        pltpu.VMEM((slots, slots), F32),
        pltpu.VMEM((slots, slots), F32),
        pltpu.VMEM((8, slots), F32),
        pltpu.VMEM((8, slots), F32),
    ]


def backward_scratch(slots, hidden):
    return [
        pltpu.VMEM((slots, hidden), BF),
        pltpu.VMEM((slots, D), BF),
        pltpu.VMEM((D, slots), BF),
        pltpu.VMEM((HEADS, slots), F32),
        pltpu.VMEM((3 * D, slots), BF),
    ]


def call(kernel, outs, in_specs, out_specs, scratch, name):
    return pl.pallas_call(
        kernel,
        out_shape=outs,
        in_specs=in_specs,
        out_specs=out_specs,
        scratch_shapes=scratch,
        name=name,
        compiler_params=pltpu.CompilerParams(vmem_limit_bytes=40 << 20),
    )


def prefetch(after, owners, saved_inputs, weights):
    shapes = [(owners.shape, jnp.int32), (saved_inputs.shape[1:], BF)]
    shapes += [(w.shape[1:], BF) for w in weights]
    return call(
        prefetch_kernel,
        tuple(jax.ShapeDtypeStruct(*k) for k in shapes),
        [HBM_SPEC] * 2 + [VMEM_SPEC] + [HBM_SPEC] * 4,
        (VMEM_SPEC,) * 6,
        [pltpu.SemaphoreType.DMA((6,))],
        "prefetch",
    )(owners, saved_inputs, after, *weights)


def whole_layer(my_index, xg, owners, next_x, weights):
    slots, hidden, points = xg.shape[0], weights[2].shape[1], next_x.shape[0]
    return call(
        whole_layer_kernel,
        (jax.ShapeDtypeStruct((slots, 2 * D), BF), jax.ShapeDtypeStruct((8, points), F32)),
        [SMEM_SPEC] + [VMEM_SPEC] * 7,
        (VMEM_SPEC, VMEM_SPEC),
        [pltpu.VMEM(*k) for k in kept_shapes(slots)]
        + forward_scratch(slots)
        + backward_scratch(slots, hidden),
        "whole_layer",
    )(my_index, xg, owners, next_x, *weights)


def forward(my_index, rx, owners, weights):
    slots = rx.shape[0]
    shapes = kept_shapes(slots)
    return call(
        forward_kernel,
        tuple(jax.ShapeDtypeStruct(*shapes[i]) for i in (4, 5))
        + tuple(jax.ShapeDtypeStruct(w.shape[1:], BF) for w in weights)
        + tuple(pltpu.HBM(*k) for k in (shapes[3], shapes[0], shapes[0], shapes[1], shapes[2])),
        [SMEM_SPEC, VMEM_SPEC] + [HBM_SPEC] * 5,
        (VMEM_SPEC,) * 6 + (HBM_SPEC,) * 5,
        [pltpu.VMEM(*shapes[i]) for i in (3, 0, 1, 2)]
        + forward_scratch(slots)
        + [
            pltpu.VMEM(owners.shape[1:], jnp.int32),
            pltpu.SemaphoreType.DMA((6,)),
            pltpu.SemaphoreType.DMA((HEADS,)),
            pltpu.SemaphoreType.DMA((3,)),
        ],
        "layer_forward",
    )(my_index, rx, owners, *weights)


def backward(g, kept, hidden):
    slots = g.shape[0]
    return call(
        backward_kernel,
        jax.ShapeDtypeStruct((slots, D), BF),
        [VMEM_SPEC] * 7 + [HBM_SPEC] * 5,
        VMEM_SPEC,
        [pltpu.VMEM(*kept_shapes(slots)[i]) for i in (0, 3, 0, 1, 2)]
        + backward_scratch(slots, hidden)
        + [pltpu.SemaphoreType.DMA((4 + HEADS,))],
        "layer_backward",
    )(g, *kept[:6], *(in_hbm(k) for k in kept[6:]))


def per_device(saved_inputs, output_grads, owner_ids, attend, output, up, down):
    devices = lax.axis_size("blk")
    points = saved_inputs.shape[1]
    slots = devices * 8
    my_index = lax.axis_index("blk").astype(jnp.int32).reshape(1)
    owners = in_hbm(owner_ids.reshape(2, devices * points // LANES, LANES))
    saved_inputs, output_grads = in_hbm(saved_inputs), in_hbm(output_grads)
    weights = tuple(in_hbm(w) for w in (attend, output, up, down))

    def exchange(rows):
        width = rows.shape[1]
        moved = lax.all_to_all(
            rows.reshape(devices, 8, width), "blk", split_axis=0, concat_axis=0, tiled=True
        )
        return moved.reshape(slots, width)

    dest_one, packed = call(
        route_kernel,
        (jax.ShapeDtypeStruct((8, points), F32), pltpu.HBM((slots, 2 * D), BF)),
        [SMEM_SPEC] + [HBM_SPEC] * 3,
        (VMEM_SPEC, HBM_SPEC),
        [
            pltpu.VMEM(owners.shape[1:], jnp.int32),
            pltpu.VMEM((points, D), BF),
            pltpu.VMEM((points, D), BF),
            pltpu.VMEM((slots, D), BF),
            pltpu.VMEM((slots, D), BF),
            pltpu.SemaphoreType.DMA((3,)),
            pltpu.SemaphoreType.DMA((2,)),
        ],
        "route",
    )(my_index, owners, saved_inputs, output_grads)
    xg = exchange(packed)
    fetched = prefetch(dest_one, owners, saved_inputs, weights)
    result, dest_zero = whole_layer(my_index, xg, *fetched[:2], fetched[2:])
    rx = exchange(result)
    packed = call(
        repack_kernel,
        pltpu.HBM((slots, D), BF),
        [VMEM_SPEC] * 3,
        HBM_SPEC,
        [pltpu.VMEM((slots, D), BF), pltpu.SemaphoreType.DMA((2,))],
        "repack",
    )(dest_one, dest_zero, rx)
    g_zero = exchange(packed)
    kept = forward(my_index, rx, owners, weights)
    result = backward(g_zero, kept, up.shape[2])
    return call(
        unpack_kernel, jax.ShapeDtypeStruct((points, D), BF), [VMEM_SPEC] * 2, VMEM_SPEC, [], "unpack"
    )(dest_zero, exchange(result))


def solution(mesh):
    placed = (
        P(None, ("rep", "blk"), None),
        P(("rep", "blk"), None),
        P(None, "rep", None),
        P(),
        P(),
        P(),
        P(),
    )
    return jax.shard_map(
        per_device, mesh=mesh, in_specs=placed, out_specs=P(("rep", "blk"), None), check_vma=False
    )
```

```python
import jax
import jax.numpy as jnp
from jax import lax
from jax.experimental import pallas as pl
from jax.experimental.pallas import tpu as pltpu
from jax.sharding import PartitionSpec as P

D = 256
HEADS = 8
HD = D // HEADS
EPSILON = 1e-05
MASKED = -1e30
SCALE = HD ** (-0.5)
LOG2E = 1.4426950408889634
BF = jnp.bfloat16
F32 = jnp.float32


def mm(left, right):
    return lax.dot_general(left, right, (((1,), (0,)), ((), ())), preferred_element_type=F32)


def mm_t(left, right):
    return lax.dot_general(left, right, (((1,), (1,)), ((), ())), preferred_element_type=F32)


def iota(shape, axis):
    return lax.broadcasted_iota(jnp.int32, shape, axis)


def destination_row(owners, my_index, points):
    wide_rows = points // LANES
    own_row = jnp.concatenate(
        [owners[pl.ds(my_index * wide_rows + i, 1), :] for i in range(wide_rows)], axis=1
    ).astype(F32)
    rows, cols = iota((points, points), 0), iota((points, points), 1)
    wide = jnp.broadcast_to(own_row, (points, points))
    own_col = jnp.sum(jnp.where(rows == cols, wide, 0.0), axis=1, keepdims=True)
    same = jnp.where((own_col == wide) & (rows < cols), 1.0, 0.0)
    rank = jnp.sum(same, axis=0, keepdims=True)
    return own_row * 8.0 + rank


def one_hot(dest_row, slots):
    shape = (slots, dest_row.shape[1])
    return jnp.where(iota(shape, 0).astype(F32) == dest_row, 1.0, 0.0).astype(BF)


def key_bias(owners, my_index, slots):
    rows = owners.shape[0]
    per_source = rows * 8 // slots
    count = jnp.sum(jnp.where(owners == my_index, 1.0, 0.0), axis=1, keepdims=True)
    shape = (slots, rows)
    spread = jnp.where(iota(shape, 0) // 8 == iota(shape, 1) // per_source, 1.0, 0.0).astype(BF)
    slot_count = mm(spread, jnp.broadcast_to(count, (rows, D)).astype(BF))
    rank = (iota(slot_count.shape, 0) % 8).astype(F32)
    return jnp.where(rank < slot_count, 0.0, MASKED).astype(BF)


def unpack(dest_row, rows):
    hot = one_hot(dest_row, rows.shape[0])
    return lax.dot_general(hot, rows, (((0,), (0,)), ((), ())), preferred_element_type=F32).astype(BF)


def fetch(sem, pairs):
    copies = [pltpu.make_async_copy(a, b, sem.at[i]) for i, (a, b) in enumerate(pairs)]
    for copy in copies:
        copy.start()
    return copies


def route_kernel(
    index_ref, owners_hbm, saved_hbm, g_hbm, dest_ref, out_hbm,
    owners_ref, x_ref, g_ref, packed_x_ref, packed_g_ref, sem, out_sem,
):
    slots, points = out_hbm.shape[0], g_hbm.shape[0]
    owners_in, x_in, g_in = fetch(
        sem, [(owners_hbm.at[1], owners_ref), (saved_hbm.at[1], x_ref), (g_hbm, g_ref)]
    )
    owners_in.wait()
    dest = destination_row(owners_ref, index_ref[0], points)
    dest_ref[...] = jnp.broadcast_to(dest, dest_ref.shape)
    hot = one_hot(dest, slots)
    x_in.wait()
    packed_x_ref[...] = mm(hot, x_ref[...]).astype(BF)
    x_out = pltpu.make_async_copy(packed_x_ref, out_hbm.at[:, pl.ds(0, D)], out_sem.at[0])
    x_out.start()
    g_in.wait()
    packed_g_ref[...] = mm(hot, g_ref[...]).astype(BF)
    g_out = pltpu.make_async_copy(packed_g_ref, out_hbm.at[:, pl.ds(D, D)], out_sem.at[1])
    g_out.start()
    x_out.wait()
    g_out.wait()


def repack_kernel(dest_one_ref, dest_zero_ref, rows_ref, out_hbm, packed_ref, sem):
    gradient = unpack(dest_one_ref[0:1, :], rows_ref[:, :D])
    slots = packed_ref.shape[0]
    hot = one_hot(dest_zero_ref[0:1, :], slots)
    copies = []
    for part in range(2):
        rows = pl.ds(part * (slots // 2), slots // 2)
        at = slice(part * (slots // 2), (part + 1) * (slots // 2))
        packed_ref[at, :] = mm(hot[at], gradient).astype(BF)
        copies.append(pltpu.make_async_copy(packed_ref.at[rows], out_hbm.at[rows], sem.at[part]))
        copies[part].start()
    for copy in copies:
        copy.wait()


def unpack_kernel(dest_ref, rows_ref, out_ref):
    out_ref[...] = unpack(dest_ref[0:1, :], rows_ref[...])


def normalized(values):
    centered = values - jnp.mean(values, axis=1, keepdims=True)
    inverse = lax.rsqrt(jnp.mean(centered * centered, axis=1, keepdims=True) + EPSILON)
    return centered * inverse, inverse


def norm_gradient(upstream, hat, inverse):
    mean_one = jnp.mean(upstream, axis=1, keepdims=True)
    mean_two = jnp.mean(upstream * hat, axis=1, keepdims=True)
    return inverse * (upstream - mean_one - hat * mean_two)


def head_lanes(shape, head):
    lane = iota(shape, 1)
    return (lane >= head * HD) & (lane < head * HD + HD)


def gelu_slope(pre):
    root, cubic = 0.7978845608028654, 0.044715
    square = pre * pre
    bend = jnp.tanh(pre * (root + (root * cubic) * square))
    rise = pre * (root + (3.0 * root * cubic) * square)
    return (0.5 + 0.5 * bend) * (1.0 + (1.0 - bend) * rise)


LANES = 128


def forward_part(x, weights, kept, work, wait, after_head, unroll):
    attend_ref, output_ref = weights[:2]
    value_ref, query_t_ref, key_t_ref, probs_ref, norm_ref, mixed_t_ref = kept
    bias_ref, query_ref, key_ref, value_t_ref, even_ref, odd_ref, even_max_ref, odd_max_ref = work
    slots = x.shape[0]
    normed, _ = normalized(x)
    wait("attend")
    qkv = mm(normed.astype(BF), attend_ref[...]).astype(BF)
    key_ref[...] = qkv[:, D : 2 * D]
    value_ref[...] = qkv[:, 2 * D :]
    value_t_ref[...] = qkv[:, 2 * D :].T
    query_t_ref[...] = qkv[:, :D].T
    key_t_ref[...] = qkv[:, D : 2 * D].T
    lane = iota((slots, D), 1)
    query_ref[...] = jnp.where(lane == 0, jnp.ones((slots, D), BF), qkv[:, :D])
    wait("owners")

    def score(keys, queries, scores_ref, max_ref):
        scores = mm_t(keys, queries)
        scores_ref[...] = scores
        max_ref[...] = jnp.broadcast_to(jnp.max(scores, axis=0, keepdims=True), (8, slots))

    def soften(head, scores_ref, max_ref):
        exponent = jnp.exp2((scores_ref[...] - max_ref[0:1, :]) * (SCALE * LOG2E))
        total = jnp.sum(exponent, axis=0, keepdims=True)
        probs = (exponent * (1.0 / total)).astype(BF)
        probs_ref[head] = probs
        at = pl.multiple_of(head * HD, HD)
        mixed_t_ref[pl.ds(at, HD), :] = mm(value_t_ref[pl.ds(at, HD), :], probs)

    bias = bias_ref[...]
    first_keys = jnp.where(
        head_lanes((slots, D), 0),
        qkv[:, D : 2 * D],
        jnp.where(lane == D - 1, bias, jnp.zeros_like(bias)),
    )
    first_queries = jnp.where(lane == D - 1, jnp.ones((slots, D), BF), qkv[:, :D])
    bias_ref[...] = jnp.where(lane == 0, bias, jnp.zeros_like(bias))
    score(first_keys, first_queries, even_ref, even_max_ref)

    def step(head, following, here, here_max, there, there_max):
        keys = jnp.where(head_lanes((slots, D), following), key_ref[...], bias_ref[...])
        score(keys, query_ref[...], there, there_max)
        soften(head, here, here_max)
        after_head(head)

    def pair(index, carry):
        step(2 * index, 2 * index + 1, even_ref, even_max_ref, odd_ref, odd_max_ref)
        following = jnp.minimum(2 * index + 2, HEADS - 1)
        step(2 * index + 1, following, odd_ref, odd_max_ref, even_ref, even_max_ref)
        return carry

    lax.fori_loop(0, HEADS // 2, pair, 0, unroll=unroll)
    attended = mixed_t_ref[...].astype(BF).T
    wait("output")
    mixed = mm(attended, output_ref[...]).astype(BF).astype(F32)
    hat, inverse = normalized(x + mixed)
    norm_ref[:, :D] = hat
    norm_ref[:, D:] = jnp.broadcast_to(inverse, (slots, LANES))


def backward_part(x_ref, g, weights, kept, work, wait, before_heads):
    attend_ref, output_ref, up_ref, down_ref = weights
    value_ref, query_t_ref, key_t_ref, probs_ref, norm_ref, mixed_t_ref = kept
    pre_grad_ref, up_grad_ref, up_grad_t_ref, delta_ref, grads_t_ref = work
    slots = g.shape[0]
    rounded = norm_ref[:, :D].astype(BF)
    wait("up")
    blocks = [slice(at, at + D) for at in range(0, up_ref.shape[1], D)]
    slopes = [gelu_slope(mm(rounded, up_ref[:, block])) for block in blocks]
    wait("down")
    for block, slope in zip(blocks, slopes):
        pre_grad_ref[:, block] = (slope * mm_t(g, down_ref[block, :])).astype(BF)
    normed_grad = mm_t(pre_grad_ref[...], up_ref[...])
    grad_mid = (
        g.astype(F32) + norm_gradient(normed_grad, norm_ref[:, :D], norm_ref[:, D : D + 1])
    ).astype(BF)
    wait("output")
    up_grad_ref[...] = mm_t(grad_mid, output_ref[...]).astype(BF)
    up_grad_t = mm_t(output_ref[...], grad_mid).astype(BF)
    up_grad_t_ref[...] = up_grad_t
    weighted = mixed_t_ref[...] * up_grad_t.astype(F32)
    for head in range(HEADS):
        delta_ref[head : head + 1, :] = jnp.sum(
            weighted[head * HD : (head + 1) * HD], axis=0, keepdims=True
        )

    def one_head(head, carry):
        values = jnp.where(
            head_lanes((slots, D), head), value_ref[...], jnp.zeros((slots, D), BF)
        )
        at = pl.multiple_of(head * HD, HD)
        prob_grads = mm_t(values, up_grad_ref[...])
        probs = probs_ref[head]
        delta = delta_ref[pl.ds(head, 1), :]
        score_grads = (probs.astype(F32) * (prob_grads - delta)).astype(BF)
        value_grad = mm_t(up_grad_t_ref[pl.ds(at, HD), :], probs)
        key_grad = mm_t(query_t_ref[pl.ds(at, HD), :], score_grads)
        grads_t_ref[pl.ds(at, HD), :] = (mm(key_t_ref[pl.ds(at, HD), :], score_grads) * SCALE).astype(BF)
        grads_t_ref[pl.ds(pl.multiple_of(D + at, HD), HD), :] = (key_grad * SCALE).astype(BF)
        grads_t_ref[pl.ds(pl.multiple_of(2 * D + at, HD), HD), :] = value_grad.astype(BF)
        return carry

    before_heads()
    lax.fori_loop(0, HEADS, one_head, 0, unroll=HEADS)
    wait("attend")
    normed_grads = mm(attend_ref[...], grads_t_ref[...]).T
    wait("x")
    hat, inverse = normalized(x_ref[...].astype(F32))
    branch = norm_gradient(normed_grads, hat, inverse).astype(BF)
    return (grad_mid.astype(F32) + branch.astype(F32)).astype(BF)


def prefetch_kernel(owners_hbm, saved_hbm, *rest):
    weights_hbm, (owners_ref, next_x_ref), weights = rest[1:5], rest[5:7], rest[7:11]
    copies = fetch(
        rest[11],
        [(owners_hbm, owners_ref), (saved_hbm.at[0], next_x_ref)]
        + [(hbm.at[1], ref) for hbm, ref in zip(weights_hbm, weights)],
    )
    for copy in copies:
        copy.wait()


def whole_layer_kernel(index_ref, xg_ref, owners_ref, next_x_ref, *rest):
    weights, (out_ref, dest_ref), rest = rest[:4], rest[4:6], rest[6:]
    kept, forward_work, backward_work = rest[:6], rest[6:14], rest[14:19]
    my = index_ref[0]
    slots = out_ref.shape[0]
    forward_work[0][...] = key_bias(owners_ref[1], my, slots)

    def wait(name):
        return None

    forward_part(
        xg_ref[:, :D].astype(F32), weights, kept, forward_work, wait, lambda head: None,
        HEADS // 2,
    )
    dest = destination_row(owners_ref.at[0], my, next_x_ref.shape[0])
    dest_ref[...] = jnp.broadcast_to(dest, dest_ref.shape)
    out_ref[:, D:] = mm(one_hot(dest, slots), next_x_ref[...]).astype(BF)
    out_ref[:, :D] = backward_part(
        xg_ref.at[:, pl.ds(0, D)], xg_ref[:, D:], weights, kept, backward_work, wait,
        lambda: None,
    )


def forward_kernel(index_ref, rx_ref, owners_hbm, *rest):
    attend_hbm, output_hbm, up_hbm, down_hbm = rest[:4]
    norm_ref, mixed_t_ref, output_ref, up_ref, down_ref = rest[4:9]
    probs_out, x_out, value_out, query_out, key_out = rest[9:14]
    attend_ref, probs_ref, value_ref, query_t_ref, key_t_ref = rest[14:19]
    work = rest[19:27]
    owners_ref, in_sem, probs_sem, out_sem = rest[27:]
    my = index_ref[0]
    slots = rx_ref.shape[0]
    copies = fetch(
        in_sem,
        [
            (attend_hbm.at[0], attend_ref),
            (owners_hbm.at[0], owners_ref),
            (output_hbm.at[0], output_ref),
            (up_hbm.at[0], up_ref),
            (down_hbm.at[0], down_ref),
            (rx_ref.at[:, pl.ds(D, D)], x_out),
        ],
    )
    order = dict(attend=0, owners=1, output=2)

    def wait(name):
        copies[order[name]].wait()
        if name == "owners":
            work[0][...] = key_bias(owners_ref[...], my, slots)

    def probs_copy(head):
        return pltpu.make_async_copy(probs_ref.at[head], probs_out.at[head], probs_sem.at[head])

    forward_part(
        rx_ref[:, D:].astype(F32),
        (attend_ref, output_ref),
        (value_ref, query_t_ref, key_t_ref, probs_ref, norm_ref, mixed_t_ref),
        work, wait, lambda head: probs_copy(head).start(), 1,
    )
    for copy in copies[3:] + fetch(
        out_sem, [(value_ref, value_out), (query_t_ref, query_out), (key_t_ref, key_out)]
    ):
        copy.wait()
    for head in range(HEADS):
        probs_copy(head).wait()


def backward_kernel(
    g_ref, norm_ref, mixed_t_ref, output_ref, up_ref, down_ref,
    probs_hbm, x_hbm, value_hbm, query_hbm, key_hbm, attend_hbm,
    out_ref,
    attend_ref, x_ref, probs_ref, value_ref, query_t_ref, key_t_ref, *rest,
):
    work, sem = rest[:5], rest[5]
    pairs = [(value_hbm, value_ref), (query_hbm, query_t_ref), (key_hbm, key_t_ref)]
    pairs += [(x_hbm, x_ref)]
    pairs += [(probs_hbm.at[head], probs_ref.at[head]) for head in range(HEADS)]
    pairs.append((attend_hbm.at[0], attend_ref))
    copies = fetch(sem, pairs)

    def before_heads():
        for copy in copies:
            copy.wait()

    out_ref[...] = backward_part(
        x_ref, g_ref[...], (attend_ref, output_ref, up_ref, down_ref),
        (value_ref, query_t_ref, key_t_ref, probs_ref, norm_ref, mixed_t_ref),
        work, lambda name: None, before_heads,
    )


SMEM_SPEC = pl.BlockSpec(memory_space=pltpu.SMEM)
VMEM_SPEC = pl.BlockSpec(memory_space=pltpu.VMEM)
HBM_SPEC = pl.BlockSpec(memory_space=pltpu.HBM)


def in_hbm(array):
    return pltpu.with_memory_space_constraint(array, pltpu.HBM)


def kept_shapes(slots):
    return [
        ((slots, D), BF),
        ((D, slots), BF),
        ((D, slots), BF),
        ((HEADS, slots, slots), BF),
        ((slots, D + LANES), F32),
        ((D, slots), F32),
    ]


def forward_scratch(slots):
    return [
        pltpu.VMEM((slots, D), BF),
        pltpu.VMEM((slots, D), BF),
        pltpu.VMEM((slots, D), BF),
        pltpu.VMEM((D, slots), BF),
        pltpu.VMEM((slots, slots), F32),
        pltpu.VMEM((slots, slots), F32),
        pltpu.VMEM((8, slots), F32),
        pltpu.VMEM((8, slots), F32),
    ]


def backward_scratch(slots, hidden):
    return [
        pltpu.VMEM((slots, hidden), BF),
        pltpu.VMEM((slots, D), BF),
        pltpu.VMEM((D, slots), BF),
        pltpu.VMEM((HEADS, slots), F32),
        pltpu.VMEM((3 * D, slots), BF),
    ]


def call(kernel, outs, in_specs, out_specs, scratch, name):
    return pl.pallas_call(
        kernel,
        out_shape=outs,
        in_specs=in_specs,
        out_specs=out_specs,
        scratch_shapes=scratch,
        name=name,
        compiler_params=pltpu.CompilerParams(vmem_limit_bytes=40 << 20),
    )


def prefetch(after, owners, saved_inputs, weights):
    shapes = [(owners.shape, jnp.int32), (saved_inputs.shape[1:], BF)]
    shapes += [(w.shape[1:], BF) for w in weights]
    return call(
        prefetch_kernel,
        tuple(jax.ShapeDtypeStruct(*k) for k in shapes),
        [HBM_SPEC] * 2 + [VMEM_SPEC] + [HBM_SPEC] * 4,
        (VMEM_SPEC,) * 6,
        [pltpu.SemaphoreType.DMA((6,))],
        "prefetch",
    )(owners, saved_inputs, after, *weights)


def whole_layer(my_index, xg, owners, next_x, weights):
    slots, hidden, points = xg.shape[0], weights[2].shape[1], next_x.shape[0]
    return call(
        whole_layer_kernel,
        (jax.ShapeDtypeStruct((slots, 2 * D), BF), jax.ShapeDtypeStruct((8, points), F32)),
        [SMEM_SPEC] + [VMEM_SPEC] * 7,
        (VMEM_SPEC, VMEM_SPEC),
        [pltpu.VMEM(*k) for k in kept_shapes(slots)]
        + forward_scratch(slots)
        + backward_scratch(slots, hidden),
        "whole_layer",
    )(my_index, xg, owners, next_x, *weights)


def forward(my_index, rx, owners, weights):
    slots = rx.shape[0]
    shapes = kept_shapes(slots)
    return call(
        forward_kernel,
        tuple(jax.ShapeDtypeStruct(*shapes[i]) for i in (4, 5))
        + tuple(jax.ShapeDtypeStruct(w.shape[1:], BF) for w in weights[1:])
        + tuple(pltpu.HBM(*k) for k in (shapes[3], shapes[0], shapes[0], shapes[1], shapes[2])),
        [SMEM_SPEC, VMEM_SPEC] + [HBM_SPEC] * 5,
        (VMEM_SPEC,) * 5 + (HBM_SPEC,) * 5,
        [pltpu.VMEM(weights[0].shape[1:], BF)]
        + [pltpu.VMEM(*shapes[i]) for i in (3, 0, 1, 2)]
        + forward_scratch(slots)
        + [
            pltpu.VMEM(owners.shape[1:], jnp.int32),
            pltpu.SemaphoreType.DMA((6,)),
            pltpu.SemaphoreType.DMA((HEADS,)),
            pltpu.SemaphoreType.DMA((3,)),
        ],
        "layer_forward",
    )(my_index, rx, owners, *weights)


def backward(g, kept, weights):
    slots, hidden = g.shape[0], weights[2].shape[2]
    return call(
        backward_kernel,
        jax.ShapeDtypeStruct((slots, D), BF),
        [VMEM_SPEC] * 6 + [HBM_SPEC] * 6,
        VMEM_SPEC,
        [pltpu.VMEM(weights[0].shape[1:], BF)]
        + [pltpu.VMEM(*kept_shapes(slots)[i]) for i in (0, 3, 0, 1, 2)]
        + backward_scratch(slots, hidden)
        + [pltpu.SemaphoreType.DMA((5 + HEADS,))],
        "layer_backward",
    )(g, *kept[:5], *(in_hbm(k) for k in kept[5:]), weights[0])


def per_device(saved_inputs, output_grads, owner_ids, attend, output, up, down):
    devices = lax.axis_size("blk")
    points = saved_inputs.shape[1]
    slots = devices * 8
    my_index = lax.axis_index("blk").astype(jnp.int32).reshape(1)
    owners = in_hbm(owner_ids.reshape(2, devices * points // LANES, LANES))
    saved_inputs, output_grads = in_hbm(saved_inputs), in_hbm(output_grads)
    weights = tuple(in_hbm(w) for w in (attend, output, up, down))

    def exchange(rows):
        width = rows.shape[1]
        moved = lax.all_to_all(
            rows.reshape(devices, 8, width), "blk", split_axis=0, concat_axis=0, tiled=True
        )
        return moved.reshape(slots, width)

    dest_one, packed = call(
        route_kernel,
        (jax.ShapeDtypeStruct((8, points), F32), pltpu.HBM((slots, 2 * D), BF)),
        [SMEM_SPEC] + [HBM_SPEC] * 3,
        (VMEM_SPEC, HBM_SPEC),
        [
            pltpu.VMEM(owners.shape[1:], jnp.int32),
            pltpu.VMEM((points, D), BF),
            pltpu.VMEM((points, D), BF),
            pltpu.VMEM((slots, D), BF),
            pltpu.VMEM((slots, D), BF),
            pltpu.SemaphoreType.DMA((3,)),
            pltpu.SemaphoreType.DMA((2,)),
        ],
        "route",
    )(my_index, owners, saved_inputs, output_grads)
    xg = exchange(packed)
    fetched = prefetch(dest_one, owners, saved_inputs, weights)
    result, dest_zero = whole_layer(my_index, xg, *fetched[:2], fetched[2:])
    rx = exchange(result)
    packed = call(
        repack_kernel,
        pltpu.HBM((slots, D), BF),
        [VMEM_SPEC] * 3,
        HBM_SPEC,
        [pltpu.VMEM((slots, D), BF), pltpu.SemaphoreType.DMA((2,))],
        "repack",
    )(dest_one, dest_zero, rx)
    g_zero = exchange(packed)
    kept = forward(my_index, rx, owners, weights)
    result = backward(g_zero, kept, weights)
    return call(
        unpack_kernel, jax.ShapeDtypeStruct((points, D), BF), [VMEM_SPEC] * 2, VMEM_SPEC, [], "unpack"
    )(dest_zero, exchange(result))


def solution(mesh):
    placed = (
        P(None, ("rep", "blk"), None),
        P(("rep", "blk"), None),
        P(None, "rep", None),
        P(),
        P(),
        P(),
        P(),
    )
    return jax.shard_map(
        per_device, mesh=mesh, in_specs=placed, out_specs=P(("rep", "blk"), None), check_vma=False
    )
```

```python
import jax
import jax.numpy as jnp
from jax import lax
from jax.experimental import pallas as pl
from jax.experimental.pallas import tpu as pltpu
from jax.sharding import PartitionSpec as P

D = 256
HEADS = 8
HD = D // HEADS
EPSILON = 1e-05
MASKED = -1e30
SCALE = HD ** (-0.5)
LOG2E = 1.4426950408889634
BF = jnp.bfloat16
F32 = jnp.float32


def mm(left, right):
    return lax.dot_general(left, right, (((1,), (0,)), ((), ())), preferred_element_type=F32)


def mm_t(left, right):
    return lax.dot_general(left, right, (((1,), (1,)), ((), ())), preferred_element_type=F32)


def iota(shape, axis):
    return lax.broadcasted_iota(jnp.int32, shape, axis)


def destination_row(owners, my_index, points):
    wide_rows = points // LANES
    own_row = jnp.concatenate(
        [owners[pl.ds(my_index * wide_rows + i, 1), :] for i in range(wide_rows)], axis=1
    ).astype(F32)
    rows, cols = iota((points, points), 0), iota((points, points), 1)
    wide = jnp.broadcast_to(own_row, (points, points))
    own_col = jnp.sum(jnp.where(rows == cols, wide, 0.0), axis=1, keepdims=True)
    same = jnp.where((own_col == wide) & (rows < cols), 1.0, 0.0)
    rank = jnp.sum(same, axis=0, keepdims=True)
    return own_row * 8.0 + rank


def one_hot(dest_row, slots):
    shape = (slots, dest_row.shape[1])
    return jnp.where(iota(shape, 0).astype(F32) == dest_row, 1.0, 0.0).astype(BF)


def key_bias(owners, my_index, slots):
    rows = owners.shape[0]
    per_source = rows * 8 // slots
    count = jnp.sum(jnp.where(owners == my_index, 1.0, 0.0), axis=1, keepdims=True)
    shape = (slots, rows)
    spread = jnp.where(iota(shape, 0) // 8 == iota(shape, 1) // per_source, 1.0, 0.0).astype(BF)
    slot_count = mm(spread, jnp.broadcast_to(count, (rows, D)).astype(BF))
    rank = (iota(slot_count.shape, 0) % 8).astype(F32)
    return jnp.where(rank < slot_count, 0.0, MASKED).astype(BF)


def unpack(dest_row, rows):
    hot = one_hot(dest_row, rows.shape[0])
    return lax.dot_general(hot, rows, (((0,), (0,)), ((), ())), preferred_element_type=F32).astype(BF)


def fetch(sem, pairs):
    copies = [pltpu.make_async_copy(a, b, sem.at[i]) for i, (a, b) in enumerate(pairs)]
    for copy in copies:
        copy.start()
    return copies


def route_kernel(
    index_ref, owners_hbm, saved_hbm, g_hbm, *rest
):
    weights_hbm, (dest_ref, out_ref, all_owners_ref, next_x_ref), rest = rest[:4], rest[4:8], rest[8:]
    weights, (x_ref, g_ref, sem) = rest[:4], rest[4:]
    slots, points = out_ref.shape[0], g_hbm.shape[0]
    owners_in, x_in, g_in, *others = fetch(
        sem,
        [(owners_hbm, all_owners_ref), (saved_hbm.at[1], x_ref), (g_hbm, g_ref)]
        + [(saved_hbm.at[0], next_x_ref)]
        + [(hbm.at[1], ref) for hbm, ref in zip(weights_hbm, weights)],
    )
    owners_in.wait()
    dest = destination_row(all_owners_ref.at[1], index_ref[0], points)
    dest_ref[...] = jnp.broadcast_to(dest, dest_ref.shape)
    hot = one_hot(dest, slots)
    x_in.wait()
    out_ref[:, :D] = mm(hot, x_ref[...]).astype(BF)
    g_in.wait()
    out_ref[:, D:] = mm(hot, g_ref[...]).astype(BF)
    for copy in others:
        copy.wait()


def repack_kernel(dest_one_ref, dest_zero_ref, rows_ref, out_ref):
    gradient = unpack(dest_one_ref[0:1, :], rows_ref[:, :D])
    out_ref[...] = mm(one_hot(dest_zero_ref[0:1, :], out_ref.shape[0]), gradient).astype(BF)


def unpack_kernel(dest_ref, rows_ref, out_ref):
    out_ref[...] = unpack(dest_ref[0:1, :], rows_ref[...])


def normalized(values):
    centered = values - jnp.mean(values, axis=1, keepdims=True)
    inverse = lax.rsqrt(jnp.mean(centered * centered, axis=1, keepdims=True) + EPSILON)
    return centered * inverse, inverse


def norm_gradient(upstream, hat, inverse):
    mean_one = jnp.mean(upstream, axis=1, keepdims=True)
    mean_two = jnp.mean(upstream * hat, axis=1, keepdims=True)
    return inverse * (upstream - mean_one - hat * mean_two)


def head_lanes(shape, head):
    lane = iota(shape, 1)
    return (lane >= head * HD) & (lane < head * HD + HD)


def gelu_slope(pre):
    root, cubic = 0.7978845608028654, 0.044715
    square = pre * pre
    bend = jnp.tanh(pre * (root + (root * cubic) * square))
    rise = pre * (root + (3.0 * root * cubic) * square)
    return (0.5 + 0.5 * bend) * (1.0 + (1.0 - bend) * rise)


LANES = 128


def forward_part(x, weights, kept, work, wait, after_head, unroll):
    attend_ref, output_ref = weights[:2]
    value_ref, query_t_ref, key_t_ref, probs_ref, norm_ref, mixed_t_ref = kept
    bias_ref, query_ref, key_ref, value_t_ref, even_ref, odd_ref, even_max_ref, odd_max_ref = work
    slots = x.shape[0]
    normed, _ = normalized(x)
    wait("attend")
    qkv = mm(normed.astype(BF), attend_ref[...]).astype(BF)
    key_ref[...] = qkv[:, D : 2 * D]
    value_ref[...] = qkv[:, 2 * D :]
    value_t_ref[...] = qkv[:, 2 * D :].T
    query_t_ref[...] = qkv[:, :D].T
    key_t_ref[...] = qkv[:, D : 2 * D].T
    lane = iota((slots, D), 1)
    query_ref[...] = jnp.where(lane == 0, jnp.ones((slots, D), BF), qkv[:, :D])
    wait("owners")

    def score(keys, queries, scores_ref, max_ref):
        scores = mm_t(keys, queries)
        scores_ref[...] = scores
        max_ref[...] = jnp.broadcast_to(jnp.max(scores, axis=0, keepdims=True), (8, slots))

    def soften(head, scores_ref, max_ref):
        exponent = jnp.exp2((scores_ref[...] - max_ref[0:1, :]) * (SCALE * LOG2E))
        total = jnp.sum(exponent, axis=0, keepdims=True)
        probs = (exponent * (1.0 / total)).astype(BF)
        probs_ref[head] = probs
        at = pl.multiple_of(head * HD, HD)
        mixed_t_ref[pl.ds(at, HD), :] = mm(value_t_ref[pl.ds(at, HD), :], probs)

    bias = bias_ref[...]
    first_keys = jnp.where(
        head_lanes((slots, D), 0),
        qkv[:, D : 2 * D],
        jnp.where(lane == D - 1, bias, jnp.zeros_like(bias)),
    )
    first_queries = jnp.where(lane == D - 1, jnp.ones((slots, D), BF), qkv[:, :D])
    bias_ref[...] = jnp.where(lane == 0, bias, jnp.zeros_like(bias))
    score(first_keys, first_queries, even_ref, even_max_ref)

    def step(head, following, here, here_max, there, there_max):
        keys = jnp.where(head_lanes((slots, D), following), key_ref[...], bias_ref[...])
        score(keys, query_ref[...], there, there_max)
        soften(head, here, here_max)
        after_head(head)

    def pair(index, carry):
        step(2 * index, 2 * index + 1, even_ref, even_max_ref, odd_ref, odd_max_ref)
        following = jnp.minimum(2 * index + 2, HEADS - 1)
        step(2 * index + 1, following, odd_ref, odd_max_ref, even_ref, even_max_ref)
        return carry

    lax.fori_loop(0, HEADS // 2, pair, 0, unroll=unroll)
    attended = mixed_t_ref[...].astype(BF).T
    wait("output")
    mixed = mm(attended, output_ref[...]).astype(BF).astype(F32)
    hat, inverse = normalized(x + mixed)
    norm_ref[:, :D] = hat
    norm_ref[:, D:] = jnp.broadcast_to(inverse, (slots, LANES))


def backward_part(x_ref, g, weights, kept, work, wait, before_heads):
    attend_ref, output_ref, up_ref, down_ref = weights
    value_ref, query_t_ref, key_t_ref, probs_ref, norm_ref, mixed_t_ref = kept
    pre_grad_ref, up_grad_ref, up_grad_t_ref, delta_ref, grads_t_ref = work
    slots = g.shape[0]
    rounded = norm_ref[:, :D].astype(BF)
    wait("up")
    blocks = [slice(at, at + D) for at in range(0, up_ref.shape[1], D)]
    slopes = [gelu_slope(mm(rounded, up_ref[:, block])) for block in blocks]
    wait("down")
    for block, slope in zip(blocks, slopes):
        pre_grad_ref[:, block] = (slope * mm_t(g, down_ref[block, :])).astype(BF)
    normed_grad = mm_t(pre_grad_ref[...], up_ref[...])
    grad_mid = (
        g.astype(F32) + norm_gradient(normed_grad, norm_ref[:, :D], norm_ref[:, D : D + 1])
    ).astype(BF)
    wait("output")
    up_grad_ref[...] = mm_t(grad_mid, output_ref[...]).astype(BF)
    up_grad_t = mm_t(output_ref[...], grad_mid).astype(BF)
    up_grad_t_ref[...] = up_grad_t
    weighted = mixed_t_ref[...] * up_grad_t.astype(F32)
    for head in range(HEADS):
        delta_ref[head : head + 1, :] = jnp.sum(
            weighted[head * HD : (head + 1) * HD], axis=0, keepdims=True
        )

    def one_head(head, carry):
        values = jnp.where(
            head_lanes((slots, D), head), value_ref[...], jnp.zeros((slots, D), BF)
        )
        at = pl.multiple_of(head * HD, HD)
        prob_grads = mm_t(values, up_grad_ref[...])
        probs = probs_ref[head]
        delta = delta_ref[pl.ds(head, 1), :]
        score_grads = (probs.astype(F32) * (prob_grads - delta)).astype(BF)
        value_grad = mm_t(up_grad_t_ref[pl.ds(at, HD), :], probs)
        key_grad = mm_t(query_t_ref[pl.ds(at, HD), :], score_grads)
        grads_t_ref[pl.ds(at, HD), :] = (mm(key_t_ref[pl.ds(at, HD), :], score_grads) * SCALE).astype(BF)
        grads_t_ref[pl.ds(pl.multiple_of(D + at, HD), HD), :] = (key_grad * SCALE).astype(BF)
        grads_t_ref[pl.ds(pl.multiple_of(2 * D + at, HD), HD), :] = value_grad.astype(BF)
        return carry

    before_heads()
    lax.fori_loop(0, HEADS, one_head, 0, unroll=HEADS)
    wait("attend")
    normed_grads = mm(attend_ref[...], grads_t_ref[...]).T
    wait("x")
    hat, inverse = normalized(x_ref[...].astype(F32))
    branch = norm_gradient(normed_grads, hat, inverse).astype(BF)
    return (grad_mid.astype(F32) + branch.astype(F32)).astype(BF)


def whole_layer_kernel(index_ref, xg_ref, owners_ref, next_x_ref, *rest):
    weights, (out_ref, dest_ref), rest = rest[:4], rest[4:6], rest[6:]
    kept, forward_work, backward_work = rest[:6], rest[6:14], rest[14:19]
    my = index_ref[0]
    slots = out_ref.shape[0]
    forward_work[0][...] = key_bias(owners_ref[1], my, slots)

    def wait(name):
        return None

    forward_part(
        xg_ref[:, :D].astype(F32), weights, kept, forward_work, wait, lambda head: None,
        HEADS // 2,
    )
    dest = destination_row(owners_ref.at[0], my, next_x_ref.shape[0])
    dest_ref[...] = jnp.broadcast_to(dest, dest_ref.shape)
    out_ref[:, D:] = mm(one_hot(dest, slots), next_x_ref[...]).astype(BF)
    out_ref[:, :D] = backward_part(
        xg_ref.at[:, pl.ds(0, D)], xg_ref[:, D:], weights, kept, backward_work, wait,
        lambda: None,
    )


def forward_kernel(index_ref, rx_ref, owners_hbm, *rest):
    attend_hbm, output_hbm, up_hbm, down_hbm = rest[:4]
    value_ref, norm_ref, mixed_t_ref, up_ref, down_ref = rest[4:9]
    probs_out, x_out, query_out, key_out = rest[9:13]
    attend_ref, output_ref, probs_ref, query_t_ref, key_t_ref = rest[13:18]
    work = rest[18:26]
    owners_ref, in_sem, probs_sem, out_sem = rest[26:]
    my = index_ref[0]
    slots = rx_ref.shape[0]
    copies = fetch(
        in_sem,
        [
            (attend_hbm.at[0], attend_ref),
            (owners_hbm.at[0], owners_ref),
            (output_hbm.at[0], output_ref),
            (up_hbm.at[0], up_ref),
            (down_hbm.at[0], down_ref),
            (rx_ref.at[:, pl.ds(D, D)], x_out),
        ],
    )
    order = dict(attend=0, owners=1, output=2)

    def wait(name):
        copies[order[name]].wait()
        if name == "owners":
            work[0][...] = key_bias(owners_ref[...], my, slots)

    def probs_copy(head):
        return pltpu.make_async_copy(probs_ref.at[head], probs_out.at[head], probs_sem.at[head])

    forward_part(
        rx_ref[:, D:].astype(F32),
        (attend_ref, output_ref),
        (value_ref, query_t_ref, key_t_ref, probs_ref, norm_ref, mixed_t_ref),
        work, wait, lambda head: probs_copy(head).start(), 1,
    )
    for copy in copies[3:] + fetch(out_sem, [(query_t_ref, query_out), (key_t_ref, key_out)]):
        copy.wait()
    for head in range(HEADS):
        probs_copy(head).wait()


def backward_kernel(
    g_ref, value_ref, norm_ref, mixed_t_ref, up_ref, down_ref, probs_hbm,
    x_hbm, query_hbm, key_hbm, attend_hbm, output_hbm,
    out_ref,
    attend_ref, output_ref, x_ref, probs_ref, query_t_ref, key_t_ref, *rest,
):
    work, (sem, probs_sem) = rest[:5], rest[5:]
    pairs = [(output_hbm.at[0], output_ref), (query_hbm, query_t_ref), (key_hbm, key_t_ref)]
    pairs += [(attend_hbm.at[0], attend_ref), (x_hbm, x_ref)]
    copies = [pltpu.make_async_copy(a, b, sem.at[i]) for i, (a, b) in enumerate(pairs)]
    for copy in copies[:3]:
        copy.start()
    order = dict(output=0, attend=3, x=4)

    def probs_copy(head):
        return pltpu.make_async_copy(probs_hbm.at[head], probs_ref.at[head], probs_sem.at[head])

    for head in range(HEADS):
        probs_copy(head).start()
    for copy in copies[3:]:
        copy.start()

    def wait(name):
        if name in order:
            copies[order[name]].wait()

    def before_heads():
        copies[1].wait()
        copies[2].wait()
        for head in range(HEADS):
            probs_copy(head).wait()

    out_ref[...] = backward_part(
        x_ref, g_ref[...], (attend_ref, output_ref, up_ref, down_ref),
        (value_ref, query_t_ref, key_t_ref, probs_ref, norm_ref, mixed_t_ref),
        work, wait, before_heads,
    )


SMEM_SPEC = pl.BlockSpec(memory_space=pltpu.SMEM)
VMEM_SPEC = pl.BlockSpec(memory_space=pltpu.VMEM)
HBM_SPEC = pl.BlockSpec(memory_space=pltpu.HBM)


def in_hbm(array):
    return pltpu.with_memory_space_constraint(array, pltpu.HBM)


def kept_shapes(slots):
    return [
        ((slots, D), BF),
        ((D, slots), BF),
        ((D, slots), BF),
        ((HEADS, slots, slots), BF),
        ((slots, D + LANES), F32),
        ((D, slots), F32),
    ]


def weight_scratch(weights):
    return [pltpu.VMEM(w.shape[1:], BF) for w in weights]


def forward_scratch(slots):
    return [
        pltpu.VMEM((slots, D), BF),
        pltpu.VMEM((slots, D), BF),
        pltpu.VMEM((slots, D), BF),
        pltpu.VMEM((D, slots), BF),
        pltpu.VMEM((slots, slots), F32),
        pltpu.VMEM((slots, slots), F32),
        pltpu.VMEM((8, slots), F32),
        pltpu.VMEM((8, slots), F32),
    ]


def backward_scratch(slots, hidden):
    return [
        pltpu.VMEM((slots, hidden), BF),
        pltpu.VMEM((slots, D), BF),
        pltpu.VMEM((D, slots), BF),
        pltpu.VMEM((HEADS, slots), F32),
        pltpu.VMEM((3 * D, slots), BF),
    ]


def call(kernel, outs, in_specs, out_specs, scratch, name):
    return pl.pallas_call(
        kernel,
        out_shape=outs,
        in_specs=in_specs,
        out_specs=out_specs,
        scratch_shapes=scratch,
        name=name,
        compiler_params=pltpu.CompilerParams(vmem_limit_bytes=40 << 20),
    )


def whole_layer(my_index, xg, owners, next_x, weights):
    slots, hidden, points = xg.shape[0], weights[2].shape[1], next_x.shape[0]
    return call(
        whole_layer_kernel,
        (jax.ShapeDtypeStruct((slots, 2 * D), BF), jax.ShapeDtypeStruct((8, points), F32)),
        [SMEM_SPEC] + [VMEM_SPEC] * 7,
        (VMEM_SPEC, VMEM_SPEC),
        [pltpu.VMEM(*k) for k in kept_shapes(slots)]
        + forward_scratch(slots)
        + backward_scratch(slots, hidden),
        "whole_layer",
    )(my_index, xg, owners, next_x, *weights)


def forward(my_index, rx, owners, weights):
    slots = rx.shape[0]
    shapes = kept_shapes(slots)
    attend, output, up, down = weights
    return call(
        forward_kernel,
        tuple(jax.ShapeDtypeStruct(*shapes[i]) for i in (0, 4, 5))
        + tuple(jax.ShapeDtypeStruct(w.shape[1:], BF) for w in (up, down))
        + tuple(pltpu.HBM(*k) for k in (shapes[3], shapes[0], shapes[1], shapes[2])),
        [SMEM_SPEC, VMEM_SPEC] + [HBM_SPEC] * 5,
        (VMEM_SPEC,) * 5 + (HBM_SPEC,) * 4,
        weight_scratch((attend, output))
        + [pltpu.VMEM(*shapes[i]) for i in (3, 1, 2)]
        + forward_scratch(slots)
        + [
            pltpu.VMEM(owners.shape[1:], jnp.int32),
            pltpu.SemaphoreType.DMA((6,)),
            pltpu.SemaphoreType.DMA((HEADS,)),
            pltpu.SemaphoreType.DMA((2,)),
        ],
        "layer_forward",
    )(my_index, rx, owners, *weights)


def backward(g, kept, weights):
    slots = g.shape[0]
    attend, output, up, _ = weights
    return call(
        backward_kernel,
        jax.ShapeDtypeStruct((slots, D), BF),
        [VMEM_SPEC] * 6 + [HBM_SPEC] * 6,
        VMEM_SPEC,
        weight_scratch((attend, output))
        + [pltpu.VMEM(*kept_shapes(slots)[i]) for i in (0, 3, 1, 2)]
        + backward_scratch(slots, up.shape[2])
        + [pltpu.SemaphoreType.DMA((5,)), pltpu.SemaphoreType.DMA((HEADS,))],
        "layer_backward",
    )(g, *kept[:5], *(in_hbm(k) for k in kept[5:]), attend, output)


def per_device(saved_inputs, output_grads, owner_ids, attend, output, up, down):
    devices = lax.axis_size("blk")
    points = saved_inputs.shape[1]
    slots = devices * 8
    my_index = lax.axis_index("blk").astype(jnp.int32).reshape(1)
    owners = in_hbm(owner_ids.reshape(2, devices * points // LANES, LANES))
    saved_inputs, output_grads = in_hbm(saved_inputs), in_hbm(output_grads)
    weights = tuple(in_hbm(w) for w in (attend, output, up, down))

    def exchange(rows):
        width = rows.shape[1]
        moved = lax.all_to_all(
            rows.reshape(devices, 8, width), "blk", split_axis=0, concat_axis=0, tiled=True
        )
        return moved.reshape(slots, width)

    fetched_shapes = [(owners.shape, jnp.int32), ((points, D), BF)]
    fetched_shapes += [(w.shape[1:], BF) for w in weights]
    dest_one, packed, *fetched = call(
        route_kernel,
        (jax.ShapeDtypeStruct((8, points), F32), jax.ShapeDtypeStruct((slots, 2 * D), BF))
        + tuple(jax.ShapeDtypeStruct(*k) for k in fetched_shapes),
        [SMEM_SPEC] + [HBM_SPEC] * 7,
        (VMEM_SPEC,) * 8,
        [
            pltpu.VMEM((points, D), BF),
            pltpu.VMEM((points, D), BF),
            pltpu.SemaphoreType.DMA((8,)),
        ],
        "route",
    )(my_index, owners, saved_inputs, output_grads, *weights)
    xg = exchange(packed)
    result, dest_zero = whole_layer(my_index, xg, *fetched[:2], fetched[2:])
    rx = exchange(result)
    packed = call(
        repack_kernel, jax.ShapeDtypeStruct((slots, D), BF), [VMEM_SPEC] * 3, VMEM_SPEC, [], "repack"
    )(dest_one, dest_zero, rx)
    g_zero = exchange(packed)
    kept = forward(my_index, rx, owners, weights)
    result = backward(g_zero, kept, weights)
    return call(
        unpack_kernel, jax.ShapeDtypeStruct((points, D), BF), [VMEM_SPEC] * 2, VMEM_SPEC, [], "unpack"
    )(dest_zero, exchange(result))


def solution(mesh):
    placed = (
        P(None, ("rep", "blk"), None),
        P(("rep", "blk"), None),
        P(None, "rep", None),
        P(),
        P(),
        P(),
        P(),
    )
    return jax.shard_map(
        per_device, mesh=mesh, in_specs=placed, out_specs=P(("rep", "blk"), None), check_vma=False
    )
```

```python
import jax
import jax.numpy as jnp
from jax import lax
from jax.experimental import pallas as pl
from jax.experimental.pallas import tpu as pltpu
from jax.sharding import PartitionSpec as P

D = 256
HEADS = 8
HD = D // HEADS
EPSILON = 1e-05
MASKED = -1e30
SCALE = HD ** (-0.5)
LOG2E = 1.4426950408889634
BF = jnp.bfloat16
F32 = jnp.float32


def mm(left, right):
    return lax.dot_general(left, right, (((1,), (0,)), ((), ())), preferred_element_type=F32)


def mm_t(left, right):
    return lax.dot_general(left, right, (((1,), (1,)), ((), ())), preferred_element_type=F32)


def iota(shape, axis):
    return lax.broadcasted_iota(jnp.int32, shape, axis)


def destination_row(owners, my_index, points):
    wide_rows = points // LANES
    own_row = jnp.concatenate(
        [owners[pl.ds(my_index * wide_rows + i, 1), :] for i in range(wide_rows)], axis=1
    ).astype(F32)
    rows, cols = iota((points, points), 0), iota((points, points), 1)
    wide = jnp.broadcast_to(own_row, (points, points))
    own_col = jnp.sum(jnp.where(rows == cols, wide, 0.0), axis=1, keepdims=True)
    same = jnp.where((own_col == wide) & (rows < cols), 1.0, 0.0)
    rank = jnp.sum(same, axis=0, keepdims=True)
    return own_row * 8.0 + rank


def one_hot(dest_row, slots):
    shape = (slots, dest_row.shape[1])
    return jnp.where(iota(shape, 0).astype(F32) == dest_row, 1.0, 0.0).astype(BF)


def key_bias(owners, my_index, slots):
    rows = owners.shape[0]
    per_source = rows * 8 // slots
    count = jnp.sum(jnp.where(owners == my_index, 1.0, 0.0), axis=1, keepdims=True)
    shape = (slots, rows)
    spread = jnp.where(iota(shape, 0) // 8 == iota(shape, 1) // per_source, 1.0, 0.0).astype(BF)
    slot_count = mm(spread, jnp.broadcast_to(count, (rows, D)).astype(BF))
    rank = (iota(slot_count.shape, 0) % 8).astype(F32)
    return jnp.where(rank < slot_count, 0.0, MASKED).astype(BF)


def unpack(dest_row, rows):
    hot = one_hot(dest_row, rows.shape[0])
    return lax.dot_general(hot, rows, (((0,), (0,)), ((), ())), preferred_element_type=F32).astype(BF)


def fetch(sem, pairs):
    copies = [pltpu.make_async_copy(a, b, sem.at[i]) for i, (a, b) in enumerate(pairs)]
    for copy in copies:
        copy.start()
    return copies


def route_kernel(
    index_ref, owners_hbm, saved_hbm, g_hbm, *rest
):
    weights_hbm, (dest_ref, out_ref, all_owners_ref, next_x_ref), rest = rest[:4], rest[4:8], rest[8:]
    weights, (x_ref, g_ref, sem) = rest[:4], rest[4:]
    slots, points = out_ref.shape[0], g_hbm.shape[0]
    owners_in, x_in, g_in, *others = fetch(
        sem,
        [(owners_hbm, all_owners_ref), (saved_hbm.at[1], x_ref), (g_hbm, g_ref)]
        + [(saved_hbm.at[0], next_x_ref)]
        + [(hbm.at[1], ref) for hbm, ref in zip(weights_hbm, weights)],
    )
    owners_in.wait()
    dest = destination_row(all_owners_ref.at[1], index_ref[0], points)
    dest_ref[...] = jnp.broadcast_to(dest, dest_ref.shape)
    hot = one_hot(dest, slots)
    x_in.wait()
    out_ref[:, :D] = mm(hot, x_ref[...]).astype(BF)
    g_in.wait()
    out_ref[:, D:] = mm(hot, g_ref[...]).astype(BF)
    for copy in others:
        copy.wait()


def repack_kernel(dest_one_ref, dest_zero_ref, rows_ref, out_hbm, packed_ref, sem):
    gradient = unpack(dest_one_ref[0:1, :], rows_ref[:, :D])
    slots = packed_ref.shape[0]
    hot = one_hot(dest_zero_ref[0:1, :], slots)
    copies = []
    for part in range(2):
        rows = pl.ds(part * (slots // 2), slots // 2)
        at = slice(part * (slots // 2), (part + 1) * (slots // 2))
        packed_ref[at, :] = mm(hot[at], gradient).astype(BF)
        copies.append(pltpu.make_async_copy(packed_ref.at[rows], out_hbm.at[rows], sem.at[part]))
        copies[part].start()
    for copy in copies:
        copy.wait()


def unpack_kernel(dest_ref, rows_ref, out_ref):
    out_ref[...] = unpack(dest_ref[0:1, :], rows_ref[...])


def normalized(values):
    centered = values - jnp.mean(values, axis=1, keepdims=True)
    inverse = lax.rsqrt(jnp.mean(centered * centered, axis=1, keepdims=True) + EPSILON)
    return centered * inverse, inverse


def norm_gradient(upstream, hat, inverse):
    mean_one = jnp.mean(upstream, axis=1, keepdims=True)
    mean_two = jnp.mean(upstream * hat, axis=1, keepdims=True)
    return inverse * (upstream - mean_one - hat * mean_two)


def head_lanes(shape, head):
    lane = iota(shape, 1)
    return (lane >= head * HD) & (lane < head * HD + HD)


def gelu_slope(pre):
    root, cubic = 0.7978845608028654, 0.044715
    square = pre * pre
    bend = jnp.tanh(pre * (root + (root * cubic) * square))
    rise = pre * (root + (3.0 * root * cubic) * square)
    return (0.5 + 0.5 * bend) * (1.0 + (1.0 - bend) * rise)


LANES = 128


def forward_part(x, weights, kept, work, wait, after_head, unroll):
    attend_ref, output_ref = weights[:2]
    value_ref, query_t_ref, key_t_ref, probs_ref, norm_ref, mixed_t_ref = kept
    bias_ref, query_ref, key_ref, value_t_ref, even_ref, odd_ref, even_max_ref, odd_max_ref = work
    slots = x.shape[0]
    normed, _ = normalized(x)
    wait("attend")
    qkv = mm(normed.astype(BF), attend_ref[...]).astype(BF)
    key_ref[...] = qkv[:, D : 2 * D]
    value_ref[...] = qkv[:, 2 * D :]
    value_t_ref[...] = qkv[:, 2 * D :].T
    query_t_ref[...] = qkv[:, :D].T
    key_t_ref[...] = qkv[:, D : 2 * D].T
    lane = iota((slots, D), 1)
    query_ref[...] = jnp.where(lane == 0, jnp.ones((slots, D), BF), qkv[:, :D])
    wait("owners")

    def score(keys, queries, scores_ref, max_ref):
        scores = mm_t(keys, queries)
        scores_ref[...] = scores
        max_ref[...] = jnp.broadcast_to(jnp.max(scores, axis=0, keepdims=True), (8, slots))

    def soften(head, scores_ref, max_ref):
        exponent = jnp.exp2((scores_ref[...] - max_ref[0:1, :]) * (SCALE * LOG2E))
        total = jnp.sum(exponent, axis=0, keepdims=True)
        probs = (exponent * (1.0 / total)).astype(BF)
        probs_ref[head] = probs
        at = pl.multiple_of(head * HD, HD)
        mixed_t_ref[pl.ds(at, HD), :] = mm(value_t_ref[pl.ds(at, HD), :], probs)

    bias = bias_ref[...]
    first_keys = jnp.where(
        head_lanes((slots, D), 0),
        qkv[:, D : 2 * D],
        jnp.where(lane == D - 1, bias, jnp.zeros_like(bias)),
    )
    first_queries = jnp.where(lane == D - 1, jnp.ones((slots, D), BF), qkv[:, :D])
    bias_ref[...] = jnp.where(lane == 0, bias, jnp.zeros_like(bias))
    score(first_keys, first_queries, even_ref, even_max_ref)

    def step(head, following, here, here_max, there, there_max):
        keys = jnp.where(head_lanes((slots, D), following), key_ref[...], bias_ref[...])
        score(keys, query_ref[...], there, there_max)
        soften(head, here, here_max)
        after_head(head)

    def pair(index, carry):
        step(2 * index, 2 * index + 1, even_ref, even_max_ref, odd_ref, odd_max_ref)
        following = jnp.minimum(2 * index + 2, HEADS - 1)
        step(2 * index + 1, following, odd_ref, odd_max_ref, even_ref, even_max_ref)
        return carry

    lax.fori_loop(0, HEADS // 2, pair, 0, unroll=unroll)
    attended = mixed_t_ref[...].astype(BF).T
    wait("output")
    mixed = mm(attended, output_ref[...]).astype(BF).astype(F32)
    hat, inverse = normalized(x + mixed)
    norm_ref[:, :D] = hat
    norm_ref[:, D:] = jnp.broadcast_to(inverse, (slots, LANES))


def backward_part(x_ref, g, weights, kept, work, wait, before_heads):
    attend_ref, output_ref, up_ref, down_ref = weights
    value_ref, query_t_ref, key_t_ref, probs_ref, norm_ref, mixed_t_ref = kept
    pre_grad_ref, up_grad_ref, up_grad_t_ref, delta_ref, grads_t_ref = work
    slots = g.shape[0]
    rounded = norm_ref[:, :D].astype(BF)
    wait("up")
    blocks = [slice(at, at + D) for at in range(0, up_ref.shape[1], D)]
    slopes = [gelu_slope(mm(rounded, up_ref[:, block])) for block in blocks]
    wait("down")
    for block, slope in zip(blocks, slopes):
        pre_grad_ref[:, block] = (slope * mm_t(g, down_ref[block, :])).astype(BF)
    normed_grad = mm_t(pre_grad_ref[...], up_ref[...])
    grad_mid = (
        g.astype(F32) + norm_gradient(normed_grad, norm_ref[:, :D], norm_ref[:, D : D + 1])
    ).astype(BF)
    wait("output")
    up_grad_ref[...] = mm_t(grad_mid, output_ref[...]).astype(BF)
    up_grad_t = mm_t(output_ref[...], grad_mid).astype(BF)
    up_grad_t_ref[...] = up_grad_t
    weighted = mixed_t_ref[...] * up_grad_t.astype(F32)
    for head in range(HEADS):
        delta_ref[head : head + 1, :] = jnp.sum(
            weighted[head * HD : (head + 1) * HD], axis=0, keepdims=True
        )

    def one_head(head, carry):
        values = jnp.where(
            head_lanes((slots, D), head), value_ref[...], jnp.zeros((slots, D), BF)
        )
        at = pl.multiple_of(head * HD, HD)
        prob_grads = mm_t(values, up_grad_ref[...])
        probs = probs_ref[head]
        delta = delta_ref[pl.ds(head, 1), :]
        score_grads = (probs.astype(F32) * (prob_grads - delta)).astype(BF)
        value_grad = mm_t(up_grad_t_ref[pl.ds(at, HD), :], probs)
        key_grad = mm_t(query_t_ref[pl.ds(at, HD), :], score_grads)
        grads_t_ref[pl.ds(at, HD), :] = (mm(key_t_ref[pl.ds(at, HD), :], score_grads) * SCALE).astype(BF)
        grads_t_ref[pl.ds(pl.multiple_of(D + at, HD), HD), :] = (key_grad * SCALE).astype(BF)
        grads_t_ref[pl.ds(pl.multiple_of(2 * D + at, HD), HD), :] = value_grad.astype(BF)
        return carry

    before_heads()
    lax.fori_loop(0, HEADS, one_head, 0, unroll=HEADS)
    wait("attend")
    normed_grads = mm(attend_ref[...], grads_t_ref[...]).T
    wait("x")
    hat, inverse = normalized(x_ref[...].astype(F32))
    branch = norm_gradient(normed_grads, hat, inverse).astype(BF)
    return (grad_mid.astype(F32) + branch.astype(F32)).astype(BF)


def whole_layer_kernel(index_ref, xg_ref, owners_ref, next_x_ref, *rest):
    weights, (out_ref, dest_ref), rest = rest[:4], rest[4:6], rest[6:]
    kept, forward_work, backward_work = rest[:6], rest[6:14], rest[14:19]
    my = index_ref[0]
    slots = out_ref.shape[0]
    forward_work[0][...] = key_bias(owners_ref[1], my, slots)

    def wait(name):
        return None

    forward_part(
        xg_ref[:, :D].astype(F32), weights, kept, forward_work, wait, lambda head: None,
        HEADS // 2,
    )
    dest = destination_row(owners_ref.at[0], my, next_x_ref.shape[0])
    dest_ref[...] = jnp.broadcast_to(dest, dest_ref.shape)
    out_ref[:, D:] = mm(one_hot(dest, slots), next_x_ref[...]).astype(BF)
    out_ref[:, :D] = backward_part(
        xg_ref.at[:, pl.ds(0, D)], xg_ref[:, D:], weights, kept, backward_work, wait,
        lambda: None,
    )


def forward_kernel(index_ref, rx_ref, owners_hbm, *rest):
    attend_hbm, output_hbm, up_hbm, down_hbm = rest[:4]
    value_ref, norm_ref, mixed_t_ref, up_ref, down_ref = rest[4:9]
    probs_out, x_out, query_out, key_out = rest[9:13]
    attend_ref, output_ref, probs_ref, query_t_ref, key_t_ref = rest[13:18]
    work = rest[18:26]
    owners_ref, in_sem, probs_sem, out_sem = rest[26:]
    my = index_ref[0]
    slots = rx_ref.shape[0]
    copies = fetch(
        in_sem,
        [
            (attend_hbm.at[0], attend_ref),
            (owners_hbm.at[0], owners_ref),
            (output_hbm.at[0], output_ref),
            (up_hbm.at[0], up_ref),
            (down_hbm.at[0], down_ref),
            (rx_ref.at[:, pl.ds(D, D)], x_out),
        ],
    )
    order = dict(attend=0, owners=1, output=2)

    def wait(name):
        copies[order[name]].wait()
        if name == "owners":
            work[0][...] = key_bias(owners_ref[...], my, slots)

    def probs_copy(head):
        return pltpu.make_async_copy(probs_ref.at[head], probs_out.at[head], probs_sem.at[head])

    forward_part(
        rx_ref[:, D:].astype(F32),
        (attend_ref, output_ref),
        (value_ref, query_t_ref, key_t_ref, probs_ref, norm_ref, mixed_t_ref),
        work, wait, lambda head: probs_copy(head).start(), 1,
    )
    for copy in copies[3:] + fetch(out_sem, [(query_t_ref, query_out), (key_t_ref, key_out)]):
        copy.wait()
    for head in range(HEADS):
        probs_copy(head).wait()


def backward_kernel(
    g_ref, value_ref, norm_ref, mixed_t_ref, up_ref, down_ref, probs_hbm,
    x_hbm, query_hbm, key_hbm, attend_hbm, output_hbm,
    out_ref,
    attend_ref, output_ref, x_ref, probs_ref, query_t_ref, key_t_ref, *rest,
):
    work, (sem, probs_sem) = rest[:5], rest[5:]
    pairs = [(output_hbm.at[0], output_ref), (query_hbm, query_t_ref), (key_hbm, key_t_ref)]
    pairs += [(attend_hbm.at[0], attend_ref), (x_hbm, x_ref)]
    copies = [pltpu.make_async_copy(a, b, sem.at[i]) for i, (a, b) in enumerate(pairs)]
    for copy in copies[:3]:
        copy.start()
    order = dict(output=0, attend=3, x=4)

    def probs_copy(head):
        return pltpu.make_async_copy(probs_hbm.at[head], probs_ref.at[head], probs_sem.at[head])

    for head in range(HEADS):
        probs_copy(head).start()
    for copy in copies[3:]:
        copy.start()

    def wait(name):
        if name in order:
            copies[order[name]].wait()

    def before_heads():
        copies[1].wait()
        copies[2].wait()
        for head in range(HEADS):
            probs_copy(head).wait()

    out_ref[...] = backward_part(
        x_ref, g_ref[...], (attend_ref, output_ref, up_ref, down_ref),
        (value_ref, query_t_ref, key_t_ref, probs_ref, norm_ref, mixed_t_ref),
        work, wait, before_heads,
    )


SMEM_SPEC = pl.BlockSpec(memory_space=pltpu.SMEM)
VMEM_SPEC = pl.BlockSpec(memory_space=pltpu.VMEM)
HBM_SPEC = pl.BlockSpec(memory_space=pltpu.HBM)


def in_hbm(array):
    return pltpu.with_memory_space_constraint(array, pltpu.HBM)


def kept_shapes(slots):
    return [
        ((slots, D), BF),
        ((D, slots), BF),
        ((D, slots), BF),
        ((HEADS, slots, slots), BF),
        ((slots, D + LANES), F32),
        ((D, slots), F32),
    ]


def weight_scratch(weights):
    return [pltpu.VMEM(w.shape[1:], BF) for w in weights]


def forward_scratch(slots):
    return [
        pltpu.VMEM((slots, D), BF),
        pltpu.VMEM((slots, D), BF),
        pltpu.VMEM((slots, D), BF),
        pltpu.VMEM((D, slots), BF),
        pltpu.VMEM((slots, slots), F32),
        pltpu.VMEM((slots, slots), F32),
        pltpu.VMEM((8, slots), F32),
        pltpu.VMEM((8, slots), F32),
    ]


def backward_scratch(slots, hidden):
    return [
        pltpu.VMEM((slots, hidden), BF),
        pltpu.VMEM((slots, D), BF),
        pltpu.VMEM((D, slots), BF),
        pltpu.VMEM((HEADS, slots), F32),
        pltpu.VMEM((3 * D, slots), BF),
    ]


def call(kernel, outs, in_specs, out_specs, scratch, name):
    return pl.pallas_call(
        kernel,
        out_shape=outs,
        in_specs=in_specs,
        out_specs=out_specs,
        scratch_shapes=scratch,
        name=name,
        compiler_params=pltpu.CompilerParams(vmem_limit_bytes=40 << 20),
    )


def whole_layer(my_index, xg, owners, next_x, weights):
    slots, hidden, points = xg.shape[0], weights[2].shape[1], next_x.shape[0]
    return call(
        whole_layer_kernel,
        (jax.ShapeDtypeStruct((slots, 2 * D), BF), jax.ShapeDtypeStruct((8, points), F32)),
        [SMEM_SPEC] + [VMEM_SPEC] * 7,
        (VMEM_SPEC, VMEM_SPEC),
        [pltpu.VMEM(*k) for k in kept_shapes(slots)]
        + forward_scratch(slots)
        + backward_scratch(slots, hidden),
        "whole_layer",
    )(my_index, xg, owners, next_x, *weights)


def forward(my_index, rx, owners, weights):
    slots = rx.shape[0]
    shapes = kept_shapes(slots)
    attend, output, up, down = weights
    return call(
        forward_kernel,
        tuple(jax.ShapeDtypeStruct(*shapes[i]) for i in (0, 4, 5))
        + tuple(jax.ShapeDtypeStruct(w.shape[1:], BF) for w in (up, down))
        + tuple(pltpu.HBM(*k) for k in (shapes[3], shapes[0], shapes[1], shapes[2])),
        [SMEM_SPEC, VMEM_SPEC] + [HBM_SPEC] * 5,
        (VMEM_SPEC,) * 5 + (HBM_SPEC,) * 4,
        weight_scratch((attend, output))
        + [pltpu.VMEM(*shapes[i]) for i in (3, 1, 2)]
        + forward_scratch(slots)
        + [
            pltpu.VMEM(owners.shape[1:], jnp.int32),
            pltpu.SemaphoreType.DMA((6,)),
            pltpu.SemaphoreType.DMA((HEADS,)),
            pltpu.SemaphoreType.DMA((2,)),
        ],
        "layer_forward",
    )(my_index, rx, owners, *weights)


def backward(g, kept, weights):
    slots = g.shape[0]
    attend, output, up, _ = weights
    return call(
        backward_kernel,
        jax.ShapeDtypeStruct((slots, D), BF),
        [VMEM_SPEC] * 6 + [HBM_SPEC] * 6,
        VMEM_SPEC,
        weight_scratch((attend, output))
        + [pltpu.VMEM(*kept_shapes(slots)[i]) for i in (0, 3, 1, 2)]
        + backward_scratch(slots, up.shape[2])
        + [pltpu.SemaphoreType.DMA((5,)), pltpu.SemaphoreType.DMA((HEADS,))],
        "layer_backward",
    )(g, *kept[:5], *(in_hbm(k) for k in kept[5:]), attend, output)


def per_device(saved_inputs, output_grads, owner_ids, attend, output, up, down):
    devices = lax.axis_size("blk")
    points = saved_inputs.shape[1]
    slots = devices * 8
    my_index = lax.axis_index("blk").astype(jnp.int32).reshape(1)
    owners = in_hbm(owner_ids.reshape(2, devices * points // LANES, LANES))
    saved_inputs, output_grads = in_hbm(saved_inputs), in_hbm(output_grads)
    weights = tuple(in_hbm(w) for w in (attend, output, up, down))

    def exchange(rows):
        width = rows.shape[1]
        moved = lax.all_to_all(
            rows.reshape(devices, 8, width), "blk", split_axis=0, concat_axis=0, tiled=True
        )
        return moved.reshape(slots, width)

    fetched_shapes = [(owners.shape, jnp.int32), ((points, D), BF)]
    fetched_shapes += [(w.shape[1:], BF) for w in weights]
    dest_one, packed, *fetched = call(
        route_kernel,
        (jax.ShapeDtypeStruct((8, points), F32), jax.ShapeDtypeStruct((slots, 2 * D), BF))
        + tuple(jax.ShapeDtypeStruct(*k) for k in fetched_shapes),
        [SMEM_SPEC] + [HBM_SPEC] * 7,
        (VMEM_SPEC,) * 8,
        [
            pltpu.VMEM((points, D), BF),
            pltpu.VMEM((points, D), BF),
            pltpu.SemaphoreType.DMA((8,)),
        ],
        "route",
    )(my_index, owners, saved_inputs, output_grads, *weights)
    xg = exchange(packed)
    result, dest_zero = whole_layer(my_index, xg, *fetched[:2], fetched[2:])
    rx = exchange(result)
    packed = call(
        repack_kernel,
        pltpu.HBM((slots, D), BF),
        [VMEM_SPEC] * 3,
        HBM_SPEC,
        [pltpu.VMEM((slots, D), BF), pltpu.SemaphoreType.DMA((2,))],
        "repack",
    )(dest_one, dest_zero, rx)
    g_zero = exchange(packed)
    kept = forward(my_index, rx, owners, weights)
    result = backward(g_zero, kept, weights)
    return call(
        unpack_kernel, jax.ShapeDtypeStruct((points, D), BF), [VMEM_SPEC] * 2, VMEM_SPEC, [], "unpack"
    )(dest_zero, exchange(result))


def solution(mesh):
    placed = (
        P(None, ("rep", "blk"), None),
        P(("rep", "blk"), None),
        P(None, "rep", None),
        P(),
        P(),
        P(),
        P(),
    )
    return jax.shard_map(
        per_device, mesh=mesh, in_specs=placed, out_specs=P(("rep", "blk"), None), check_vma=False
    )
```
